256 devices in a mesh: tile: 128 (over y, z, x), basin: 2 (over core).
Axes of the slice: x: 4, y: 4, z: 8, core: 2. Of those that a mesh axis runs over, the one named last changes fastest.
Arguments:
- cell_features: bfloat16 [65536, 512], P(('tile', 'basin')), may hold values from -6 to 6
- encoded: bfloat16 [1024, 512], P('tile'), may hold values from -6 to 6
- w_query: bfloat16 [512, 512], replicated, may hold values from -0.375 to 0.375
- w_key: bfloat16 [512, 512], replicated, may hold values from -0.375 to 0.375
- w_value: bfloat16 [512, 512], replicated, may hold values from -0.25 to 0.25
- w_out: bfloat16 [512, 512], replicated, may hold values from -0.25 to 0.25
- pattern: int32 [256, 16], P(('tile', 'basin')), may hold values from 0 to 127, all different within a row
- cell_basin: int32 [65536], P(('tile', 'basin')), may hold values from 0 to 511, as said below
- pooled_grad: bfloat16 [512, 512], P(('tile', 'basin')), may hold values from -24 to 24
Outputs:
- pooled: bfloat16 [512, 512], P(('tile', 'basin'))
- grad_cells: bfloat16 [65536, 512], P(('tile', 'basin'))
- grad_gauges: bfloat16 [1024, 512], P('tile')
- grad_query_weight: float32 [512, 512], replicated
- grad_key_weight: float32 [512, 512], replicated
- grad_value_weight: float32 [512, 512], replicated
- grad_out_weight: float32 [512, 512], replicated
The draws below stay inside these ranges and needn't reach their ends.
Inputs may be any that keep to these rules, and one draw needn't show every extreme that they name: `pattern`: each row names 16 different gauge blocks; every block is named by some row. `cell_basin`: cell c lies in basin (2 * (c // 256) + k) mod 512 for some k with -2 <= k < 4; when c % 256 < 6, k = c % 256 - 2.
All inputs are finite; a program needn't handle non-finite values.
Results may differ from the reference program's by a relative error of at most 0.012.
The reference program's roundings to bfloat16 on the way count: a program that leaves them out, or rounds other values in their place, can miss the bound.
Values may be sent and summed in bfloat16 or wider, within the bound.
No kernel may reach another device: no remote copies, remote signals or barrier semaphores. Data moves between devices by JAX's collectives and lax.ppermute only.
A program may use at most 64 MiB of HBM per device.

```python
import math
import jax
import jax.numpy as jnp
from jax import lax

D = 512
HEADS = 8
HEAD_DIM = 64
CELL_DEV = 256
GAUGE_DEV = 8
KSEL = 16
BAS_DEV = 2
GROUPS = 256
CELLS = 65536
GAUGES = 1024
NBASIN = 512
N_TILE = 128


def draw_cell_basin(key, part):
    positions = jnp.arange(CELLS, dtype=jnp.int32)
    owner = positions // CELL_DEV
    within = positions % CELL_DEV
    offset = jax.random.randint(key, (CELLS,), -BAS_DEV, 2 * BAS_DEV, dtype=jnp.int32)
    offset = jnp.where(within < 3 * BAS_DEV, within - BAS_DEV, offset)
    return (owner * BAS_DEV + offset) % NBASIN


def block_scale(rng, shape, cuts, low, top_value):
    def one(dim, blocks):
        steps = jax.random.uniform(jax.random.fold_in(jax.random.fold_in(rng, 6), dim), (blocks,), jnp.float32, low / len(cuts), top_value / len(cuts))
        return jnp.repeat(jnp.exp(steps), shape[dim] // blocks).reshape((-1,) + (1,) * (len(shape) - dim - 1))

    factor_of = one(*cuts[0])
    for cut in cuts[1:]:
        factor_of = factor_of * one(*cut)
    return factor_of


def distinct(own_key, rows, amount, top, lift):
    ranking = jax.random.permutation(jax.random.fold_in(own_key, 1), amount)
    pull = ranking
    for power in range(3):
        pull = pull * pull // amount
    pull = pull * lift // amount
    chance = jax.random.randint(jax.random.fold_in(own_key, 2), (rows, amount), 0, 4096) + pull
    sure = jax.random.permutation(jax.random.fold_in(own_key, 3), rows)[jnp.arange(amount) % rows]
    chance = jnp.where(jnp.arange(rows)[:, None] == sure[None, :], 1 << 14, chance)
    score = chance * amount + jnp.arange(amount)
    return lax.top_k(score.astype(jnp.int32), top)[1].astype(jnp.int32)


def normal_values(rng, extent, scale, limit, shards=(), kind=jnp.bfloat16):
    array = scale * jax.random.normal(rng, extent, jnp.float32)
    if shards:
        array = array * block_scale(rng, extent, shards, -0.22, 0.18)
    return jnp.clip(array, -limit, limit).astype(kind)


def setup_inputs(seed: int = 0) -> dict:
    splits = jax.random.split(jax.random.key(seed), 10)
    cell_features = normal_values(splits[0], (CELLS, D), 1.0, 6.0, ((0, 256),))
    encoded = normal_values(splits[1], (GAUGES, D), 1.0, 6.0, ((0, 128),))
    w_query = normal_values(splits[2], (D, D), (D // 2) ** -0.5, 0.375)
    w_key = normal_values(splits[3], (D, D), (D // 2) ** -0.5, 0.375)
    w_value = normal_values(splits[4], (D, D), D ** -0.5, 0.25)
    w_out = normal_values(splits[5], (D, D), D ** -0.5, 0.25)
    pattern = distinct(splits[6], GROUPS, N_TILE, KSEL, 2048)
    cell_basin = draw_cell_basin(jax.random.fold_in(splits[9], 71), 0)
    pooled_grad = normal_values(splits[8], (NBASIN, D), 4.0, 24.0, ((0, 256),))
    return dict(cell_features=cell_features, encoded=encoded, w_query=w_query, w_key=w_key, w_value=w_value, w_out=w_out, pattern=pattern, cell_basin=cell_basin, pooled_grad=pooled_grad)


score_cap = 30.0

def key_rows(source, chosen_blocks):
    shaped = source.reshape(-1, GAUGE_DEV, source.shape[1])
    return jnp.take(shaped, chosen_blocks, axis=0).reshape(-1, source.shape[1])

def add_rows(source, chosen_blocks, addend):
    shaped = source.reshape(-1, GAUGE_DEV, source.shape[1])
    shaped = shaped.at[chosen_blocks].add(addend.reshape(-1, GAUGE_DEV, source.shape[1]))
    return shaped.reshape(-1, source.shape[1])

def forward_heads(queries, key_sel, value_sel):
    row_count = queries.shape[0]
    key_count = key_sel.shape[0]
    query_heads = queries.astype(jnp.float32).reshape(row_count, HEADS, HEAD_DIM)
    key_heads = key_sel.astype(jnp.float32).reshape(key_count, HEADS, HEAD_DIM)
    value_heads = value_sel.astype(jnp.float32).reshape(key_count, HEADS, HEAD_DIM)
    scores = jnp.einsum('rhd,khd->hrk', query_heads, key_heads) * (1.0 / math.sqrt(HEAD_DIM))
    tanh_val = jnp.tanh(scores / score_cap)
    exponent = jnp.exp(score_cap * tanh_val)
    weights = exponent / lax.optimization_barrier(jnp.sum(exponent, axis=-1, keepdims=True))
    weights_bf = weights.astype(jnp.bfloat16)
    attended = jnp.einsum('hrk,khd->rhd', weights_bf.astype(jnp.float32), value_heads)
    attended = attended.reshape(row_count, HEADS * HEAD_DIM).astype(jnp.bfloat16)
    return (attended, weights, weights_bf, tanh_val)

def backward_heads(queries, key_sel, value_sel, weights, weights_bf, tanh_val, attended_grad):
    row_count = queries.shape[0]
    key_count = key_sel.shape[0]
    query_heads = queries.astype(jnp.float32).reshape(row_count, HEADS, HEAD_DIM)
    key_heads = key_sel.astype(jnp.float32).reshape(key_count, HEADS, HEAD_DIM)
    value_heads = value_sel.astype(jnp.float32).reshape(key_count, HEADS, HEAD_DIM)
    grad_heads = attended_grad.astype(jnp.float32).reshape(row_count, HEADS, HEAD_DIM)
    weight_grad = jnp.einsum('rhd,khd->hrk', grad_heads, value_heads)
    value_grad = jnp.einsum('hrk,rhd->khd', weights_bf.astype(jnp.float32), grad_heads)
    inner_sum = lax.optimization_barrier(jnp.sum(weights * weight_grad, axis=-1, keepdims=True))
    score_grad = weights * (weight_grad - inner_sum) * (1.0 - tanh_val * tanh_val) * (1.0 / math.sqrt(HEAD_DIM))
    score_grad = score_grad.astype(jnp.bfloat16).astype(jnp.float32)
    query_grad = jnp.einsum('hrk,khd->rhd', score_grad, key_heads)
    query_grad = query_grad.reshape(row_count, HEADS * HEAD_DIM).astype(jnp.bfloat16)
    key_grad = jnp.einsum('hrk,rhd->khd', score_grad, query_heads).reshape(key_count, HEADS * HEAD_DIM)
    return (query_grad, key_grad, value_grad.reshape(key_count, HEADS * HEAD_DIM))

def reference(cell_features, encoded, w_query, w_key, w_value, w_out, pattern, cell_basin, pooled_grad):
    highest = lax.Precision.HIGHEST
    queries = jnp.dot(cell_features, w_query, preferred_element_type=jnp.float32).astype(jnp.bfloat16)
    keys = jnp.dot(encoded, w_key, preferred_element_type=jnp.float32).astype(jnp.bfloat16)
    values = jnp.dot(encoded, w_value, preferred_element_type=jnp.float32).astype(jnp.bfloat16)
    group_ids = jnp.arange(GROUPS, dtype=jnp.int32)

    def forward_group(group):
        group_queries = lax.dynamic_slice_in_dim(queries, group * CELL_DEV, CELL_DEV, 0)
        chosen = pattern[group]
        return forward_heads(group_queries, key_rows(keys, chosen), key_rows(values, chosen))[0]
    attended = lax.map(forward_group, group_ids).reshape(CELLS, D)
    cell_out = jnp.dot(attended, w_out, preferred_element_type=jnp.float32).astype(jnp.bfloat16)
    counts = jax.ops.segment_sum(jnp.ones((CELLS,), jnp.float32), cell_basin, num_segments=NBASIN)
    basin_sums = jax.ops.segment_sum(cell_out.astype(jnp.float32), cell_basin, num_segments=NBASIN)
    count_root = jnp.sqrt(counts)
    pooled = (basin_sums / count_root[:, None]).astype(jnp.bfloat16)
    scaled_table = pooled_grad.astype(jnp.float32) / count_root[:, None]
    out_grad = jnp.take(scaled_table, cell_basin, axis=0).astype(jnp.bfloat16)
    grad_out_weight = jnp.dot(attended.T, out_grad, preferred_element_type=jnp.float32)
    attended_grad = jnp.dot(out_grad, w_out.T, preferred_element_type=jnp.float32).astype(jnp.bfloat16)

    def backward_group(running, group):
        key_grad, value_grad = running
        group_queries = lax.dynamic_slice_in_dim(queries, group * CELL_DEV, CELL_DEV, 0)
        group_grad = lax.dynamic_slice_in_dim(attended_grad, group * CELL_DEV, CELL_DEV, 0)
        chosen = pattern[group]
        key_sel = key_rows(keys, chosen)
        value_sel = key_rows(values, chosen)
        unused, weights, weights_bf, tanh_val = forward_heads(group_queries, key_sel, value_sel)
        query_grad, key_grad_sel, value_grad_sel = backward_heads(group_queries, key_sel, value_sel, weights, weights_bf, tanh_val, group_grad)
        key_grad = add_rows(key_grad, chosen, key_grad_sel)
        value_grad = add_rows(value_grad, chosen, value_grad_sel)
        return ((key_grad, value_grad), query_grad)
    empty = jnp.zeros((GAUGES, D), jnp.float32)
    (key_grad, value_grad), query_grad = lax.scan(backward_group, (empty, empty), group_ids)
    query_grad = query_grad.reshape(CELLS, D)
    grad_query_weight = jnp.dot(cell_features.T, query_grad, preferred_element_type=jnp.float32)
    grad_cells = jnp.dot(query_grad, w_query.T, preferred_element_type=jnp.float32).astype(jnp.bfloat16)
    encoded_wide = encoded.astype(jnp.float32)
    grad_key_weight = jnp.dot(encoded_wide.T, key_grad, precision=highest)
    grad_value_weight = jnp.dot(encoded_wide.T, value_grad, precision=highest)
    grad_gauges = jnp.dot(key_grad, w_key.astype(jnp.float32).T, precision=highest)
    grad_gauges = grad_gauges + jnp.dot(value_grad, w_value.astype(jnp.float32).T, precision=highest)
    grad_gauges = grad_gauges.astype(jnp.bfloat16)
    return (pooled, grad_cells, grad_gauges, grad_query_weight, grad_key_weight, grad_value_weight, grad_out_weight)
```

```python
import functools
import math

import jax
import jax.numpy as jnp
from jax import lax
from jax.experimental import pallas as pl
from jax.experimental.pallas import tpu as pltpu
from jax.sharding import Mesh
from jax.sharding import PartitionSpec as P

HEADS = 8
HEAD_DIM = 64
PAIR = 2 * HEAD_DIM
KEYS = 128
GAUGE_ROWS = 8
SLOTS = 16
score_cap = 30.0

EVERY = ("y", "z", "x", "c")
PLANE = ("y", "x")
SIZES = {"y": 4, "z": 8, "x": 4, "c": 2}

bf16 = jnp.bfloat16
f32 = jnp.float32


def mm(left, right):
    return jnp.dot(left, right, preferred_element_type=f32)


def mm_cols(left, right):
    return lax.dot_general(left, right, (((1,), (1,)), ((), ())), preferred_element_type=f32)


def mm_rows(left, right):
    return lax.dot_general(left, right, (((0,), (0,)), ((), ())), preferred_element_type=f32)


def two_parts(value):
    high = value.astype(bf16)
    return high, (value - high.astype(f32)).astype(bf16)


def group_kernel(
    core_ref, rows_ref, slot_ref, table_ref, mine_ref, other_ref, cells_ref,
    wq_ref, wk_ref, wv_ref, wo_ref,
    grad_cells_ref, sums_ref, keep_ref, send_ref,
):
    core = core_ref[0]
    first = core == 0
    width = 2 * mine_ref.shape[1]
    half = width // 2
    gauges = mine_ref.shape[0]
    pairs = width // PAIR
    plane = SIZES["y"] * SIZES["x"]
    gauge_chunk = gauges // plane
    weight_chunk = 4 * width // plane
    chunk = gauge_chunk + weight_chunk

    def store(row, value):
        low, high = value[:, :half].astype(bf16), value[:, half:].astype(bf16)
        count = value.shape[0]
        keep_ref[row : row + count, :] = jnp.where(first, low, high)
        send_ref[row : row + count, :] = jnp.where(first, high, low)

    def store_weight(which, value):
        per = value.shape[0] // weight_chunk
        for j in range(per):
            store(
                (which * per + j) * chunk,
                value[j * weight_chunk : (j + 1) * weight_chunk, :],
            )

    picks = jnp.where(
        lax.broadcasted_iota(jnp.int32, (gauges, KEYS), 0) == rows_ref[...], 1.0, 0.0
    ).astype(bf16)
    sel_mine = mm_rows(picks, mine_ref[...])
    sel_other = mm_rows(picks, other_ref[...])
    encoded_sel = jnp.concatenate(
        [jnp.where(first, sel_mine, sel_other), jnp.where(first, sel_other, sel_mine)], axis=1
    ).astype(bf16)
    keys = mm(encoded_sel, wk_ref[...]).astype(bf16)
    values = mm(encoded_sel, wv_ref[...]).astype(bf16)
    queries = mm(cells_ref[...], wq_ref[...]).astype(bf16)
    even = lax.broadcasted_iota(jnp.int32, (KEYS, PAIR), 1) < HEAD_DIM
    zero = jnp.zeros((KEYS, PAIR), bf16)
    scale = 1.0 / math.sqrt(HEAD_DIM)

    saved = []
    attended = []
    for p in range(pairs):
        columns = slice(p * PAIR, (p + 1) * PAIR)
        key_pair, value_pair = keys[:, columns], values[:, columns]
        key_two = jnp.concatenate(
            [jnp.where(even, key_pair, zero), jnp.where(even, zero, key_pair)], axis=0
        )
        value_two = jnp.concatenate(
            [jnp.where(even, value_pair, zero), jnp.where(even, zero, value_pair)], axis=0
        )
        query_pair = queries[:, columns]
        scores = mm_cols(query_pair, key_two) * scale
        tanh_val = jnp.tanh(scores / score_cap)
        exponent = jnp.exp(score_cap * tanh_val)
        parts = []
        for side in range(2):
            part = exponent[:, side * KEYS : (side + 1) * KEYS]
            parts.append(part / jnp.sum(part, axis=-1, keepdims=True))
        weights = jnp.concatenate(parts, axis=1)
        weights_bf = weights.astype(bf16)
        attended.append(mm(weights_bf, value_two).astype(bf16))
        saved.append((key_two, value_two, query_pair, tanh_val, weights, weights_bf))
    attended = jnp.concatenate(attended, axis=1)
    cell_out = mm(attended, wo_ref[...]).astype(bf16)
    onehot = jnp.where(
        lax.broadcasted_iota(jnp.int32, (SLOTS, cell_out.shape[0]), 0) == slot_ref[...], 1.0, 0.0
    ).astype(bf16)
    sums_ref[...] = mm(onehot, cell_out)
    out_grad = mm_rows(onehot, table_ref[...]).astype(bf16)
    attended_grad = mm_cols(out_grad, wo_ref[...]).astype(bf16)
    store_weight(3, mm_rows(attended, out_grad))

    query_grad, key_grad, value_grad = [], [], []
    for p in range(pairs):
        key_two, value_two, query_pair, tanh_val, weights, weights_bf = saved[p]
        grad_pair = attended_grad[:, p * PAIR : (p + 1) * PAIR]
        weight_grad = mm_cols(grad_pair, value_two)
        two = mm_rows(weights_bf, grad_pair)
        value_grad.append(jnp.where(even, two[:KEYS], two[KEYS:]))
        product = weights * weight_grad
        parts = []
        for side in range(2):
            columns = slice(side * KEYS, (side + 1) * KEYS)
            parts.append(
                weight_grad[:, columns] - jnp.sum(product[:, columns], axis=-1, keepdims=True)
            )
        centred = jnp.concatenate(parts, axis=1)
        score_grad = (weights * centred * (1.0 - tanh_val * tanh_val) * scale).astype(bf16)
        query_grad.append(mm(score_grad, key_two).astype(bf16))
        two = mm_rows(score_grad, query_pair)
        key_grad.append(jnp.where(even, two[:KEYS], two[KEYS:]))
    query_grad = jnp.concatenate(query_grad, axis=1)
    grad_cells_ref[...] = mm_cols(query_grad, wq_ref[...]).astype(bf16)
    store_weight(0, mm_rows(cells_ref[...], query_grad))
    key_high, key_low = two_parts(jnp.concatenate(key_grad, axis=1))
    value_high, value_low = two_parts(jnp.concatenate(value_grad, axis=1))
    store_weight(1, mm_rows(encoded_sel, key_high) + mm_rows(encoded_sel, key_low))
    store_weight(2, mm_rows(encoded_sel, value_high) + mm_rows(encoded_sel, value_low))
    grad_gauges = (
        mm_cols(key_high, wk_ref[...])
        + mm_cols(key_low, wk_ref[...])
        + mm_cols(value_high, wv_ref[...])
        + mm_cols(value_low, wv_ref[...])
    ).astype(bf16)
    for j in range(plane):
        store(
            j * chunk + weight_chunk,
            mm(picks[j * gauge_chunk : (j + 1) * gauge_chunk, :], grad_gauges),
        )


def swap(value):
    return lax.ppermute(value, "c", [(0, 1), (1, 0)])


def shifted(value, steps):
    count = lax.axis_size(EVERY)
    return lax.ppermute(value, EVERY, [(i, (i + steps) % count) for i in range(count)])


def spread(value, axes, count):
    rows, width = value.shape
    copies = jnp.broadcast_to(value[None], (count, rows, width)).reshape(count * rows, width)
    return lax.all_to_all(copies, axes, 0, 0, tiled=True)


def gathered(value):
    column = spread(value, "z", SIZES["z"])
    return spread(column, PLANE, SIZES["y"] * SIZES["x"])


def per_device(cells, encoded, w_query, w_key, w_value, w_out, pattern, cell_basin, pooled_grad):
    width = cells.shape[1]
    half = width // 2
    plane, depth = SIZES["y"] * SIZES["x"], SIZES["z"]
    core = lax.axis_index("c")
    device = lax.axis_index(EVERY)
    own = pooled_grad.shape[0]
    total = own * lax.axis_size(EVERY)

    slot = (cell_basin - device * own + own) % total
    counts = jnp.sum(
        (slot[None, :] == jnp.arange(3 * own, dtype=jnp.int32)[:, None]).astype(f32), axis=1
    )
    count_row = jnp.pad(counts.astype(bf16), (0, width - 3 * own))[None, :]
    packet = jnp.concatenate([pooled_grad, count_row], axis=0)
    below, above = shifted(packet, 1), shifted(packet, -1)
    below_two, above_two = shifted(count_row[:, :128], 2), shifted(count_row[:, :128], -2)
    own_counts = counts
    down, up = below[own, : 3 * own].astype(f32), above[own, : 3 * own].astype(f32)
    down_two, up_two = below_two[0, : 3 * own].astype(f32), above_two[0, : 3 * own].astype(f32)
    low, mid, top = slice(0, own), slice(own, 2 * own), slice(2 * own, 3 * own)
    all_counts = jnp.concatenate(
        [
            down_two[top] + down[mid] + own_counts[low],
            down[top] + own_counts[mid] + up[low],
            own_counts[top] + up[mid] + up_two[low],
        ]
    )
    roots = jnp.sqrt(all_counts)
    table = jnp.concatenate([below[:own], pooled_grad, above[:own]], axis=0).astype(f32)
    table = (table / roots[:, None]).astype(bf16)
    table = jnp.pad(table, ((0, SLOTS - 3 * own), (0, 0)))

    mine = gathered(lax.dynamic_slice_in_dim(encoded, core * half, half, 1))
    other = swap(mine)
    block = pattern[0]
    along_x = block % SIZES["x"]
    along_z = (block // SIZES["x"]) % depth
    along_y = block // (SIZES["x"] * depth)
    place = (along_y * SIZES["x"] + along_x) * depth + along_z
    rows = (
        place[:, None] * GAUGE_ROWS + jnp.arange(GAUGE_ROWS, dtype=jnp.int32)[None, :]
    ).reshape(1, KEYS)

    gauges = mine.shape[0]
    payload = gauges + 4 * width
    vmem = pl.BlockSpec(memory_space=pltpu.VMEM)
    grad_cells, sums, keep, send = pl.pallas_call(
        group_kernel,
        out_shape=(
            jax.ShapeDtypeStruct(cells.shape, bf16),
            jax.ShapeDtypeStruct((SLOTS, width), f32),
            jax.ShapeDtypeStruct((payload, half), bf16),
            jax.ShapeDtypeStruct((payload, half), bf16),
        ),
        in_specs=[pl.BlockSpec(memory_space=pltpu.SMEM)] + [vmem] * 10,
        out_specs=(vmem,) * 4,
        compiler_params=pltpu.CompilerParams(vmem_limit_bytes=48 << 20),
        name="group_kernel",
    )(
        core.reshape(1), rows, slot[None, :], table, mine, other, cells,
        w_query, w_key, w_value, w_out,
    )

    from_above, from_below = shifted(sums[low], -1), shifted(sums[top], 1)
    pooled = ((sums[mid] + from_above + from_below) / roots[mid][:, None]).astype(bf16)

    chip = (keep.astype(f32) + swap(send).astype(f32)).astype(bf16)
    chunk = payload // plane
    gauge_chunk = gauges // plane
    weight_chunk = chunk - gauge_chunk
    parts = lax.all_to_all(chip, PLANE, 0, 0, tiled=True).reshape(plane, chunk, half)
    column = jnp.sum(parts.astype(f32), axis=0).astype(bf16)
    column = jnp.concatenate(
        [
            column[:weight_chunk].reshape(depth, weight_chunk // depth, half),
            column[weight_chunk:].reshape(depth, gauge_chunk // depth, half),
        ],
        axis=1,
    )
    parts = lax.all_to_all(column, "z", 0, 0, tiled=True)
    reduced = jnp.sum(parts.astype(f32), axis=0).astype(bf16)
    own_weight = reduced[: weight_chunk // depth]
    own_gauge = reduced[weight_chunk // depth :]

    weights = gathered(own_weight)
    both = jnp.concatenate([weights, own_gauge], axis=0)
    far = swap(both)
    full = jnp.where(
        core == 0,
        jnp.concatenate([both, far], axis=1),
        jnp.concatenate([far, both], axis=1),
    )
    grads = [full[i * width : (i + 1) * width].astype(f32) for i in range(4)]
    grad_gauges = full[4 * width :]
    return (pooled, grad_cells, grad_gauges, grads[0], grads[1], grads[2], grads[3])


def solution(mesh):
    grid = Mesh(mesh.devices.reshape(tuple(SIZES[a] for a in EVERY)), EVERY)
    tiles = ("y", "z", "x")
    return jax.shard_map(
        per_device,
        mesh=grid,
        in_specs=(
            P(EVERY, None), P(tiles, None), P(), P(), P(), P(),
            P(EVERY, None), P(EVERY), P(EVERY, None),
        ),
        out_specs=(P(EVERY, None), P(EVERY, None), P(tiles, None), P(), P(), P(), P()),
        check_vma=False,
    )
```

```python
import functools
import math

import jax
import jax.numpy as jnp
from jax import lax
from jax.experimental import pallas as pl
from jax.experimental.pallas import tpu as pltpu
from jax.sharding import Mesh
from jax.sharding import PartitionSpec as P

HEADS = 8
HEAD_DIM = 64
PAIR = 2 * HEAD_DIM
KEYS = 128
GAUGE_ROWS = 8
SLOTS = 16
score_cap = 30.0

EVERY = ("y", "z", "x", "c")
PLANE = ("y", "x")
SIZES = {"y": 4, "z": 8, "x": 4, "c": 2}

bf16 = jnp.bfloat16
f32 = jnp.float32


def mm(left, right):
    return jnp.dot(left, right, preferred_element_type=f32)


def mm_cols(left, right):
    return lax.dot_general(left, right, (((1,), (1,)), ((), ())), preferred_element_type=f32)


def mm_rows(left, right):
    return lax.dot_general(left, right, (((0,), (0,)), ((), ())), preferred_element_type=f32)


def two_parts(value):
    high = value.astype(bf16)
    return high, (value - high.astype(f32)).astype(bf16)


def group_kernel(
    core_ref, rows_ref, places_ref, slot_ref, table_ref, mine_ref, other_ref,
    wk_ref, wv_ref, wq_ref, cells_hbm, wo_hbm,
    grad_cells_ref, sums_ref, keep_ref, send_ref,
    cells_ref, wo_ref, sems,
):
    load_cells = pltpu.make_async_copy(cells_hbm, cells_ref, sems.at[0])
    load_wo = pltpu.make_async_copy(wo_hbm, wo_ref, sems.at[1])
    load_cells.start()
    load_wo.start()
    core = core_ref[0]
    first = core == 0
    width = 2 * mine_ref.shape[1]
    half = width // 2
    gauges = mine_ref.shape[0]
    pairs = width // PAIR
    plane = SIZES["y"] * SIZES["x"]
    gauge_chunk = gauges // plane
    weight_chunk = 4 * width // plane
    chunk = gauge_chunk + weight_chunk

    def store(row, value):
        low, high = value[:, :half].astype(bf16), value[:, half:].astype(bf16)
        count = value.shape[0]
        keep_ref[row : row + count, :] = jnp.where(first, low, high)
        send_ref[row : row + count, :] = jnp.where(first, high, low)

    def store_weight(which, value):
        per = value.shape[0] // weight_chunk
        for j in range(per):
            store(
                (which * per + j) * chunk,
                value[j * weight_chunk : (j + 1) * weight_chunk, :],
            )

    gauge_ids = lax.broadcasted_iota(jnp.int32, (gauges, KEYS), 0)
    picks = jnp.where(gauge_ids == rows_ref[...], 1.0, 0.0).astype(bf16)
    sel_mine = mm_rows(picks, mine_ref[...])
    sel_other = mm_rows(picks, other_ref[...])
    encoded_sel = jnp.concatenate(
        [jnp.where(first, sel_mine, sel_other), jnp.where(first, sel_other, sel_mine)], axis=1
    ).astype(bf16)
    keys = mm(encoded_sel, wk_ref[...]).astype(bf16)
    values = mm(encoded_sel, wv_ref[...]).astype(bf16)
    load_cells.wait()
    queries = mm(cells_ref[...], wq_ref[...]).astype(bf16)
    even = lax.broadcasted_iota(jnp.int32, (KEYS, PAIR), 1) < HEAD_DIM
    zero = jnp.zeros((KEYS, PAIR), bf16)
    scale = 1.0 / math.sqrt(HEAD_DIM)

    saved = []
    attended = []
    for p in range(pairs):
        columns = slice(p * PAIR, (p + 1) * PAIR)
        key_pair, value_pair = keys[:, columns], values[:, columns]
        key_two = jnp.concatenate(
            [jnp.where(even, key_pair, zero), jnp.where(even, zero, key_pair)], axis=0
        )
        value_two = jnp.concatenate(
            [jnp.where(even, value_pair, zero), jnp.where(even, zero, value_pair)], axis=0
        )
        query_pair = queries[:, columns]
        scores = mm_cols(query_pair, key_two) * scale
        tanh_val = jnp.tanh(scores / score_cap)
        exponent = jnp.exp(score_cap * tanh_val)
        parts = []
        for side in range(2):
            part = exponent[:, side * KEYS : (side + 1) * KEYS]
            parts.append(part / jnp.sum(part, axis=-1, keepdims=True))
        weights = jnp.concatenate(parts, axis=1)
        weights_bf = weights.astype(bf16)
        attended.append(mm(weights_bf, value_two).astype(bf16))
        saved.append((key_two, value_two, query_pair, tanh_val, weights, weights_bf))
    attended = jnp.concatenate(attended, axis=1)
    load_wo.wait()
    cell_out = mm(attended, wo_ref[...]).astype(bf16)
    onehot = jnp.where(
        lax.broadcasted_iota(jnp.int32, (SLOTS, cell_out.shape[0]), 0) == slot_ref[...], 1.0, 0.0
    ).astype(bf16)
    sums_ref[...] = mm(onehot, cell_out)
    out_grad = mm_rows(onehot, table_ref[...]).astype(bf16)
    attended_grad = mm_cols(out_grad, wo_ref[...]).astype(bf16)
    store_weight(3, mm_rows(attended, out_grad))

    query_grad, key_grad, value_grad = [], [], []
    for p in range(pairs):
        key_two, value_two, query_pair, tanh_val, weights, weights_bf = saved[p]
        grad_pair = attended_grad[:, p * PAIR : (p + 1) * PAIR]
        weight_grad = mm_cols(grad_pair, value_two)
        two = mm_rows(weights_bf, grad_pair)
        value_grad.append(jnp.where(even, two[:KEYS], two[KEYS:]))
        product = weights * weight_grad
        parts = []
        for side in range(2):
            columns = slice(side * KEYS, (side + 1) * KEYS)
            parts.append(
                weight_grad[:, columns] - jnp.sum(product[:, columns], axis=-1, keepdims=True)
            )
        centred = jnp.concatenate(parts, axis=1)
        score_grad = (weights * centred * (1.0 - tanh_val * tanh_val) * scale).astype(bf16)
        query_grad.append(mm(score_grad, key_two).astype(bf16))
        two = mm_rows(score_grad, query_pair)
        key_grad.append(jnp.where(even, two[:KEYS], two[KEYS:]))
    query_grad = jnp.concatenate(query_grad, axis=1)
    grad_cells_ref[...] = mm_cols(query_grad, wq_ref[...]).astype(bf16)
    store_weight(0, mm_rows(cells_ref[...], query_grad))
    key_high, key_low = two_parts(jnp.concatenate(key_grad, axis=1))
    value_high, value_low = two_parts(jnp.concatenate(value_grad, axis=1))
    store_weight(1, mm_rows(encoded_sel, key_high) + mm_rows(encoded_sel, key_low))
    store_weight(2, mm_rows(encoded_sel, value_high) + mm_rows(encoded_sel, value_low))
    grad_gauges = (
        mm_cols(key_high, wk_ref[...])
        + mm_cols(key_low, wk_ref[...])
        + mm_cols(value_high, wv_ref[...])
        + mm_cols(value_low, wv_ref[...])
    ).astype(bf16)
    places = jnp.where(gauge_ids == places_ref[...], 1.0, 0.0).astype(bf16)
    for j in range(plane):
        store(
            j * chunk + weight_chunk,
            mm(places[j * gauge_chunk : (j + 1) * gauge_chunk, :], grad_gauges),
        )


def widen_kernel(core_ref, mine_ref, far_ref, *out_refs):
    first = core_ref[0] == 0
    half = mine_ref.shape[2]
    for i, out_ref in enumerate(out_refs):
        mine, far = mine_ref[i], far_ref[i]
        out_ref[:, :half] = jnp.where(first, mine, far).astype(f32)
        out_ref[:, half:] = jnp.where(first, far, mine).astype(f32)


def swap(value):
    return lax.ppermute(value, "c", [(0, 1), (1, 0)])


def shifted(value, steps):
    count = lax.axis_size(EVERY)
    return lax.ppermute(value, EVERY, [(i, (i + steps) % count) for i in range(count)])


def spread(value, axes, count):
    rows, width = value.shape
    copies = jnp.broadcast_to(value[None], (count, rows, width)).reshape(count * rows, width)
    return lax.all_to_all(copies, axes, 0, 0, tiled=True)


def after(value, *others):
    return lax.optimization_barrier((value,) + others)[0]


def per_device(cells, encoded, w_query, w_key, w_value, w_out, pattern, cell_basin, pooled_grad):
    width = cells.shape[1]
    half = width // 2
    plane, depth = SIZES["y"] * SIZES["x"], SIZES["z"]
    core = lax.axis_index("c")
    device = lax.axis_index(EVERY)
    own = pooled_grad.shape[0]
    total = own * lax.axis_size(EVERY)

    tiles = ("y", "z", "x")
    rows_own = lax.dynamic_slice_in_dim(encoded, core * half, half, 1)
    copies = jnp.broadcast_to(rows_own[None], (plane * depth,) + rows_own.shape)
    copies = copies.reshape(plane * depth * rows_own.shape[0], half)
    mine = lax.all_to_all(copies, tiles, 0, 0, tiled=True)
    other = swap(mine)

    slot = (cell_basin - device * own + own) % total
    counts = jnp.sum(
        (slot[None, :] == jnp.arange(3 * own, dtype=jnp.int32)[:, None]).astype(f32), axis=1
    )
    count_row = jnp.pad(counts.astype(bf16), (0, width - 3 * own))[None, :]
    packet = after(jnp.concatenate([pooled_grad, count_row], axis=0), copies)
    small = packet[own:, :128]
    below, above = shifted(packet, 1), shifted(packet, -1)
    below_two, above_two = shifted(small, 2), shifted(small, -2)
    own_counts = counts
    down, up = below[own, : 3 * own].astype(f32), above[own, : 3 * own].astype(f32)
    down_two, up_two = below_two[0, : 3 * own].astype(f32), above_two[0, : 3 * own].astype(f32)
    low, mid, top = slice(0, own), slice(own, 2 * own), slice(2 * own, 3 * own)
    all_counts = jnp.concatenate(
        [
            down_two[top] + down[mid] + own_counts[low],
            down[top] + own_counts[mid] + up[low],
            own_counts[top] + up[mid] + up_two[low],
        ]
    )
    roots = jnp.sqrt(all_counts)
    table = jnp.concatenate([below[:own], pooled_grad, above[:own]], axis=0).astype(f32)
    table = (table / roots[:, None]).astype(bf16)
    table = jnp.pad(table, ((0, SLOTS - 3 * own), (0, 0)))

    block = pattern[0]
    along_x = block % SIZES["x"]
    along_z = (block // SIZES["x"]) % depth
    along_y = block // (SIZES["x"] * depth)
    place = (along_y * SIZES["x"] + along_x) * depth + along_z
    within = jnp.arange(GAUGE_ROWS, dtype=jnp.int32)[None, :]
    rows = (block[:, None] * GAUGE_ROWS + within).reshape(1, KEYS)
    places = (place[:, None] * GAUGE_ROWS + within).reshape(1, KEYS)

    gauges = mine.shape[0]
    payload = gauges + 4 * width
    vmem = pl.BlockSpec(memory_space=pltpu.VMEM)
    smem = pl.BlockSpec(memory_space=pltpu.SMEM)
    hbm = pl.BlockSpec(memory_space=pltpu.HBM)
    grad_cells, sums, keep, send = pl.pallas_call(
        group_kernel,
        out_shape=(
            jax.ShapeDtypeStruct(cells.shape, bf16),
            jax.ShapeDtypeStruct((SLOTS, width), f32),
            jax.ShapeDtypeStruct((payload, half), bf16),
            jax.ShapeDtypeStruct((payload, half), bf16),
        ),
        in_specs=[smem] + [vmem] * 9 + [hbm] * 2,
        out_specs=(vmem,) * 4,
        scratch_shapes=[
            pltpu.VMEM(cells.shape, bf16),
            pltpu.VMEM(w_out.shape, bf16),
            pltpu.SemaphoreType.DMA((2,)),
        ],
        compiler_params=pltpu.CompilerParams(vmem_limit_bytes=48 << 20),
        name="group_kernel",
    )(
        core.reshape(1), rows, places, slot[None, :], table, mine, other,
        w_key, w_value, w_query, cells, w_out,
    )

    from_above, from_below = shifted(sums[low], -1), shifted(sums[top], 1)
    pooled = ((sums[mid] + from_above + from_below) / roots[mid][:, None]).astype(bf16)

    chip = (keep.astype(f32) + swap(send).astype(f32)).astype(bf16)
    chunk = payload // plane
    gauge_chunk = gauges // plane
    weight_chunk = chunk - gauge_chunk
    parts = lax.all_to_all(chip, PLANE, 0, 0, tiled=True).reshape(plane, chunk, half)
    parts = after(parts, from_above, from_below)
    column = jnp.sum(parts.astype(f32), axis=0).astype(bf16)
    column = jnp.concatenate(
        [
            jnp.broadcast_to(column[None, :weight_chunk], (depth, weight_chunk, half)),
            column[weight_chunk:].reshape(depth, gauge_chunk // depth, half),
        ],
        axis=1,
    )
    parts = lax.all_to_all(column, "z", 0, 0, tiled=True)
    reduced = jnp.sum(parts.astype(f32), axis=0).astype(bf16)
    own_gauge = reduced[weight_chunk:]
    far_gauge = swap(own_gauge)
    grad_gauges = jnp.where(
        core == 0,
        jnp.concatenate([own_gauge, far_gauge], axis=1),
        jnp.concatenate([far_gauge, own_gauge], axis=1),
    )

    weights = spread(reduced[:weight_chunk], PLANE, plane)
    weights = after(weights, far_gauge)
    far = swap(weights)
    steps = 4
    block_in = pl.BlockSpec((4, width // steps, half), lambda i: (0, i, 0))
    block_out = pl.BlockSpec((width // steps, width), lambda i: (i, 0))
    grads = pl.pallas_call(
        widen_kernel,
        out_shape=(jax.ShapeDtypeStruct((width, width), f32),) * 4,
        grid=(steps,),
        in_specs=[smem, block_in, block_in],
        out_specs=(block_out,) * 4,
        compiler_params=pltpu.CompilerParams(vmem_limit_bytes=48 << 20),
        name="widen_kernel",
    )(core.reshape(1), weights.reshape(4, width, half), far.reshape(4, width, half))
    return (pooled, grad_cells, grad_gauges, grads[0], grads[1], grads[2], grads[3])


def solution(mesh):
    grid = Mesh(mesh.devices.reshape(tuple(SIZES[a] for a in EVERY)), EVERY)
    tiles = ("y", "z", "x")
    return jax.shard_map(
        per_device,
        mesh=grid,
        in_specs=(
            P(EVERY, None), P(tiles, None), P(), P(), P(), P(),
            P(EVERY, None), P(EVERY), P(EVERY, None),
        ),
        out_specs=(P(EVERY, None), P(EVERY, None), P(tiles, None), P(), P(), P(), P()),
        check_vma=False,
    )
```

```python
import functools
import math

import jax
import jax.numpy as jnp
from jax import lax
from jax.experimental import pallas as pl
from jax.experimental.pallas import tpu as pltpu
from jax.sharding import Mesh
from jax.sharding import PartitionSpec as P

HEADS = 8
HEAD_DIM = 64
PAIR = 2 * HEAD_DIM
KEYS = 128
GAUGE_ROWS = 8
SLOTS = 16
score_cap = 30.0

EVERY = ("y", "z", "x", "c")
PLANE = ("y", "x")
SIZES = {"y": 4, "z": 8, "x": 4, "c": 2}

bf16 = jnp.bfloat16
f32 = jnp.float32


def mm(left, right):
    return jnp.dot(left, right, preferred_element_type=f32)


def mm_cols(left, right):
    return lax.dot_general(left, right, (((1,), (1,)), ((), ())), preferred_element_type=f32)


def mm_rows(left, right):
    return lax.dot_general(left, right, (((0,), (0,)), ((), ())), preferred_element_type=f32)


def two_parts(value):
    high = value.astype(bf16)
    return high, (value - high.astype(f32)).astype(bf16)


def group_kernel(
    core_ref, rows_ref, places_ref, slot_ref, table_ref, mine_ref, other_ref,
    wk_ref, wv_ref, wq_ref, cells_hbm, wo_hbm,
    grad_cells_ref, sums_ref, keep_ref, send_ref,
    cells_ref, wo_ref, sems,
):
    load_cells = pltpu.make_async_copy(cells_hbm, cells_ref, sems.at[0])
    load_wo = pltpu.make_async_copy(wo_hbm, wo_ref, sems.at[1])
    load_cells.start()
    load_wo.start()
    core = core_ref[0]
    first = core == 0
    width = 2 * mine_ref.shape[1]
    half = width // 2
    gauges = mine_ref.shape[0]
    pairs = width // PAIR
    plane = SIZES["y"] * SIZES["x"]
    gauge_chunk = gauges // plane
    weight_chunk = 4 * width // plane
    chunk = gauge_chunk + weight_chunk

    def store(row, value):
        low, high = value[:, :half].astype(bf16), value[:, half:].astype(bf16)
        count = value.shape[0]
        keep_ref[row : row + count, :] = jnp.where(first, low, high)
        send_ref[row : row + count, :] = jnp.where(first, high, low)

    def store_weight(which, value):
        per = value.shape[0] // weight_chunk
        for j in range(per):
            store(
                (which * per + j) * chunk,
                value[j * weight_chunk : (j + 1) * weight_chunk, :],
            )

    gauge_ids = lax.broadcasted_iota(jnp.int32, (gauges, KEYS), 0)
    picks = jnp.where(gauge_ids == rows_ref[...], 1.0, 0.0).astype(bf16)
    sel_mine = mm_rows(picks, mine_ref[...])
    sel_other = mm_rows(picks, other_ref[...])
    encoded_sel = jnp.concatenate(
        [jnp.where(first, sel_mine, sel_other), jnp.where(first, sel_other, sel_mine)], axis=1
    ).astype(bf16)
    keys = mm(encoded_sel, wk_ref[...]).astype(bf16)
    values = mm(encoded_sel, wv_ref[...]).astype(bf16)
    load_cells.wait()
    queries = mm(cells_ref[...], wq_ref[...]).astype(bf16)
    even = lax.broadcasted_iota(jnp.int32, (KEYS, PAIR), 1) < HEAD_DIM
    zero = jnp.zeros((KEYS, PAIR), bf16)
    scale = 1.0 / math.sqrt(HEAD_DIM)

    saved = []
    attended = []
    for p in range(pairs):
        columns = slice(p * PAIR, (p + 1) * PAIR)
        key_pair, value_pair = keys[:, columns], values[:, columns]
        key_two = jnp.concatenate(
            [jnp.where(even, key_pair, zero), jnp.where(even, zero, key_pair)], axis=0
        )
        value_two = jnp.concatenate(
            [jnp.where(even, value_pair, zero), jnp.where(even, zero, value_pair)], axis=0
        )
        query_pair = queries[:, columns]
        scores = mm_cols(query_pair, key_two) * scale
        tanh_val = jnp.tanh(scores / score_cap)
        exponent = jnp.exp(score_cap * tanh_val)
        parts = []
        for side in range(2):
            part = exponent[:, side * KEYS : (side + 1) * KEYS]
            parts.append(part / jnp.sum(part, axis=-1, keepdims=True))
        weights = jnp.concatenate(parts, axis=1)
        weights_bf = weights.astype(bf16)
        attended.append(mm(weights_bf, value_two).astype(bf16))
        saved.append((key_two, value_two, query_pair, tanh_val, weights, weights_bf))
    attended = jnp.concatenate(attended, axis=1)
    load_wo.wait()
    cell_out = mm(attended, wo_ref[...]).astype(bf16)
    onehot = jnp.where(
        lax.broadcasted_iota(jnp.int32, (SLOTS, cell_out.shape[0]), 0) == slot_ref[...], 1.0, 0.0
    ).astype(bf16)
    sums_ref[...] = mm(onehot, cell_out)
    out_grad = mm_rows(onehot, table_ref[...]).astype(bf16)
    attended_grad = mm_cols(out_grad, wo_ref[...]).astype(bf16)
    store_weight(3, mm_rows(attended, out_grad))

    query_grad, key_grad, value_grad = [], [], []
    for p in range(pairs):
        key_two, value_two, query_pair, tanh_val, weights, weights_bf = saved[p]
        grad_pair = attended_grad[:, p * PAIR : (p + 1) * PAIR]
        weight_grad = mm_cols(grad_pair, value_two)
        two = mm_rows(weights_bf, grad_pair)
        value_grad.append(jnp.where(even, two[:KEYS], two[KEYS:]))
        product = weights * weight_grad
        parts = []
        for side in range(2):
            columns = slice(side * KEYS, (side + 1) * KEYS)
            parts.append(
                weight_grad[:, columns] - jnp.sum(product[:, columns], axis=-1, keepdims=True)
            )
        centred = jnp.concatenate(parts, axis=1)
        score_grad = (weights * centred * (1.0 - tanh_val * tanh_val) * scale).astype(bf16)
        query_grad.append(mm(score_grad, key_two).astype(bf16))
        two = mm_rows(score_grad, query_pair)
        key_grad.append(jnp.where(even, two[:KEYS], two[KEYS:]))
    query_grad = jnp.concatenate(query_grad, axis=1)
    grad_cells_ref[...] = mm_cols(query_grad, wq_ref[...]).astype(bf16)
    store_weight(0, mm_rows(cells_ref[...], query_grad))
    key_high, key_low = two_parts(jnp.concatenate(key_grad, axis=1))
    value_high, value_low = two_parts(jnp.concatenate(value_grad, axis=1))
    store_weight(1, mm_rows(encoded_sel, key_high) + mm_rows(encoded_sel, key_low))
    store_weight(2, mm_rows(encoded_sel, value_high) + mm_rows(encoded_sel, value_low))
    grad_gauges = (
        mm_cols(key_high, wk_ref[...])
        + mm_cols(key_low, wk_ref[...])
        + mm_cols(value_high, wv_ref[...])
        + mm_cols(value_low, wv_ref[...])
    ).astype(bf16)
    places = jnp.where(gauge_ids == places_ref[...], 1.0, 0.0).astype(bf16)
    for j in range(plane):
        store(
            j * chunk + weight_chunk,
            mm(places[j * gauge_chunk : (j + 1) * gauge_chunk, :], grad_gauges),
        )


def widen_kernel(core_ref, mine_ref, far_ref, *out_refs):
    first = core_ref[0] == 0
    half = mine_ref.shape[2]
    for i, out_ref in enumerate(out_refs):
        mine, far = mine_ref[i], far_ref[i]
        out_ref[:, :half] = jnp.where(first, mine, far).astype(f32)
        out_ref[:, half:] = jnp.where(first, far, mine).astype(f32)


def swap(value):
    return lax.ppermute(value, "c", [(0, 1), (1, 0)])


def shifted(value, steps):
    count = lax.axis_size(EVERY)
    return lax.ppermute(value, EVERY, [(i, (i + steps) % count) for i in range(count)])


def spread(value, axes, count):
    rows, width = value.shape
    copies = jnp.broadcast_to(value[None], (count, rows, width)).reshape(count * rows, width)
    return lax.all_to_all(copies, axes, 0, 0, tiled=True)


def after(value, *others):
    return lax.optimization_barrier((value,) + others)[0]


def per_device(cells, encoded, w_query, w_key, w_value, w_out, pattern, cell_basin, pooled_grad):
    width = cells.shape[1]
    half = width // 2
    plane, depth = SIZES["y"] * SIZES["x"], SIZES["z"]
    core = lax.axis_index("c")
    device = lax.axis_index(EVERY)
    own = pooled_grad.shape[0]
    total = own * lax.axis_size(EVERY)

    tiles = ("y", "z", "x")
    rows_own = lax.dynamic_slice_in_dim(encoded, core * half, half, 1)
    copies = jnp.broadcast_to(rows_own[None], (plane * depth,) + rows_own.shape)
    copies = copies.reshape(plane * depth * rows_own.shape[0], half)
    mine = lax.all_to_all(copies, tiles, 0, 0, tiled=True)
    other = swap(mine)

    slot = (cell_basin - device * own + own) % total
    counts = jnp.sum(
        (slot[None, :] == jnp.arange(3 * own, dtype=jnp.int32)[:, None]).astype(f32), axis=1
    )
    count_row = jnp.pad(counts.astype(bf16), (0, width - 3 * own))[None, :]
    packet = after(jnp.concatenate([pooled_grad, count_row], axis=0), copies)
    small = packet[own:, :128]
    below, above = shifted(packet, 1), shifted(packet, -1)
    below_two, above_two = shifted(small, 2), shifted(small, -2)
    own_counts = counts
    down, up = below[own, : 3 * own].astype(f32), above[own, : 3 * own].astype(f32)
    down_two, up_two = below_two[0, : 3 * own].astype(f32), above_two[0, : 3 * own].astype(f32)
    low, mid, top = slice(0, own), slice(own, 2 * own), slice(2 * own, 3 * own)
    all_counts = jnp.concatenate(
        [
            down_two[top] + down[mid] + own_counts[low],
            down[top] + own_counts[mid] + up[low],
            own_counts[top] + up[mid] + up_two[low],
        ]
    )
    roots = jnp.sqrt(all_counts)
    table = jnp.concatenate([below[:own], pooled_grad, above[:own]], axis=0).astype(f32)
    table = (table / roots[:, None]).astype(bf16)
    table = jnp.pad(table, ((0, SLOTS - 3 * own), (0, 0)))

    block = pattern[0]
    along_x = block % SIZES["x"]
    along_z = (block // SIZES["x"]) % depth
    along_y = block // (SIZES["x"] * depth)
    place = (along_y * SIZES["x"] + along_x) * depth + along_z
    within = jnp.arange(GAUGE_ROWS, dtype=jnp.int32)[None, :]
    rows = (block[:, None] * GAUGE_ROWS + within).reshape(1, KEYS)
    places = (place[:, None] * GAUGE_ROWS + within).reshape(1, KEYS)

    gauges = mine.shape[0]
    payload = gauges + 4 * width
    vmem = pl.BlockSpec(memory_space=pltpu.VMEM)
    smem = pl.BlockSpec(memory_space=pltpu.SMEM)
    hbm = pl.BlockSpec(memory_space=pltpu.HBM)
    grad_cells, sums, keep, send = pl.pallas_call(
        group_kernel,
        out_shape=(
            jax.ShapeDtypeStruct(cells.shape, bf16),
            jax.ShapeDtypeStruct((SLOTS, width), f32),
            jax.ShapeDtypeStruct((payload, half), bf16),
            jax.ShapeDtypeStruct((payload, half), bf16),
        ),
        in_specs=[smem] + [vmem] * 9 + [hbm] * 2,
        out_specs=(vmem,) * 4,
        scratch_shapes=[
            pltpu.VMEM(cells.shape, bf16),
            pltpu.VMEM(w_out.shape, bf16),
            pltpu.SemaphoreType.DMA((2,)),
        ],
        compiler_params=pltpu.CompilerParams(vmem_limit_bytes=48 << 20),
        name="group_kernel",
    )(
        core.reshape(1), rows, places, slot[None, :], table, mine, other,
        w_key, w_value, w_query,
        pltpu.with_memory_space_constraint(cells, pltpu.HBM),
        pltpu.with_memory_space_constraint(w_out, pltpu.HBM),
    )

    chip = (keep.astype(f32) + swap(send).astype(f32)).astype(bf16)
    chunk = payload // plane
    gauge_chunk = gauges // plane
    weight_chunk = chunk - gauge_chunk
    parts = lax.all_to_all(chip, PLANE, 0, 0, tiled=True).reshape(plane, chunk, half)
    column = jnp.sum(parts.astype(f32), axis=0).astype(bf16)
    column = jnp.concatenate(
        [
            column[:weight_chunk].reshape(depth, weight_chunk // depth, half),
            column[weight_chunk:].reshape(depth, gauge_chunk // depth, half),
        ],
        axis=1,
    )
    parts = lax.all_to_all(column, "z", 0, 0, tiled=True)
    reduced = jnp.sum(parts.astype(f32), axis=0).astype(bf16)
    own_weight = reduced[: weight_chunk // depth]
    own_gauge = reduced[weight_chunk // depth :]

    line = spread(own_weight, "z", depth)
    weights = spread(line, PLANE, plane)
    late_sums, late_gauge = lax.optimization_barrier((sums, own_gauge, line))[:2]
    far_gauge = swap(late_gauge)
    from_above, from_below = shifted(late_sums[low], -1), shifted(late_sums[top], 1)
    weights = after(weights, far_gauge, from_above, from_below)
    pooled = ((sums[mid] + from_above + from_below) / roots[mid][:, None]).astype(bf16)
    grad_gauges = jnp.where(
        core == 0,
        jnp.concatenate([own_gauge, far_gauge], axis=1),
        jnp.concatenate([far_gauge, own_gauge], axis=1),
    )
    far = swap(weights)
    steps = 4
    block_in = pl.BlockSpec((4, width // steps, half), lambda i: (0, i, 0))
    block_out = pl.BlockSpec((width // steps, width), lambda i: (i, 0))
    grads = pl.pallas_call(
        widen_kernel,
        out_shape=(jax.ShapeDtypeStruct((width, width), f32),) * 4,
        grid=(steps,),
        in_specs=[smem, block_in, block_in],
        out_specs=(block_out,) * 4,
        compiler_params=pltpu.CompilerParams(vmem_limit_bytes=48 << 20),
        name="widen_kernel",
    )(core.reshape(1), weights.reshape(4, width, half), far.reshape(4, width, half))
    return (pooled, grad_cells, grad_gauges, grads[0], grads[1], grads[2], grads[3])


def solution(mesh):
    grid = Mesh(mesh.devices.reshape(tuple(SIZES[a] for a in EVERY)), EVERY)
    tiles = ("y", "z", "x")
    return jax.shard_map(
        per_device,
        mesh=grid,
        in_specs=(
            P(EVERY, None), P(tiles, None), P(), P(), P(), P(),
            P(EVERY, None), P(EVERY), P(EVERY, None),
        ),
        out_specs=(P(EVERY, None), P(EVERY, None), P(tiles, None), P(), P(), P(), P()),
        check_vma=False,
    )
```

```python
import functools
import math

import jax
import jax.numpy as jnp
from jax import lax
from jax.experimental import pallas as pl
from jax.experimental.pallas import tpu as pltpu
from jax.sharding import Mesh
from jax.sharding import PartitionSpec as P

HEADS = 8
HEAD_DIM = 64
PAIR = 2 * HEAD_DIM
KEYS = 128
GAUGE_ROWS = 8
SLOTS = 16
score_cap = 30.0

EVERY = ("y", "z", "x", "c")
PLANE = ("y", "x")
SIZES = {"y": 4, "z": 8, "x": 4, "c": 2}

bf16 = jnp.bfloat16
f32 = jnp.float32


def mm(left, right):
    return jnp.dot(left, right, preferred_element_type=f32)


def mm_cols(left, right):
    return lax.dot_general(left, right, (((1,), (1,)), ((), ())), preferred_element_type=f32)


def mm_rows(left, right):
    return lax.dot_general(left, right, (((0,), (0,)), ((), ())), preferred_element_type=f32)


def two_parts(value):
    high = value.astype(bf16)
    return high, (value - high.astype(f32)).astype(bf16)


def group_kernel(
    core_ref, rows_ref, places_ref, slot_ref, table_ref, mine_ref, other_ref,
    wk_ref, wv_ref, wq_ref, cells_hbm, wo_hbm,
    grad_cells_ref, sums_ref, keep_ref, send_ref,
    cells_ref, wo_ref, sems,
):
    load_cells = pltpu.make_async_copy(cells_hbm, cells_ref, sems.at[0])
    load_wo = pltpu.make_async_copy(wo_hbm, wo_ref, sems.at[1])
    load_cells.start()
    load_wo.start()
    core = core_ref[0]
    first = core == 0
    width = 2 * mine_ref.shape[1]
    half = width // 2
    gauges = mine_ref.shape[0]
    pairs = width // PAIR
    plane = SIZES["y"] * SIZES["x"]
    gauge_chunk = gauges // plane
    weight_chunk = 4 * width // plane
    chunk = gauge_chunk + weight_chunk

    def store(row, value):
        low, high = value[:, :half].astype(bf16), value[:, half:].astype(bf16)
        count = value.shape[0]
        keep_ref[row : row + count, :] = jnp.where(first, low, high)
        send_ref[row : row + count, :] = jnp.where(first, high, low)

    def store_weight(which, value):
        per = value.shape[0] // weight_chunk
        for j in range(per):
            store(
                (which * per + j) * chunk,
                value[j * weight_chunk : (j + 1) * weight_chunk, :],
            )

    gauge_ids = lax.broadcasted_iota(jnp.int32, (gauges, KEYS), 0)
    picks = jnp.where(gauge_ids == rows_ref[...], 1.0, 0.0).astype(bf16)
    sel_mine = mm_rows(picks, mine_ref[...])
    sel_other = mm_rows(picks, other_ref[...])
    encoded_sel = jnp.concatenate(
        [jnp.where(first, sel_mine, sel_other), jnp.where(first, sel_other, sel_mine)], axis=1
    ).astype(bf16)
    keys = mm(encoded_sel, wk_ref[...]).astype(bf16)
    values = mm(encoded_sel, wv_ref[...]).astype(bf16)
    load_cells.wait()
    queries = mm(cells_ref[...], wq_ref[...]).astype(bf16)
    even = lax.broadcasted_iota(jnp.int32, (KEYS, PAIR), 1) < HEAD_DIM
    zero = jnp.zeros((KEYS, PAIR), bf16)
    scale = 1.0 / math.sqrt(HEAD_DIM)

    saved = []
    attended = []
    for p in range(pairs):
        columns = slice(p * PAIR, (p + 1) * PAIR)
        key_pair, value_pair = keys[:, columns], values[:, columns]
        key_two = jnp.concatenate(
            [jnp.where(even, key_pair, zero), jnp.where(even, zero, key_pair)], axis=0
        )
        value_two = jnp.concatenate(
            [jnp.where(even, value_pair, zero), jnp.where(even, zero, value_pair)], axis=0
        )
        query_pair = queries[:, columns]
        scores = mm_cols(query_pair, key_two) * scale
        tanh_val = jnp.tanh(scores / score_cap)
        exponent = jnp.exp(score_cap * tanh_val)
        parts = []
        for side in range(2):
            part = exponent[:, side * KEYS : (side + 1) * KEYS]
            parts.append(part / jnp.sum(part, axis=-1, keepdims=True))
        weights = jnp.concatenate(parts, axis=1)
        weights_bf = weights.astype(bf16)
        attended.append(mm(weights_bf, value_two).astype(bf16))
        saved.append((key_two, value_two, query_pair, tanh_val, weights, weights_bf))
    attended = jnp.concatenate(attended, axis=1)
    load_wo.wait()
    cell_out = mm(attended, wo_ref[...]).astype(bf16)
    onehot = jnp.where(
        lax.broadcasted_iota(jnp.int32, (SLOTS, cell_out.shape[0]), 0) == slot_ref[...], 1.0, 0.0
    ).astype(bf16)
    sums_ref[...] = mm(onehot, cell_out)
    out_grad = mm_rows(onehot, table_ref[...]).astype(bf16)
    attended_grad = mm_cols(out_grad, wo_ref[...]).astype(bf16)
    store_weight(3, mm_rows(attended, out_grad))

    query_grad, key_grad, value_grad = [], [], []
    for p in range(pairs):
        key_two, value_two, query_pair, tanh_val, weights, weights_bf = saved[p]
        grad_pair = attended_grad[:, p * PAIR : (p + 1) * PAIR]
        weight_grad = mm_cols(grad_pair, value_two)
        two = mm_rows(weights_bf, grad_pair)
        value_grad.append(jnp.where(even, two[:KEYS], two[KEYS:]))
        product = weights * weight_grad
        parts = []
        for side in range(2):
            columns = slice(side * KEYS, (side + 1) * KEYS)
            parts.append(
                weight_grad[:, columns] - jnp.sum(product[:, columns], axis=-1, keepdims=True)
            )
        centred = jnp.concatenate(parts, axis=1)
        score_grad = (weights * centred * (1.0 - tanh_val * tanh_val) * scale).astype(bf16)
        query_grad.append(mm(score_grad, key_two).astype(bf16))
        two = mm_rows(score_grad, query_pair)
        key_grad.append(jnp.where(even, two[:KEYS], two[KEYS:]))
    query_grad = jnp.concatenate(query_grad, axis=1)
    grad_cells_ref[...] = mm_cols(query_grad, wq_ref[...]).astype(bf16)
    store_weight(0, mm_rows(cells_ref[...], query_grad))
    key_high, key_low = two_parts(jnp.concatenate(key_grad, axis=1))
    value_high, value_low = two_parts(jnp.concatenate(value_grad, axis=1))
    store_weight(1, mm_rows(encoded_sel, key_high) + mm_rows(encoded_sel, key_low))
    store_weight(2, mm_rows(encoded_sel, value_high) + mm_rows(encoded_sel, value_low))
    grad_gauges = (
        mm_cols(key_high, wk_ref[...])
        + mm_cols(key_low, wk_ref[...])
        + mm_cols(value_high, wv_ref[...])
        + mm_cols(value_low, wv_ref[...])
    ).astype(bf16)
    places = jnp.where(gauge_ids == places_ref[...], 1.0, 0.0).astype(bf16)
    for j in range(plane):
        store(
            j * chunk + weight_chunk,
            mm(places[j * gauge_chunk : (j + 1) * gauge_chunk, :], grad_gauges),
        )


def widen_kernel(side_ref, part_ref, *refs):
    for i, out_ref in enumerate(refs[-4:]):
        out_ref[...] = part_ref[i].astype(f32)


def widen(side, part, grads):
    half = part.shape[1]
    width = 2 * half
    steps = 4
    given = () if grads is None else tuple(grads)
    block_in = pl.BlockSpec((4, width // steps, half), lambda i, side: (0, i, 0))
    block_out = pl.BlockSpec((width // steps, half), lambda i, side: (i, side[0]))
    return pl.pallas_call(
        widen_kernel,
        out_shape=(jax.ShapeDtypeStruct((width, width), f32),) * 4,
        grid_spec=pltpu.PrefetchScalarGridSpec(
            num_scalar_prefetch=1,
            grid=(steps,),
            in_specs=[block_in] + [pl.BlockSpec(memory_space=pl.ANY)] * len(given),
            out_specs=(block_out,) * 4,
        ),
        input_output_aliases={2 + i: i for i in range(len(given))},
        compiler_params=pltpu.CompilerParams(vmem_limit_bytes=48 << 20),
        name="widen_kernel",
    )(side.reshape(1), part.reshape(4, width, half), *given)


def swap(value):
    return lax.ppermute(value, "c", [(0, 1), (1, 0)])


def shifted(value, steps):
    count = lax.axis_size(EVERY)
    return lax.ppermute(value, EVERY, [(i, (i + steps) % count) for i in range(count)])


def spread(value, axes, count):
    rows, width = value.shape
    copies = jnp.broadcast_to(value[None], (count, rows, width)).reshape(count * rows, width)
    return lax.all_to_all(copies, axes, 0, 0, tiled=True)


def after(value, *others):
    return lax.optimization_barrier((value,) + others)[0]


def per_device(cells, encoded, w_query, w_key, w_value, w_out, pattern, cell_basin, pooled_grad):
    width = cells.shape[1]
    half = width // 2
    plane, depth = SIZES["y"] * SIZES["x"], SIZES["z"]
    core = lax.axis_index("c")
    device = lax.axis_index(EVERY)
    own = pooled_grad.shape[0]
    total = own * lax.axis_size(EVERY)

    tiles = ("y", "z", "x")
    rows_own = lax.dynamic_slice_in_dim(encoded, core * half, half, 1)
    copies = jnp.broadcast_to(rows_own[None], (plane * depth,) + rows_own.shape)
    copies = copies.reshape(plane * depth * rows_own.shape[0], half)
    mine = lax.all_to_all(copies, tiles, 0, 0, tiled=True)
    other = swap(mine)

    slot = (cell_basin - device * own + own) % total
    counts = jnp.sum(
        (slot[None, :] == jnp.arange(3 * own, dtype=jnp.int32)[:, None]).astype(f32), axis=1
    )
    count_row = jnp.pad(counts.astype(bf16), (0, width - 3 * own))[None, :]
    packet = after(jnp.concatenate([pooled_grad, count_row], axis=0), copies)
    small = packet[own:, :128]
    below, above = shifted(packet, 1), shifted(packet, -1)
    below_two, above_two = shifted(small, 2), shifted(small, -2)
    own_counts = counts
    down, up = below[own, : 3 * own].astype(f32), above[own, : 3 * own].astype(f32)
    down_two, up_two = below_two[0, : 3 * own].astype(f32), above_two[0, : 3 * own].astype(f32)
    low, mid, top = slice(0, own), slice(own, 2 * own), slice(2 * own, 3 * own)
    all_counts = jnp.concatenate(
        [
            down_two[top] + down[mid] + own_counts[low],
            down[top] + own_counts[mid] + up[low],
            own_counts[top] + up[mid] + up_two[low],
        ]
    )
    roots = jnp.sqrt(all_counts)
    table = jnp.concatenate([below[:own], pooled_grad, above[:own]], axis=0).astype(f32)
    table = (table / roots[:, None]).astype(bf16)
    table = jnp.pad(table, ((0, SLOTS - 3 * own), (0, 0)))

    block = pattern[0]
    along_x = block % SIZES["x"]
    along_z = (block // SIZES["x"]) % depth
    along_y = block // (SIZES["x"] * depth)
    place = (along_y * SIZES["x"] + along_x) * depth + along_z
    within = jnp.arange(GAUGE_ROWS, dtype=jnp.int32)[None, :]
    rows = (block[:, None] * GAUGE_ROWS + within).reshape(1, KEYS)
    places = (place[:, None] * GAUGE_ROWS + within).reshape(1, KEYS)

    gauges = mine.shape[0]
    payload = gauges + 4 * width
    vmem = pl.BlockSpec(memory_space=pltpu.VMEM)
    smem = pl.BlockSpec(memory_space=pltpu.SMEM)
    hbm = pl.BlockSpec(memory_space=pltpu.HBM)
    grad_cells, sums, keep, send = pl.pallas_call(
        group_kernel,
        out_shape=(
            jax.ShapeDtypeStruct(cells.shape, bf16),
            jax.ShapeDtypeStruct((SLOTS, width), f32),
            jax.ShapeDtypeStruct((payload, half), bf16),
            jax.ShapeDtypeStruct((payload, half), bf16),
        ),
        in_specs=[smem] + [vmem] * 9 + [hbm] * 2,
        out_specs=(vmem,) * 4,
        scratch_shapes=[
            pltpu.VMEM(cells.shape, bf16),
            pltpu.VMEM(w_out.shape, bf16),
            pltpu.SemaphoreType.DMA((2,)),
        ],
        compiler_params=pltpu.CompilerParams(vmem_limit_bytes=48 << 20),
        name="group_kernel",
    )(
        core.reshape(1), rows, places, slot[None, :], table, mine, other,
        w_key, w_value, w_query,
        pltpu.with_memory_space_constraint(cells, pltpu.HBM),
        pltpu.with_memory_space_constraint(w_out, pltpu.HBM),
    )

    chip = (keep.astype(f32) + swap(send).astype(f32)).astype(bf16)
    chunk = payload // plane
    gauge_chunk = gauges // plane
    weight_chunk = chunk - gauge_chunk
    parts = lax.all_to_all(chip, PLANE, 0, 0, tiled=True).reshape(plane, chunk, half)
    column = jnp.sum(parts.astype(f32), axis=0).astype(bf16)
    column = jnp.concatenate(
        [
            column[:weight_chunk].reshape(depth, weight_chunk // depth, half),
            column[weight_chunk:].reshape(depth, gauge_chunk // depth, half),
        ],
        axis=1,
    )
    parts = lax.all_to_all(column, "z", 0, 0, tiled=True)
    reduced = jnp.sum(parts.astype(f32), axis=0).astype(bf16)
    own_weight = reduced[: weight_chunk // depth]
    own_gauge = reduced[weight_chunk // depth :]

    line = spread(own_weight, "z", depth)
    late_sums, late_gauge = lax.optimization_barrier((sums, own_gauge))
    far_gauge = swap(late_gauge)
    from_above, from_below = shifted(late_sums[low], -1), shifted(late_sums[top], 1)
    line = after(line, far_gauge, from_above, from_below)
    weights = spread(line, PLANE, plane)
    pooled = ((sums[mid] + from_above + from_below) / roots[mid][:, None]).astype(bf16)
    grad_gauges = jnp.where(
        core == 0,
        jnp.concatenate([own_gauge, far_gauge], axis=1),
        jnp.concatenate([far_gauge, own_gauge], axis=1),
    )
    far = swap(weights)
    grads = widen(core, weights, None)
    grads = widen(1 - core, far, grads)
    return (pooled, grad_cells, grad_gauges, grads[0], grads[1], grads[2], grads[3])


def solution(mesh):
    grid = Mesh(mesh.devices.reshape(tuple(SIZES[a] for a in EVERY)), EVERY)
    tiles = ("y", "z", "x")
    return jax.shard_map(
        per_device,
        mesh=grid,
        in_specs=(
            P(EVERY, None), P(tiles, None), P(), P(), P(), P(),
            P(EVERY, None), P(EVERY), P(EVERY, None),
        ),
        out_specs=(P(EVERY, None), P(EVERY, None), P(tiles, None), P(), P(), P(), P()),
        check_vma=False,
    )
```

```python
import functools
import math

import jax
import jax.numpy as jnp
from jax import lax
from jax.experimental import pallas as pl
from jax.experimental.pallas import tpu as pltpu
from jax.sharding import Mesh
from jax.sharding import PartitionSpec as P

HEADS = 8
HEAD_DIM = 64
PAIR = 2 * HEAD_DIM
KEYS = 128
GAUGE_ROWS = 8
SLOTS = 16
score_cap = 30.0

EVERY = ("y", "far", "near", "x", "c")
TILES = ("y", "far", "near", "x")
GROUP = ("y", "x", "near")
SIZES = {"y": 4, "far": 4, "near": 2, "x": 4, "c": 2}
MEMBERS = SIZES["y"] * SIZES["x"] * SIZES["near"]

bf16 = jnp.bfloat16
f32 = jnp.float32


def mm(left, right):
    return jnp.dot(left, right, preferred_element_type=f32)


def mm_cols(left, right):
    return lax.dot_general(left, right, (((1,), (1,)), ((), ())), preferred_element_type=f32)


def mm_rows(left, right):
    return lax.dot_general(left, right, (((0,), (0,)), ((), ())), preferred_element_type=f32)


def two_parts(value):
    high = value.astype(bf16)
    return high, (value - high.astype(f32)).astype(bf16)


def group_kernel(
    core_ref, rows_ref, places_ref, slot_ref, table_ref, mine_ref, other_ref,
    wk_ref, wv_ref, wq_ref, cells_hbm, wo_hbm,
    grad_cells_ref, sums_ref, keep_ref, send_ref,
    cells_ref, wo_ref, sems,
):
    load_cells = pltpu.make_async_copy(cells_hbm, cells_ref, sems.at[0])
    load_wo = pltpu.make_async_copy(wo_hbm, wo_ref, sems.at[1])
    load_cells.start()
    load_wo.start()
    core = core_ref[0]
    first = core == 0
    width = 2 * mine_ref.shape[1]
    half = width // 2
    gauges = mine_ref.shape[0]
    pairs = width // PAIR
    gauge_chunk = gauges // MEMBERS
    weight_chunk = 4 * width // MEMBERS
    chunk = gauge_chunk + weight_chunk

    def store(row, value):
        low, high = value[:, :half].astype(bf16), value[:, half:].astype(bf16)
        count = value.shape[0]
        keep_ref[row : row + count, :] = jnp.where(first, low, high)
        send_ref[row : row + count, :] = jnp.where(first, high, low)

    def store_weight(which, value):
        per = value.shape[0] // weight_chunk
        for j in range(per):
            store(
                (which * per + j) * chunk,
                value[j * weight_chunk : (j + 1) * weight_chunk, :],
            )

    gauge_ids = lax.broadcasted_iota(jnp.int32, (gauges, KEYS), 0)
    picks = jnp.where(gauge_ids == rows_ref[...], 1.0, 0.0).astype(bf16)
    sel_mine = mm_rows(picks, mine_ref[...])
    sel_other = mm_rows(picks, other_ref[...])
    encoded_sel = jnp.concatenate(
        [jnp.where(first, sel_mine, sel_other), jnp.where(first, sel_other, sel_mine)], axis=1
    ).astype(bf16)
    keys = mm(encoded_sel, wk_ref[...]).astype(bf16)
    values = mm(encoded_sel, wv_ref[...]).astype(bf16)
    load_cells.wait()
    queries = mm(cells_ref[...], wq_ref[...]).astype(bf16)
    even = lax.broadcasted_iota(jnp.int32, (KEYS, PAIR), 1) < HEAD_DIM
    zero = jnp.zeros((KEYS, PAIR), bf16)
    scale = 1.0 / math.sqrt(HEAD_DIM)

    saved = []
    attended = []
    for p in range(pairs):
        columns = slice(p * PAIR, (p + 1) * PAIR)
        key_pair, value_pair = keys[:, columns], values[:, columns]
        key_two = jnp.concatenate(
            [jnp.where(even, key_pair, zero), jnp.where(even, zero, key_pair)], axis=0
        )
        value_two = jnp.concatenate(
            [jnp.where(even, value_pair, zero), jnp.where(even, zero, value_pair)], axis=0
        )
        query_pair = queries[:, columns]
        scores = mm_cols(query_pair, key_two) * scale
        tanh_val = jnp.tanh(scores / score_cap)
        exponent = jnp.exp(score_cap * tanh_val)
        parts = []
        for side in range(2):
            part = exponent[:, side * KEYS : (side + 1) * KEYS]
            parts.append(part / jnp.sum(part, axis=-1, keepdims=True))
        weights = jnp.concatenate(parts, axis=1)
        weights_bf = weights.astype(bf16)
        attended.append(mm(weights_bf, value_two).astype(bf16))
        saved.append((key_two, value_two, query_pair, tanh_val, weights, weights_bf))
    attended = jnp.concatenate(attended, axis=1)
    load_wo.wait()
    cell_out = mm(attended, wo_ref[...]).astype(bf16)
    onehot = jnp.where(
        lax.broadcasted_iota(jnp.int32, (SLOTS, cell_out.shape[0]), 0) == slot_ref[...], 1.0, 0.0
    ).astype(bf16)
    sums_ref[...] = mm(onehot, cell_out)
    out_grad = mm_rows(onehot, table_ref[...]).astype(bf16)
    attended_grad = mm_cols(out_grad, wo_ref[...]).astype(bf16)
    store_weight(3, mm_rows(attended, out_grad))

    query_grad, key_grad, value_grad = [], [], []
    for p in range(pairs):
        key_two, value_two, query_pair, tanh_val, weights, weights_bf = saved[p]
        grad_pair = attended_grad[:, p * PAIR : (p + 1) * PAIR]
        weight_grad = mm_cols(grad_pair, value_two)
        two = mm_rows(weights_bf, grad_pair)
        value_grad.append(jnp.where(even, two[:KEYS], two[KEYS:]))
        product = weights * weight_grad
        parts = []
        for side in range(2):
            columns = slice(side * KEYS, (side + 1) * KEYS)
            parts.append(
                weight_grad[:, columns] - jnp.sum(product[:, columns], axis=-1, keepdims=True)
            )
        centred = jnp.concatenate(parts, axis=1)
        score_grad = (weights * centred * (1.0 - tanh_val * tanh_val) * scale).astype(bf16)
        query_grad.append(mm(score_grad, key_two).astype(bf16))
        two = mm_rows(score_grad, query_pair)
        key_grad.append(jnp.where(even, two[:KEYS], two[KEYS:]))
    query_grad = jnp.concatenate(query_grad, axis=1)
    grad_cells_ref[...] = mm_cols(query_grad, wq_ref[...]).astype(bf16)
    store_weight(0, mm_rows(cells_ref[...], query_grad))
    key_high, key_low = two_parts(jnp.concatenate(key_grad, axis=1))
    value_high, value_low = two_parts(jnp.concatenate(value_grad, axis=1))
    store_weight(1, mm_rows(encoded_sel, key_high) + mm_rows(encoded_sel, key_low))
    store_weight(2, mm_rows(encoded_sel, value_high) + mm_rows(encoded_sel, value_low))
    grad_gauges = (
        mm_cols(key_high, wk_ref[...])
        + mm_cols(key_low, wk_ref[...])
        + mm_cols(value_high, wv_ref[...])
        + mm_cols(value_low, wv_ref[...])
    ).astype(bf16)
    places = jnp.where(gauge_ids == places_ref[...], 1.0, 0.0).astype(bf16)
    for j in range(MEMBERS):
        store(
            j * chunk + weight_chunk,
            mm(places[j * gauge_chunk : (j + 1) * gauge_chunk, :], grad_gauges),
        )


def widen_kernel(side_ref, part_ref, *refs):
    out_refs, (wide_ref, sems) = refs[-6:-2], refs[-2:]
    half = part_ref.shape[2]
    columns = pl.ds(pl.multiple_of(side_ref[0] * half, half), half)
    copies = []
    for i, out_ref in enumerate(out_refs):
        wide_ref[i] = part_ref[i].astype(f32)
        copies.append(
            pltpu.make_async_copy(wide_ref.at[i], out_ref.at[:, columns], sems.at[i])
        )
        copies[-1].start()
    for copy in copies:
        copy.wait()


def widen(side, part, grads):
    half = part.shape[1]
    width = 2 * half
    given = () if grads is None else tuple(grads)
    hbm = pl.BlockSpec(memory_space=pltpu.HBM)
    return pl.pallas_call(
        widen_kernel,
        out_shape=(jax.ShapeDtypeStruct((width, width), f32),) * 4,
        in_specs=[
            pl.BlockSpec(memory_space=pltpu.SMEM),
            pl.BlockSpec(memory_space=pltpu.VMEM),
        ]
        + [hbm] * len(given),
        out_specs=(hbm,) * 4,
        scratch_shapes=[
            pltpu.VMEM((4, width, half), f32),
            pltpu.SemaphoreType.DMA((4,)),
        ],
        input_output_aliases={2 + i: i for i in range(len(given))},
        compiler_params=pltpu.CompilerParams(vmem_limit_bytes=32 << 20),
        name="widen_kernel",
    )(side.reshape(1), part.reshape(4, width, half), *given)


def swap(value):
    return lax.ppermute(value, "c", [(0, 1), (1, 0)])


def shifted(value, steps):
    count = lax.axis_size(EVERY)
    return lax.ppermute(value, EVERY, [(i, (i + steps) % count) for i in range(count)])


def copied(value, count):
    rows, width = value.shape
    return jnp.broadcast_to(value[None], (count, rows, width)).reshape(count * rows, width)


def after(value, *others):
    return lax.optimization_barrier((value,) + others)[0]


def per_device(cells, encoded, w_query, w_key, w_value, w_out, pattern, cell_basin, pooled_grad):
    width = cells.shape[1]
    half = width // 2
    core = lax.axis_index("c")
    device = lax.axis_index(EVERY)
    own = pooled_grad.shape[0]
    total = own * lax.axis_size(EVERY)

    rows_own = lax.dynamic_slice_in_dim(encoded, core * half, half, 1)
    copies = copied(rows_own, MEMBERS * SIZES["far"])
    mine = lax.all_to_all(copies, TILES, 0, 0, tiled=True)
    other = swap(mine)

    slot = (cell_basin - device * own + own) % total
    counts = jnp.sum(
        (slot[None, :] == jnp.arange(3 * own, dtype=jnp.int32)[:, None]).astype(f32), axis=1
    )
    count_row = jnp.pad(counts.astype(bf16), (0, width - 3 * own))[None, :]
    packet = after(jnp.concatenate([pooled_grad, count_row], axis=0), copies)
    small = packet[own:, :128]
    below, above = shifted(packet, 1), shifted(packet, -1)
    below_two, above_two = shifted(small, 2), shifted(small, -2)
    own_counts = counts
    down, up = below[own, : 3 * own].astype(f32), above[own, : 3 * own].astype(f32)
    down_two, up_two = below_two[0, : 3 * own].astype(f32), above_two[0, : 3 * own].astype(f32)
    low, mid, top = slice(0, own), slice(own, 2 * own), slice(2 * own, 3 * own)
    all_counts = jnp.concatenate(
        [
            down_two[top] + down[mid] + own_counts[low],
            down[top] + own_counts[mid] + up[low],
            own_counts[top] + up[mid] + up_two[low],
        ]
    )
    roots = jnp.sqrt(all_counts)
    table = jnp.concatenate([below[:own], pooled_grad, above[:own]], axis=0).astype(f32)
    table = (table / roots[:, None]).astype(bf16)
    table = jnp.pad(table, ((0, SLOTS - 3 * own), (0, 0)))

    block = pattern[0]
    along_x = block % SIZES["x"]
    near = (block // SIZES["x"]) % SIZES["near"]
    far_z = (block // (SIZES["x"] * SIZES["near"])) % SIZES["far"]
    along_y = block // (SIZES["x"] * SIZES["near"] * SIZES["far"])
    place = (along_y * SIZES["x"] + along_x) * SIZES["near"] + near
    place = place * SIZES["far"] + far_z
    within = jnp.arange(GAUGE_ROWS, dtype=jnp.int32)[None, :]
    rows = (block[:, None] * GAUGE_ROWS + within).reshape(1, KEYS)
    places = (place[:, None] * GAUGE_ROWS + within).reshape(1, KEYS)

    gauges = mine.shape[0]
    payload = gauges + 4 * width
    vmem = pl.BlockSpec(memory_space=pltpu.VMEM)
    smem = pl.BlockSpec(memory_space=pltpu.SMEM)
    hbm = pl.BlockSpec(memory_space=pltpu.HBM)
    grad_cells, sums, keep, send = pl.pallas_call(
        group_kernel,
        out_shape=(
            jax.ShapeDtypeStruct(cells.shape, bf16),
            jax.ShapeDtypeStruct((SLOTS, width), f32),
            jax.ShapeDtypeStruct((payload, half), bf16),
            jax.ShapeDtypeStruct((payload, half), bf16),
        ),
        in_specs=[smem] + [vmem] * 9 + [hbm] * 2,
        out_specs=(vmem,) * 4,
        scratch_shapes=[
            pltpu.VMEM(cells.shape, bf16),
            pltpu.VMEM(w_out.shape, bf16),
            pltpu.SemaphoreType.DMA((2,)),
        ],
        compiler_params=pltpu.CompilerParams(vmem_limit_bytes=48 << 20),
        name="group_kernel",
    )(
        core.reshape(1), rows, places, slot[None, :], table, mine, other,
        w_key, w_value, w_query,
        pltpu.with_memory_space_constraint(cells, pltpu.HBM),
        pltpu.with_memory_space_constraint(w_out, pltpu.HBM),
    )

    chip = (keep.astype(f32) + swap(send).astype(f32)).astype(bf16)
    chunk = payload // MEMBERS
    gauge_chunk = gauges // MEMBERS
    weight_chunk = chunk - gauge_chunk
    parts = lax.all_to_all(chip, GROUP, 0, 0, tiled=True).reshape(MEMBERS, chunk, half)
    column = jnp.sum(parts.astype(f32), axis=0).astype(bf16)
    count = SIZES["far"]
    turns = [
        lax.ppermute(column, "far", [(i, (i + s) % count) for i in range(count)])
        for s in range(1, count)
    ]
    reduced = (
        (column.astype(f32) + turns[1].astype(f32)) + (turns[0].astype(f32) + turns[2].astype(f32))
    ).astype(bf16)
    own_gauge = lax.dynamic_slice_in_dim(
        reduced, weight_chunk + lax.axis_index("far") * GAUGE_ROWS, GAUGE_ROWS, 0
    )

    copies = copied(reduced[:weight_chunk], MEMBERS)
    weights = lax.all_to_all(copies, GROUP, 0, 0, tiled=True)
    late_sums, late_gauge = lax.optimization_barrier((sums, own_gauge, copies))[:2]
    far_gauge = swap(late_gauge)
    from_above, from_below = shifted(late_sums[low], -1), shifted(late_sums[top], 1)
    weights = after(weights, far_gauge, from_above, from_below)
    pooled = ((sums[mid] + from_above + from_below) / roots[mid][:, None]).astype(bf16)
    grad_gauges = jnp.where(
        core == 0,
        jnp.concatenate([own_gauge, far_gauge], axis=1),
        jnp.concatenate([far_gauge, own_gauge], axis=1),
    )
    far = swap(weights)
    grads = widen(core, weights, None)
    grads = widen(1 - core, far, grads)
    return (pooled, grad_cells, grad_gauges, grads[0], grads[1], grads[2], grads[3])


def solution(mesh):
    grid = Mesh(mesh.devices.reshape(tuple(SIZES[a] for a in EVERY)), EVERY)
    return jax.shard_map(
        per_device,
        mesh=grid,
        in_specs=(
            P(EVERY, None), P(TILES, None), P(), P(), P(), P(),
            P(EVERY, None), P(EVERY), P(EVERY, None),
        ),
        out_specs=(P(EVERY, None), P(EVERY, None), P(TILES, None), P(), P(), P(), P()),
        check_vma=False,
    )
```

```python
import functools
import math

import jax
import jax.numpy as jnp
from jax import lax
from jax.experimental import pallas as pl
from jax.experimental.pallas import tpu as pltpu
from jax.sharding import Mesh
from jax.sharding import PartitionSpec as P

HEADS = 8
HEAD_DIM = 64
PAIR = 2 * HEAD_DIM
KEYS = 128
GAUGE_ROWS = 8
SLOTS = 16
score_cap = 30.0

EVERY = ("y", "far", "near", "x", "c")
TILES = ("y", "far", "near", "x")
GROUP = ("y", "x", "near")
SIZES = {"y": 4, "far": 4, "near": 2, "x": 4, "c": 2}
MEMBERS = SIZES["y"] * SIZES["x"] * SIZES["near"]

bf16 = jnp.bfloat16
f32 = jnp.float32


def mm(left, right):
    return jnp.dot(left, right, preferred_element_type=f32)


def mm_cols(left, right):
    return lax.dot_general(left, right, (((1,), (1,)), ((), ())), preferred_element_type=f32)


def mm_rows(left, right):
    return lax.dot_general(left, right, (((0,), (0,)), ((), ())), preferred_element_type=f32)


def two_parts(value):
    high = value.astype(bf16)
    return high, (value - high.astype(f32)).astype(bf16)


def group_kernel(
    core_ref, places_ref, slot_ref, own_ref, below_ref, above_ref, below_two_ref, above_two_ref,
    mine_ref, other_ref, wk_ref, wv_ref, wq_ref, cells_hbm, wo_hbm,
    grad_cells_ref, sums_ref, keep_ref, send_ref,
    cells_ref, wo_ref, table_ref, sems,
):
    load_cells = pltpu.make_async_copy(cells_hbm, cells_ref, sems.at[0])
    load_wo = pltpu.make_async_copy(wo_hbm, wo_ref, sems.at[1])
    load_cells.start()
    load_wo.start()
    first = core_ref[0] == 0
    width = 2 * mine_ref.shape[1]
    half = width // 2
    gauges = mine_ref.shape[0]
    pairs = width // PAIR
    gauge_chunk = gauges // MEMBERS
    weight_chunk = 4 * width // MEMBERS
    chunk = gauge_chunk + weight_chunk

    def store(row, value):
        low, high = value[:, :half].astype(bf16), value[:, half:].astype(bf16)
        count = value.shape[0]
        keep_ref[row : row + count, :] = jnp.where(first, low, high)
        send_ref[row : row + count, :] = jnp.where(first, high, low)

    def store_weight(which, value):
        per = value.shape[0] // weight_chunk
        for j in range(per):
            store(
                (which * per + j) * chunk,
                value[j * weight_chunk : (j + 1) * weight_chunk, :],
            )

    down = jnp.broadcast_to(places_ref[...], (KEYS, KEYS)).T
    lanes = lax.broadcasted_iota(jnp.int32, (KEYS, KEYS), 1)
    picks = jnp.concatenate(
        [
            jnp.where(lanes + j * KEYS == down, 1.0, 0.0).astype(bf16)
            for j in range(gauges // KEYS)
        ],
        axis=1,
    )
    sel_mine = mm(picks, mine_ref[...])
    sel_other = mm(picks, other_ref[...])
    encoded_sel = jnp.concatenate(
        [jnp.where(first, sel_mine, sel_other), jnp.where(first, sel_other, sel_mine)], axis=1
    ).astype(bf16)
    keys = mm(encoded_sel, wk_ref[...]).astype(bf16)
    values = mm(encoded_sel, wv_ref[...]).astype(bf16)
    scale = 1.0 / math.sqrt(HEAD_DIM)
    load_cells.wait()
    queries = mm(cells_ref[...], wq_ref[...]).astype(bf16) * jnp.asarray(scale, bf16)
    even = lax.broadcasted_iota(jnp.int32, (KEYS, PAIR), 1) < HEAD_DIM
    upper = lax.broadcasted_iota(jnp.int32, (PAIR, KEYS), 0) < HEAD_DIM
    zero = jnp.zeros((KEYS, PAIR), bf16)

    def both(value):
        return jnp.concatenate([jnp.where(even, value, zero), jnp.where(even, zero, value)], axis=0)

    def both_across(value):
        turned = value.T
        return jnp.concatenate(
            [jnp.where(upper, turned, zero), jnp.where(upper, zero, turned)], axis=1
        )

    saved = []
    attended = []
    for p in range(pairs):
        columns = slice(p * PAIR, (p + 1) * PAIR)
        key_two, value_two = both(keys[:, columns]), both(values[:, columns])
        query_pair = queries[:, columns]
        tanh_val = jnp.tanh(mm_cols(key_two, query_pair) * (1.0 / score_cap))
        exponent = jnp.exp(score_cap * tanh_val)
        parts = []
        for side in range(2):
            part = exponent[side * KEYS : (side + 1) * KEYS]
            parts.append(part * (1.0 / jnp.sum(part, axis=0, keepdims=True)))
        weights = jnp.concatenate(parts, axis=0)
        weights_bf = weights.astype(bf16)
        attended.append(mm(both_across(values[:, columns]), weights_bf).astype(bf16))
        saved.append((value_two, query_pair, tanh_val, weights, weights_bf))
    attended = jnp.concatenate(attended, axis=0)
    load_wo.wait()
    cell_out = mm(attended.T, wo_ref[...]).astype(bf16)
    onehot = jnp.where(
        lax.broadcasted_iota(jnp.int32, (SLOTS, cell_out.shape[0]), 0) == slot_ref[...], 1.0, 0.0
    ).astype(bf16)
    sums_ref[...] = mm(onehot, cell_out)

    basins = own_ref.shape[0] - 1
    row = lax.broadcasted_iota(jnp.int32, (SLOTS, 128), 0)
    lane = lax.broadcasted_iota(jnp.int32, (SLOTS, 128), 1)
    counts = jnp.zeros((SLOTS, 128), f32)
    for offset, source in (
        (2 * basins, below_two_ref[0:1, :]),
        (basins, below_ref[basins : basins + 1, :128]),
        (0, own_ref[basins : basins + 1, :128]),
        (-basins, above_ref[basins : basins + 1, :128]),
        (-2 * basins, above_two_ref[0:1, :]),
    ):
        counts = counts + jnp.where(lane == row + offset, source.astype(f32), 0.0)
    counts = jnp.sum(counts, axis=1, keepdims=True)
    used = lax.broadcasted_iota(jnp.int32, (SLOTS, 1), 0) < 3 * basins
    table_ref[...] = jnp.zeros_like(table_ref)
    for place, source in enumerate((below_ref, own_ref, above_ref)):
        table_ref[place * basins : (place + 1) * basins, :] = source[0:basins, :].astype(f32)
    table = (table_ref[...] / jnp.sqrt(jnp.where(used, counts, 1.0))).astype(bf16)
    out_grad = mm_rows(onehot, table).astype(bf16)
    attended_grad = mm_cols(out_grad, wo_ref[...]).astype(bf16)
    store_weight(3, mm(attended, out_grad))

    query_grad, key_grad, value_grad = [], [], []
    for p in range(pairs):
        value_two, query_pair, tanh_val, weights, weights_bf = saved[p]
        columns = slice(p * PAIR, (p + 1) * PAIR)
        grad_pair = attended_grad[:, columns]
        weight_grad = mm_cols(value_two, grad_pair)
        two = mm(weights_bf, grad_pair)
        value_grad.append(jnp.where(even, two[:KEYS], two[KEYS:]))
        product = weights * weight_grad
        parts = []
        for side in range(2):
            rows = slice(side * KEYS, (side + 1) * KEYS)
            parts.append(weight_grad[rows] - jnp.sum(product[rows], axis=0, keepdims=True))
        centred = jnp.concatenate(parts, axis=0)
        score_grad = (weights * centred * (1.0 - tanh_val * tanh_val)).astype(bf16)
        query_grad.append((mm(both_across(keys[:, columns]), score_grad) * scale).astype(bf16))
        two = mm(score_grad, query_pair)
        key_grad.append(jnp.where(even, two[:KEYS], two[KEYS:]))
    query_grad = jnp.concatenate(query_grad, axis=0).T
    grad_cells_ref[...] = mm_cols(query_grad, wq_ref[...]).astype(bf16)
    store_weight(0, mm_rows(cells_ref[...], query_grad))
    encoded_two = jnp.concatenate([encoded_sel, encoded_sel], axis=0).T
    key_two = jnp.concatenate(two_parts(jnp.concatenate(key_grad, axis=1)), axis=0)
    value_two = jnp.concatenate(two_parts(jnp.concatenate(value_grad, axis=1)), axis=0)
    store_weight(1, mm(encoded_two, key_two))
    store_weight(2, mm(encoded_two, value_two))
    grad_gauges = mm_cols(key_two, wk_ref[...]) + mm_cols(value_two, wv_ref[...])
    grad_gauges = (grad_gauges[:KEYS] + grad_gauges[KEYS:]).astype(bf16)
    places = jnp.where(
        lax.broadcasted_iota(jnp.int32, (gauges, KEYS), 0) == places_ref[...], 1.0, 0.0
    ).astype(bf16)
    spread = mm(places, grad_gauges)
    for j in range(MEMBERS):
        store(
            j * chunk + weight_chunk, spread[j * gauge_chunk : (j + 1) * gauge_chunk, :]
        )


def widen_kernel(side_ref, part_ref, *refs):
    out_refs, (wide_ref, sems) = refs[-6:-2], refs[-2:]
    half = part_ref.shape[2]
    columns = pl.ds(pl.multiple_of(side_ref[0] * half, half), half)
    copies = []
    for i, out_ref in enumerate(out_refs):
        wide_ref[i] = part_ref[i].astype(f32)
        copies.append(
            pltpu.make_async_copy(wide_ref.at[i], out_ref.at[:, columns], sems.at[i])
        )
        copies[-1].start()
    for copy in copies:
        copy.wait()


def widen(side, part, grads):
    half = part.shape[1]
    width = 2 * half
    given = () if grads is None else tuple(grads)
    hbm = pl.BlockSpec(memory_space=pltpu.HBM)
    return pl.pallas_call(
        widen_kernel,
        out_shape=(jax.ShapeDtypeStruct((width, width), f32),) * 4,
        in_specs=[
            pl.BlockSpec(memory_space=pltpu.SMEM),
            pl.BlockSpec(memory_space=pltpu.VMEM),
        ]
        + [hbm] * len(given),
        out_specs=(hbm,) * 4,
        scratch_shapes=[
            pltpu.VMEM((4, width, half), f32),
            pltpu.SemaphoreType.DMA((4,)),
        ],
        input_output_aliases={2 + i: i for i in range(len(given))},
        compiler_params=pltpu.CompilerParams(vmem_limit_bytes=32 << 20),
        name="widen_kernel",
    )(side.reshape(1), part.reshape(4, width, half), *given)


def swap(value):
    return lax.ppermute(value, "c", [(0, 1), (1, 0)])


def shifted(value, steps):
    count = lax.axis_size(EVERY)
    return lax.ppermute(value, EVERY, [(i, (i + steps) % count) for i in range(count)])


def copied(value, count):
    rows, width = value.shape
    return jnp.broadcast_to(value[None], (count, rows, width)).reshape(count * rows, width)


def after(value, *others):
    return lax.optimization_barrier((value,) + others)[0]


def per_device(cells, encoded, w_query, w_key, w_value, w_out, pattern, cell_basin, pooled_grad):
    width = cells.shape[1]
    half = width // 2
    core = lax.axis_index("c")
    device = lax.axis_index(EVERY)
    own = pooled_grad.shape[0]
    total = own * lax.axis_size(EVERY)

    rows_own = lax.dynamic_slice_in_dim(encoded, core * half, half, 1)
    copies = copied(rows_own, SIZES["far"])
    line = lax.all_to_all(copies, "far", 0, 0, tiled=True)

    slot = (cell_basin - device * own + own) % total
    counts = jnp.sum(
        (slot[None, :] == jnp.arange(3 * own, dtype=jnp.int32)[:, None]).astype(f32), axis=1
    )
    count_row = jnp.pad(counts.astype(bf16), (0, width - 3 * own))[None, :]
    packet = after(jnp.concatenate([pooled_grad, count_row], axis=0), copies)
    small = packet[own:, :128]
    below, above = shifted(packet, 1), shifted(packet, -1)
    below_two, above_two = shifted(small, 2), shifted(small, -2)
    line = after(line, below, above, below_two, above_two)
    mine = lax.all_to_all(copied(line, MEMBERS), GROUP, 0, 0, tiled=True)
    other = swap(mine)
    own_counts = counts
    down, up = below[own, : 3 * own].astype(f32), above[own, : 3 * own].astype(f32)
    down_two, up_two = below_two[0, : 3 * own].astype(f32), above_two[0, : 3 * own].astype(f32)
    low, mid, top = slice(0, own), slice(own, 2 * own), slice(2 * own, 3 * own)
    all_counts = jnp.concatenate(
        [
            down_two[top] + down[mid] + own_counts[low],
            down[top] + own_counts[mid] + up[low],
            own_counts[top] + up[mid] + up_two[low],
        ]
    )
    roots = jnp.sqrt(all_counts)

    block = pattern[0]
    along_x = block % SIZES["x"]
    near = (block // SIZES["x"]) % SIZES["near"]
    far_z = (block // (SIZES["x"] * SIZES["near"])) % SIZES["far"]
    along_y = block // (SIZES["x"] * SIZES["near"] * SIZES["far"])
    place = (along_y * SIZES["x"] + along_x) * SIZES["near"] + near
    place = place * SIZES["far"] + far_z
    within = jnp.arange(GAUGE_ROWS, dtype=jnp.int32)[None, :]
    places = (place[:, None] * GAUGE_ROWS + within).reshape(1, KEYS)

    gauges = mine.shape[0]
    payload = gauges + 4 * width
    vmem = pl.BlockSpec(memory_space=pltpu.VMEM)
    smem = pl.BlockSpec(memory_space=pltpu.SMEM)
    hbm = pl.BlockSpec(memory_space=pltpu.HBM)
    grad_cells, sums, keep, send = pl.pallas_call(
        group_kernel,
        out_shape=(
            jax.ShapeDtypeStruct(cells.shape, bf16),
            jax.ShapeDtypeStruct((SLOTS, width), f32),
            jax.ShapeDtypeStruct((payload, half), bf16),
            jax.ShapeDtypeStruct((payload, half), bf16),
        ),
        in_specs=[smem] + [vmem] * 12 + [hbm] * 2,
        out_specs=(vmem,) * 4,
        scratch_shapes=[
            pltpu.VMEM(cells.shape, bf16),
            pltpu.VMEM(w_out.shape, bf16),
            pltpu.VMEM((SLOTS, width), f32),
            pltpu.SemaphoreType.DMA((2,)),
        ],
        compiler_params=pltpu.CompilerParams(vmem_limit_bytes=48 << 20),
        name="group_kernel",
    )(
        core.reshape(1), places, slot[None, :], packet, below, above, below_two, above_two,
        mine, other,
        w_key, w_value, w_query,
        pltpu.with_memory_space_constraint(cells, pltpu.HBM),
        pltpu.with_memory_space_constraint(w_out, pltpu.HBM),
    )

    chip = (keep.astype(f32) + swap(send).astype(f32)).astype(bf16)
    chunk = payload // MEMBERS
    gauge_chunk = gauges // MEMBERS
    weight_chunk = chunk - gauge_chunk
    parts = lax.all_to_all(chip, GROUP, 0, 0, tiled=True).reshape(MEMBERS, chunk, half)
    column = jnp.sum(parts.astype(f32), axis=0).astype(bf16)
    count = SIZES["far"]
    turns = [
        lax.ppermute(column, "far", [(i, (i + s) % count) for i in range(count)])
        for s in range(1, count)
    ]
    reduced = (
        (column.astype(f32) + turns[1].astype(f32)) + (turns[0].astype(f32) + turns[2].astype(f32))
    ).astype(bf16)
    own_gauge = lax.dynamic_slice_in_dim(
        reduced, weight_chunk + lax.axis_index("far") * GAUGE_ROWS, GAUGE_ROWS, 0
    )

    copies = copied(reduced[:weight_chunk], MEMBERS)
    weights = lax.all_to_all(copies, GROUP, 0, 0, tiled=True)
    late_sums, late_gauge = lax.optimization_barrier((sums, own_gauge, copies))[:2]
    far_gauge = swap(late_gauge)
    from_above, from_below = shifted(late_sums[low], -1), shifted(late_sums[top], 1)
    weights = after(weights, far_gauge, from_above, from_below)
    pooled = ((sums[mid] + from_above + from_below) / roots[mid][:, None]).astype(bf16)
    grad_gauges = jnp.where(
        core == 0,
        jnp.concatenate([own_gauge, far_gauge], axis=1),
        jnp.concatenate([far_gauge, own_gauge], axis=1),
    )
    far = swap(weights)
    grads = widen(core, weights, None)
    grads = widen(1 - core, far, grads)
    return (pooled, grad_cells, grad_gauges, grads[0], grads[1], grads[2], grads[3])


def solution(mesh):
    grid = Mesh(mesh.devices.reshape(tuple(SIZES[a] for a in EVERY)), EVERY)
    return jax.shard_map(
        per_device,
        mesh=grid,
        in_specs=(
            P(EVERY, None), P(TILES, None), P(), P(), P(), P(),
            P(EVERY, None), P(EVERY), P(EVERY, None),
        ),
        out_specs=(P(EVERY, None), P(EVERY, None), P(TILES, None), P(), P(), P(), P()),
        check_vma=False,
    )
```

```python
import functools
import math

import jax
import jax.numpy as jnp
from jax import lax
from jax.experimental import pallas as pl
from jax.experimental.pallas import tpu as pltpu
from jax.sharding import Mesh
from jax.sharding import PartitionSpec as P

HEADS = 8
HEAD_DIM = 64
PAIR = 2 * HEAD_DIM
KEYS = 128
GAUGE_ROWS = 8
SLOTS = 16
score_cap = 30.0

EVERY = ("y", "far", "near", "x", "c")
TILES = ("y", "far", "near", "x")
GROUP = ("y", "x", "near")
SIZES = {"y": 4, "far": 4, "near": 2, "x": 4, "c": 2}
MEMBERS = SIZES["y"] * SIZES["x"] * SIZES["near"]

bf16 = jnp.bfloat16
f32 = jnp.float32


def mm(left, right):
    return jnp.dot(left, right, preferred_element_type=f32)


def mm_cols(left, right):
    return lax.dot_general(left, right, (((1,), (1,)), ((), ())), preferred_element_type=f32)


def mm_rows(left, right):
    return lax.dot_general(left, right, (((0,), (0,)), ((), ())), preferred_element_type=f32)


def two_parts(value):
    high = value.astype(bf16)
    return high, (value - high.astype(f32)).astype(bf16)


def group_kernel(
    core_ref, rows_ref, places_ref, slot_ref, own_ref, below_ref, above_ref, below_two_ref, above_two_ref,
    mine_ref, other_ref, wk_ref, wv_ref, wq_ref, cells_hbm, wo_hbm,
    grad_cells_ref, sums_ref, roots_ref, keep_ref, send_ref,
    cells_ref, wo_ref, table_ref, sems,
):
    load_cells = pltpu.make_async_copy(cells_hbm, cells_ref, sems.at[0])
    load_wo = pltpu.make_async_copy(wo_hbm, wo_ref, sems.at[1])
    load_cells.start()
    load_wo.start()
    first = core_ref[0] == 0
    width = 2 * mine_ref.shape[1]
    half = width // 2
    gauges = mine_ref.shape[0]
    pairs = width // PAIR
    gauge_chunk = gauges // MEMBERS
    weight_chunk = 4 * width // MEMBERS
    chunk = gauge_chunk + weight_chunk

    def store(row, value):
        low, high = value[:, :half].astype(bf16), value[:, half:].astype(bf16)
        count = value.shape[0]
        keep_ref[row : row + count, :] = jnp.where(first, low, high)
        send_ref[row : row + count, :] = jnp.where(first, high, low)

    def store_weight(which, value):
        per = value.shape[0] // weight_chunk
        for j in range(per):
            store(
                (which * per + j) * chunk,
                value[j * weight_chunk : (j + 1) * weight_chunk, :],
            )

    down = jnp.broadcast_to(rows_ref[...], (KEYS, KEYS)).T
    lanes = lax.broadcasted_iota(jnp.int32, (KEYS, KEYS), 1)
    picks = jnp.concatenate(
        [
            jnp.where(lanes + j * KEYS == down, 1.0, 0.0).astype(bf16)
            for j in range(gauges // KEYS)
        ],
        axis=1,
    )
    sel_mine = mm(picks, mine_ref[...])
    sel_other = mm(picks, other_ref[...])
    encoded_sel = jnp.concatenate(
        [jnp.where(first, sel_mine, sel_other), jnp.where(first, sel_other, sel_mine)], axis=1
    ).astype(bf16)
    keys = mm(encoded_sel, wk_ref[...]).astype(bf16)
    values = mm(encoded_sel, wv_ref[...]).astype(bf16)
    scale = 1.0 / math.sqrt(HEAD_DIM)
    load_cells.wait()
    queries = mm(cells_ref[...], wq_ref[...]).astype(bf16) * jnp.asarray(scale, bf16)
    even = lax.broadcasted_iota(jnp.int32, (KEYS, PAIR), 1) < HEAD_DIM
    upper = lax.broadcasted_iota(jnp.int32, (PAIR, KEYS), 0) < HEAD_DIM
    zero = jnp.zeros((KEYS, PAIR), bf16)

    def both(value):
        return jnp.concatenate([jnp.where(even, value, zero), jnp.where(even, zero, value)], axis=0)

    def both_across(value):
        turned = value.T
        return jnp.concatenate(
            [jnp.where(upper, turned, zero), jnp.where(upper, zero, turned)], axis=1
        )

    saved = []
    attended = []
    for p in range(pairs):
        columns = slice(p * PAIR, (p + 1) * PAIR)
        key_two, value_two = both(keys[:, columns]), both(values[:, columns])
        query_pair = queries[:, columns]
        tanh_val = jnp.tanh(mm_cols(key_two, query_pair) * (1.0 / score_cap))
        exponent = jnp.exp(score_cap * tanh_val)
        parts = []
        for side in range(2):
            part = exponent[side * KEYS : (side + 1) * KEYS]
            parts.append(part * (1.0 / jnp.sum(part, axis=0, keepdims=True)))
        weights = jnp.concatenate(parts, axis=0)
        weights_bf = weights.astype(bf16)
        attended.append(mm(both_across(values[:, columns]), weights_bf).astype(bf16))
        saved.append((value_two, query_pair, tanh_val, weights, weights_bf))
    attended = jnp.concatenate(attended, axis=0)
    load_wo.wait()
    cell_out = mm(attended.T, wo_ref[...]).astype(bf16)
    onehot = jnp.where(
        lax.broadcasted_iota(jnp.int32, (SLOTS, cell_out.shape[0]), 0) == slot_ref[...], 1.0, 0.0
    ).astype(bf16)
    sums_ref[...] = mm(onehot, cell_out)

    basins = own_ref.shape[0] - 1
    row = lax.broadcasted_iota(jnp.int32, (SLOTS, 128), 0)
    lane = lax.broadcasted_iota(jnp.int32, (SLOTS, 128), 1)
    counts = jnp.zeros((SLOTS, 128), f32)
    for offset, source in (
        (2 * basins, below_two_ref[0:1, :]),
        (basins, below_ref[basins : basins + 1, :128]),
        (0, own_ref[basins : basins + 1, :128]),
        (-basins, above_ref[basins : basins + 1, :128]),
        (-2 * basins, above_two_ref[0:1, :]),
    ):
        counts = counts + jnp.where(lane == row + offset, source.astype(f32), 0.0)
    counts = jnp.sum(counts, axis=1, keepdims=True)
    used = lax.broadcasted_iota(jnp.int32, (SLOTS, 1), 0) < 3 * basins
    table_ref[...] = jnp.zeros_like(table_ref)
    for place, source in enumerate((below_ref, own_ref, above_ref)):
        table_ref[place * basins : (place + 1) * basins, :] = source[0:basins, :].astype(f32)
    roots = jnp.sqrt(jnp.where(used, counts, 1.0))
    roots_ref[...] = jnp.broadcast_to(roots, roots_ref.shape)
    table = (table_ref[...] / roots).astype(bf16)
    out_grad = mm_rows(onehot, table).astype(bf16)
    attended_grad = mm_cols(out_grad, wo_ref[...]).astype(bf16)
    store_weight(3, mm(attended, out_grad))

    query_grad, key_grad, value_grad = [], [], []
    for p in range(pairs):
        value_two, query_pair, tanh_val, weights, weights_bf = saved[p]
        columns = slice(p * PAIR, (p + 1) * PAIR)
        grad_pair = attended_grad[:, columns]
        weight_grad = mm_cols(value_two, grad_pair)
        two = mm(weights_bf, grad_pair)
        value_grad.append(jnp.where(even, two[:KEYS], two[KEYS:]))
        product = weights * weight_grad
        parts = []
        for side in range(2):
            rows = slice(side * KEYS, (side + 1) * KEYS)
            parts.append(weight_grad[rows] - jnp.sum(product[rows], axis=0, keepdims=True))
        centred = jnp.concatenate(parts, axis=0)
        score_grad = (weights * centred * (1.0 - tanh_val * tanh_val)).astype(bf16)
        query_grad.append((mm(both_across(keys[:, columns]), score_grad) * scale).astype(bf16))
        two = mm(score_grad, query_pair)
        key_grad.append(jnp.where(even, two[:KEYS], two[KEYS:]))
    query_grad = jnp.concatenate(query_grad, axis=0).T
    grad_cells_ref[...] = mm_cols(query_grad, wq_ref[...]).astype(bf16)
    store_weight(0, mm_rows(cells_ref[...], query_grad))
    encoded_two = jnp.concatenate([encoded_sel, encoded_sel], axis=0).T
    key_two = jnp.concatenate(two_parts(jnp.concatenate(key_grad, axis=1)), axis=0)
    value_two = jnp.concatenate(two_parts(jnp.concatenate(value_grad, axis=1)), axis=0)
    store_weight(1, mm(encoded_two, key_two))
    store_weight(2, mm(encoded_two, value_two))
    grad_gauges = mm_cols(key_two, wk_ref[...]) + mm_cols(value_two, wv_ref[...])
    grad_gauges = (grad_gauges[:KEYS] + grad_gauges[KEYS:]).astype(bf16)
    places = jnp.where(
        lax.broadcasted_iota(jnp.int32, (gauges, KEYS), 0) == places_ref[...], 1.0, 0.0
    ).astype(bf16)
    spread = mm(places, grad_gauges)
    for j in range(MEMBERS):
        store(
            j * chunk + weight_chunk, spread[j * gauge_chunk : (j + 1) * gauge_chunk, :]
        )


def widen_kernel(side_ref, part_ref, *refs):
    out_refs, (wide_ref, sems) = refs[-6:-2], refs[-2:]
    half = part_ref.shape[2]
    columns = pl.ds(pl.multiple_of(side_ref[0] * half, half), half)
    copies = []
    for i, out_ref in enumerate(out_refs):
        wide_ref[i] = part_ref[i].astype(f32)
        copies.append(
            pltpu.make_async_copy(wide_ref.at[i], out_ref.at[:, columns], sems.at[i])
        )
        copies[-1].start()
    for copy in copies:
        copy.wait()


def widen(side, part, grads):
    half = part.shape[1]
    width = 2 * half
    given = () if grads is None else tuple(grads)
    hbm = pl.BlockSpec(memory_space=pltpu.HBM)
    return pl.pallas_call(
        widen_kernel,
        out_shape=(jax.ShapeDtypeStruct((width, width), f32),) * 4,
        in_specs=[
            pl.BlockSpec(memory_space=pltpu.SMEM),
            pl.BlockSpec(memory_space=pltpu.VMEM),
        ]
        + [hbm] * len(given),
        out_specs=(hbm,) * 4,
        scratch_shapes=[
            pltpu.VMEM((4, width, half), f32),
            pltpu.SemaphoreType.DMA((4,)),
        ],
        input_output_aliases={2 + i: i for i in range(len(given))},
        compiler_params=pltpu.CompilerParams(vmem_limit_bytes=32 << 20),
        name="widen_kernel",
    )(side.reshape(1), part.reshape(4, width, half), *given)


def swap(value):
    return lax.ppermute(value, "c", [(0, 1), (1, 0)])


def shifted(value, steps):
    count = lax.axis_size(EVERY)
    return lax.ppermute(value, EVERY, [(i, (i + steps) % count) for i in range(count)])


def copied(value, count):
    rows, width = value.shape
    return jnp.broadcast_to(value[None], (count, rows, width)).reshape(count * rows, width)


def after(value, *others):
    return lax.optimization_barrier((value,) + others)[0]


def per_device(cells, encoded, w_query, w_key, w_value, w_out, pattern, cell_basin, pooled_grad):
    width = cells.shape[1]
    half = width // 2
    core = lax.axis_index("c")
    device = lax.axis_index(EVERY)
    own = pooled_grad.shape[0]
    total = own * lax.axis_size(EVERY)

    rows_own = lax.dynamic_slice_in_dim(encoded, core * half, half, 1)
    copies = copied(rows_own, MEMBERS * SIZES["far"])
    mine = lax.all_to_all(copies, TILES, 0, 0, tiled=True)

    slot = (cell_basin - device * own + own) % total
    counts = jnp.sum(
        (slot[None, :] == jnp.arange(3 * own, dtype=jnp.int32)[:, None]).astype(f32), axis=1
    )
    count_row = jnp.pad(counts.astype(bf16), (0, width - 3 * own))[None, :]
    packet = after(jnp.concatenate([pooled_grad, count_row], axis=0), copies)
    small = packet[own:, :128]
    below, above = shifted(packet, 1), shifted(packet, -1)
    below_two, above_two = shifted(small, 2), shifted(small, -2)
    mine = after(mine, below, above, below_two, above_two)
    other = swap(mine)
    low, mid, top = slice(0, own), slice(own, 2 * own), slice(2 * own, 3 * own)

    block = pattern[0]
    along_x = block % SIZES["x"]
    near = (block // SIZES["x"]) % SIZES["near"]
    far_z = (block // (SIZES["x"] * SIZES["near"])) % SIZES["far"]
    along_y = block // (SIZES["x"] * SIZES["near"] * SIZES["far"])
    place = (along_y * SIZES["x"] + along_x) * SIZES["near"] + near
    place = place * SIZES["far"] + far_z
    within = jnp.arange(GAUGE_ROWS, dtype=jnp.int32)[None, :]
    rows = (block[:, None] * GAUGE_ROWS + within).reshape(1, KEYS)
    places = (place[:, None] * GAUGE_ROWS + within).reshape(1, KEYS)

    gauges = mine.shape[0]
    payload = gauges + 4 * width
    vmem = pl.BlockSpec(memory_space=pltpu.VMEM)
    smem = pl.BlockSpec(memory_space=pltpu.SMEM)
    hbm = pl.BlockSpec(memory_space=pltpu.HBM)
    grad_cells, sums, roots, keep, send = pl.pallas_call(
        group_kernel,
        out_shape=(
            jax.ShapeDtypeStruct(cells.shape, bf16),
            jax.ShapeDtypeStruct((SLOTS, width), f32),
            jax.ShapeDtypeStruct((SLOTS, 128), f32),
            jax.ShapeDtypeStruct((payload, half), bf16),
            jax.ShapeDtypeStruct((payload, half), bf16),
        ),
        in_specs=[smem] + [vmem] * 13 + [hbm] * 2,
        out_specs=(vmem,) * 5,
        scratch_shapes=[
            pltpu.VMEM(cells.shape, bf16),
            pltpu.VMEM(w_out.shape, bf16),
            pltpu.VMEM((SLOTS, width), f32),
            pltpu.SemaphoreType.DMA((2,)),
        ],
        compiler_params=pltpu.CompilerParams(vmem_limit_bytes=24 << 20),
        name="group_kernel",
    )(
        core.reshape(1), rows, places, slot[None, :], packet, below, above, below_two, above_two,
        mine, other,
        w_key, w_value, w_query,
        pltpu.with_memory_space_constraint(cells, pltpu.HBM),
        pltpu.with_memory_space_constraint(w_out, pltpu.HBM),
    )

    chip = (keep.astype(f32) + swap(send).astype(f32)).astype(bf16)
    chunk = payload // MEMBERS
    gauge_chunk = gauges // MEMBERS
    weight_chunk = chunk - gauge_chunk
    parts = lax.all_to_all(chip, GROUP, 0, 0, tiled=True).reshape(MEMBERS, chunk, half)
    column = jnp.sum(parts.astype(f32), axis=0).astype(bf16)
    count = SIZES["far"]
    turns = [
        lax.ppermute(column, "far", [(i, (i + s) % count) for i in range(count)])
        for s in range(1, count)
    ]
    reduced = (
        (column.astype(f32) + turns[1].astype(f32)) + (turns[0].astype(f32) + turns[2].astype(f32))
    ).astype(bf16)
    own_gauge = lax.dynamic_slice_in_dim(
        reduced, weight_chunk + lax.axis_index("far") * GAUGE_ROWS, GAUGE_ROWS, 0
    )

    copies = copied(reduced[:weight_chunk], MEMBERS)
    weights = lax.all_to_all(copies, GROUP, 0, 0, tiled=True)
    late_sums, late_gauge = lax.optimization_barrier((sums, own_gauge, copies))[:2]
    far_gauge = swap(late_gauge)
    from_above, from_below = shifted(late_sums[low], -1), shifted(late_sums[top], 1)
    pooled = ((sums[mid] + from_above + from_below) / roots[mid, :1]).astype(bf16)
    grad_gauges = jnp.where(
        core == 0,
        jnp.concatenate([own_gauge, far_gauge], axis=1),
        jnp.concatenate([far_gauge, own_gauge], axis=1),
    )
    weights = after(weights, pooled, grad_gauges)
    far = swap(weights)
    grads = widen(core, weights, None)
    grads = widen(1 - core, far, grads)
    return (pooled, grad_cells, grad_gauges, grads[0], grads[1], grads[2], grads[3])


def solution(mesh):
    grid = Mesh(mesh.devices.reshape(tuple(SIZES[a] for a in EVERY)), EVERY)
    return jax.shard_map(
        per_device,
        mesh=grid,
        in_specs=(
            P(EVERY, None), P(TILES, None), P(), P(), P(), P(),
            P(EVERY, None), P(EVERY), P(EVERY, None),
        ),
        out_specs=(P(EVERY, None), P(EVERY, None), P(TILES, None), P(), P(), P(), P()),
        check_vma=False,
    )
```

```python
import functools
import math

import jax
import jax.numpy as jnp
from jax import lax
from jax.experimental import pallas as pl
from jax.experimental.pallas import tpu as pltpu
from jax.sharding import Mesh
from jax.sharding import PartitionSpec as P

HEADS = 8
HEAD_DIM = 64
PAIR = 2 * HEAD_DIM
KEYS = 128
GAUGE_ROWS = 8
SLOTS = 16
score_cap = 30.0

EVERY = ("y", "far", "near", "x", "c")
TILES = ("y", "far", "near", "x")
GROUP = ("y", "x", "near")
SIZES = {"y": 4, "far": 4, "near": 2, "x": 4, "c": 2}
MEMBERS = SIZES["y"] * SIZES["x"] * SIZES["near"]

bf16 = jnp.bfloat16
f32 = jnp.float32


def mm(left, right):
    return jnp.dot(left, right, preferred_element_type=f32)


def mm_cols(left, right):
    return lax.dot_general(left, right, (((1,), (1,)), ((), ())), preferred_element_type=f32)


def mm_rows(left, right):
    return lax.dot_general(left, right, (((0,), (0,)), ((), ())), preferred_element_type=f32)


def two_parts(value):
    high = value.astype(bf16)
    return high, (value - high.astype(f32)).astype(bf16)


def group_kernel(
    core_ref, rows_ref, places_ref, slot_ref, own_ref, below_ref, above_ref, below_two_ref, above_two_ref,
    mine_ref, other_ref, wk_ref, wv_ref, wq_ref, cells_hbm, wo_hbm,
    grad_cells_ref, inner_ref, middle_ref, outer_ref, roots_ref, keep_ref, send_ref,
    cells_ref, wo_ref, table_ref, sems,
):
    load_cells = pltpu.make_async_copy(cells_hbm, cells_ref, sems.at[0])
    load_wo = pltpu.make_async_copy(wo_hbm, wo_ref, sems.at[1])
    load_cells.start()
    load_wo.start()
    first = core_ref[0] == 0
    width = 2 * mine_ref.shape[1]
    half = width // 2
    gauges = mine_ref.shape[0]
    pairs = width // PAIR
    gauge_chunk = gauges // MEMBERS
    weight_chunk = 4 * width // MEMBERS
    chunk = gauge_chunk + weight_chunk

    def store(row, value):
        low, high = value[:, :half].astype(bf16), value[:, half:].astype(bf16)
        count = value.shape[0]
        keep_ref[row : row + count, :] = jnp.where(first, low, high)
        send_ref[row : row + count, :] = jnp.where(first, high, low)

    def store_weight(which, value):
        per = value.shape[0] // weight_chunk
        for j in range(per):
            store(
                (which * per + j) * chunk,
                value[j * weight_chunk : (j + 1) * weight_chunk, :],
            )

    down = jnp.broadcast_to(rows_ref[...], (KEYS, KEYS)).T
    lanes = lax.broadcasted_iota(jnp.int32, (KEYS, KEYS), 1)
    picks = jnp.concatenate(
        [
            jnp.where(lanes + j * KEYS == down, 1.0, 0.0).astype(bf16)
            for j in range(gauges // KEYS)
        ],
        axis=1,
    )
    sel_mine = mm(picks, mine_ref[...])
    sel_other = mm(picks, other_ref[...])
    encoded_sel = jnp.concatenate(
        [jnp.where(first, sel_mine, sel_other), jnp.where(first, sel_other, sel_mine)], axis=1
    ).astype(bf16)
    keys = mm(encoded_sel, wk_ref[...]).astype(bf16)
    values = mm(encoded_sel, wv_ref[...]).astype(bf16)
    scale = 1.0 / math.sqrt(HEAD_DIM)
    load_cells.wait()
    queries = mm(cells_ref[...], wq_ref[...]).astype(bf16) * jnp.asarray(scale, bf16)
    even = lax.broadcasted_iota(jnp.int32, (KEYS, PAIR), 1) < HEAD_DIM
    upper = lax.broadcasted_iota(jnp.int32, (PAIR, KEYS), 0) < HEAD_DIM
    zero = jnp.zeros((KEYS, PAIR), bf16)

    def both(value):
        return jnp.concatenate([jnp.where(even, value, zero), jnp.where(even, zero, value)], axis=0)

    def both_across(value):
        turned = value.T
        return jnp.concatenate(
            [jnp.where(upper, turned, zero), jnp.where(upper, zero, turned)], axis=1
        )

    saved = []
    attended = []
    for p in range(pairs):
        columns = slice(p * PAIR, (p + 1) * PAIR)
        key_two, value_two = both(keys[:, columns]), both(values[:, columns])
        query_pair = queries[:, columns]
        tanh_val = jnp.tanh(mm_cols(key_two, query_pair) * (1.0 / score_cap))
        exponent = jnp.exp(score_cap * tanh_val)
        parts = []
        for side in range(2):
            part = exponent[side * KEYS : (side + 1) * KEYS]
            parts.append(part * (1.0 / jnp.sum(part, axis=0, keepdims=True)))
        weights = jnp.concatenate(parts, axis=0)
        weights_bf = weights.astype(bf16)
        attended.append(mm(both_across(values[:, columns]), weights_bf).astype(bf16))
        saved.append((value_two, query_pair, tanh_val, weights, weights_bf))
    attended = jnp.concatenate(attended, axis=0)
    load_wo.wait()
    cell_out = mm(attended.T, wo_ref[...]).astype(bf16)
    onehot = jnp.where(
        lax.broadcasted_iota(jnp.int32, (SLOTS, cell_out.shape[0]), 0) == slot_ref[...], 1.0, 0.0
    ).astype(bf16)
    sums = mm(onehot, cell_out)
    basins = own_ref.shape[0] - 1
    low, top = sums[:basins], sums[2 * basins : 3 * basins]
    middle_ref[...] = sums[basins : 2 * basins]
    inner_ref[...] = jnp.where(first, top, low)
    outer_ref[...] = jnp.where(first, low, top)

    row = lax.broadcasted_iota(jnp.int32, (SLOTS, 128), 0)
    lane = lax.broadcasted_iota(jnp.int32, (SLOTS, 128), 1)
    counts = jnp.zeros((SLOTS, 128), f32)
    for offset, source in (
        (2 * basins, below_two_ref[0:1, :]),
        (basins, below_ref[basins : basins + 1, :128]),
        (0, own_ref[basins : basins + 1, :128]),
        (-basins, above_ref[basins : basins + 1, :128]),
        (-2 * basins, above_two_ref[0:1, :]),
    ):
        counts = counts + jnp.where(lane == row + offset, source.astype(f32), 0.0)
    counts = jnp.sum(counts, axis=1, keepdims=True)
    used = lax.broadcasted_iota(jnp.int32, (SLOTS, 1), 0) < 3 * basins
    table_ref[...] = jnp.zeros_like(table_ref)
    for place, source in enumerate((below_ref, own_ref, above_ref)):
        table_ref[place * basins : (place + 1) * basins, :] = source[0:basins, :].astype(f32)
    roots = jnp.sqrt(jnp.where(used, counts, 1.0))
    roots_ref[...] = jnp.broadcast_to(roots, roots_ref.shape)
    table = (table_ref[...] / roots).astype(bf16)
    out_grad = mm_rows(onehot, table).astype(bf16)
    attended_grad = mm_cols(out_grad, wo_ref[...]).astype(bf16)
    store_weight(3, mm(attended, out_grad))

    query_grad, key_grad, value_grad = [], [], []
    for p in range(pairs):
        value_two, query_pair, tanh_val, weights, weights_bf = saved[p]
        columns = slice(p * PAIR, (p + 1) * PAIR)
        grad_pair = attended_grad[:, columns]
        weight_grad = mm_cols(value_two, grad_pair)
        two = mm(weights_bf, grad_pair)
        value_grad.append(jnp.where(even, two[:KEYS], two[KEYS:]))
        product = weights * weight_grad
        parts = []
        for side in range(2):
            rows = slice(side * KEYS, (side + 1) * KEYS)
            parts.append(weight_grad[rows] - jnp.sum(product[rows], axis=0, keepdims=True))
        centred = jnp.concatenate(parts, axis=0)
        score_grad = (weights * centred * (1.0 - tanh_val * tanh_val)).astype(bf16)
        query_grad.append((mm(both_across(keys[:, columns]), score_grad) * scale).astype(bf16))
        two = mm(score_grad, query_pair)
        key_grad.append(jnp.where(even, two[:KEYS], two[KEYS:]))
    query_grad = jnp.concatenate(query_grad, axis=0).T
    grad_cells_ref[...] = mm_cols(query_grad, wq_ref[...]).astype(bf16)
    store_weight(0, mm_rows(cells_ref[...], query_grad))
    encoded_two = jnp.concatenate([encoded_sel, encoded_sel], axis=0).T
    key_two = jnp.concatenate(two_parts(jnp.concatenate(key_grad, axis=1)), axis=0)
    value_two = jnp.concatenate(two_parts(jnp.concatenate(value_grad, axis=1)), axis=0)
    store_weight(1, mm(encoded_two, key_two))
    store_weight(2, mm(encoded_two, value_two))
    grad_gauges = mm_cols(key_two, wk_ref[...]) + mm_cols(value_two, wv_ref[...])
    grad_gauges = (grad_gauges[:KEYS] + grad_gauges[KEYS:]).astype(bf16)
    places = jnp.where(
        lax.broadcasted_iota(jnp.int32, (gauges, KEYS), 0) == places_ref[...], 1.0, 0.0
    ).astype(bf16)
    spread = mm(places, grad_gauges)
    for j in range(MEMBERS):
        store(
            j * chunk + weight_chunk, spread[j * gauge_chunk : (j + 1) * gauge_chunk, :]
        )


def widen_kernel(side_ref, part_ref, *refs):
    out_refs, (wide_ref, sems) = refs[-6:-2], refs[-2:]
    half = part_ref.shape[2]
    columns = pl.ds(pl.multiple_of(side_ref[0] * half, half), half)
    copies = []
    for i, out_ref in enumerate(out_refs):
        wide_ref[i] = part_ref[i].astype(f32)
        copies.append(
            pltpu.make_async_copy(wide_ref.at[i], out_ref.at[:, columns], sems.at[i])
        )
        copies[-1].start()
    for copy in copies:
        copy.wait()


def widen(side, part, grads):
    half = part.shape[1]
    width = 2 * half
    given = () if grads is None else tuple(grads)
    hbm = pl.BlockSpec(memory_space=pltpu.HBM)
    return pl.pallas_call(
        widen_kernel,
        out_shape=(jax.ShapeDtypeStruct((width, width), f32),) * 4,
        in_specs=[
            pl.BlockSpec(memory_space=pltpu.SMEM),
            pl.BlockSpec(memory_space=pltpu.VMEM),
        ]
        + [hbm] * len(given),
        out_specs=(hbm,) * 4,
        scratch_shapes=[
            pltpu.VMEM((4, width, half), f32),
            pltpu.SemaphoreType.DMA((4,)),
        ],
        input_output_aliases={2 + i: i for i in range(len(given))},
        compiler_params=pltpu.CompilerParams(vmem_limit_bytes=32 << 20),
        name="widen_kernel",
    )(side.reshape(1), part.reshape(4, width, half), *given)


def swap(value):
    return lax.ppermute(value, "c", [(0, 1), (1, 0)])


def shifted(value, steps):
    count = lax.axis_size(EVERY)
    return lax.ppermute(value, EVERY, [(i, (i + steps) % count) for i in range(count)])


def copied(value, count):
    rows, width = value.shape
    return jnp.broadcast_to(value[None], (count, rows, width)).reshape(count * rows, width)


def after(value, *others):
    return lax.optimization_barrier((value,) + others)[0]


def per_device(cells, encoded, w_query, w_key, w_value, w_out, pattern, cell_basin, pooled_grad):
    width = cells.shape[1]
    half = width // 2
    core = lax.axis_index("c")
    device = lax.axis_index(EVERY)
    own = pooled_grad.shape[0]
    total = own * lax.axis_size(EVERY)

    rows_own = lax.dynamic_slice_in_dim(encoded, core * half, half, 1)
    copies = copied(rows_own, MEMBERS * SIZES["far"])
    mine = lax.all_to_all(copies, TILES, 0, 0, tiled=True)

    slot = (cell_basin - device * own + own) % total
    counts = jnp.sum(
        (slot[None, :] == jnp.arange(3 * own, dtype=jnp.int32)[:, None]).astype(f32), axis=1
    )
    count_row = jnp.pad(counts.astype(bf16), (0, width - 3 * own))[None, :]
    packet = after(jnp.concatenate([pooled_grad, count_row], axis=0), copies)
    small = packet[own:, :128]
    below, above = shifted(packet, 1), shifted(packet, -1)
    below_two, above_two = shifted(small, 2), shifted(small, -2)
    mine = after(mine, below, above, below_two, above_two)
    other = swap(mine)
    block = pattern[0]
    along_x = block % SIZES["x"]
    near = (block // SIZES["x"]) % SIZES["near"]
    far_z = (block // (SIZES["x"] * SIZES["near"])) % SIZES["far"]
    along_y = block // (SIZES["x"] * SIZES["near"] * SIZES["far"])
    place = (along_y * SIZES["x"] + along_x) * SIZES["near"] + near
    place = place * SIZES["far"] + far_z
    within = jnp.arange(GAUGE_ROWS, dtype=jnp.int32)[None, :]
    rows = (block[:, None] * GAUGE_ROWS + within).reshape(1, KEYS)
    places = (place[:, None] * GAUGE_ROWS + within).reshape(1, KEYS)

    gauges = mine.shape[0]
    payload = gauges + 4 * width
    vmem = pl.BlockSpec(memory_space=pltpu.VMEM)
    smem = pl.BlockSpec(memory_space=pltpu.SMEM)
    hbm = pl.BlockSpec(memory_space=pltpu.HBM)
    grad_cells, inner, middle, outer, roots, keep, send = pl.pallas_call(
        group_kernel,
        out_shape=(
            jax.ShapeDtypeStruct(cells.shape, bf16),
            jax.ShapeDtypeStruct((own, width), f32),
            jax.ShapeDtypeStruct((own, width), f32),
            jax.ShapeDtypeStruct((own, width), f32),
            jax.ShapeDtypeStruct((SLOTS, 128), f32),
            jax.ShapeDtypeStruct((payload, half), bf16),
            jax.ShapeDtypeStruct((payload, half), bf16),
        ),
        in_specs=[smem] + [vmem] * 13 + [hbm] * 2,
        out_specs=(vmem,) * 7,
        scratch_shapes=[
            pltpu.VMEM(cells.shape, bf16),
            pltpu.VMEM(w_out.shape, bf16),
            pltpu.VMEM((SLOTS, width), f32),
            pltpu.SemaphoreType.DMA((2,)),
        ],
        compiler_params=pltpu.CompilerParams(vmem_limit_bytes=24 << 20),
        name="group_kernel",
    )(
        core.reshape(1), rows, places, slot[None, :], packet, below, above, below_two, above_two,
        mine, other,
        w_key, w_value, w_query,
        pltpu.with_memory_space_constraint(cells, pltpu.HBM),
        pltpu.with_memory_space_constraint(w_out, pltpu.HBM),
    )

    chip = (keep.astype(f32) + swap(send).astype(f32)).astype(bf16)
    chunk = payload // MEMBERS
    gauge_chunk = gauges // MEMBERS
    weight_chunk = chunk - gauge_chunk
    parts = lax.all_to_all(chip, GROUP, 0, 0, tiled=True).reshape(MEMBERS, chunk, half)
    column = jnp.sum(parts.astype(f32), axis=0).astype(bf16)
    count = SIZES["far"]
    turns = [
        lax.ppermute(column, "far", [(i, (i + s) % count) for i in range(count)])
        for s in range(1, count)
    ]
    inner, outer = lax.optimization_barrier((inner, outer, column))[:2]
    from_inner = swap(inner)
    total_devices = lax.axis_size(EVERY)
    from_outer = lax.ppermute(
        outer,
        EVERY,
        [(i, (i + (1 if i % 2 else -1)) % total_devices) for i in range(total_devices)],
    )
    reduced = (
        (column.astype(f32) + turns[1].astype(f32)) + (turns[0].astype(f32) + turns[2].astype(f32))
    ).astype(bf16)
    reduced = after(reduced, from_inner, from_outer)
    weights = lax.all_to_all(copied(reduced[:weight_chunk], MEMBERS), GROUP, 0, 0, tiled=True)

    pooled = ((middle + from_inner + from_outer) / roots[own : 2 * own, :1]).astype(bf16)
    own_gauge = lax.dynamic_slice_in_dim(
        reduced, weight_chunk + lax.axis_index("far") * GAUGE_ROWS, GAUGE_ROWS, 0
    )
    far_gauge = swap(after(own_gauge, weights))
    grad_gauges = jnp.where(
        core == 0,
        jnp.concatenate([own_gauge, far_gauge], axis=1),
        jnp.concatenate([far_gauge, own_gauge], axis=1),
    )
    far = swap(weights)
    grads = widen(core, weights, None)
    grads = widen(1 - core, far, grads)
    return (pooled, grad_cells, grad_gauges, grads[0], grads[1], grads[2], grads[3])


def solution(mesh):
    grid = Mesh(mesh.devices.reshape(tuple(SIZES[a] for a in EVERY)), EVERY)
    return jax.shard_map(
        per_device,
        mesh=grid,
        in_specs=(
            P(EVERY, None), P(TILES, None), P(), P(), P(), P(),
            P(EVERY, None), P(EVERY), P(EVERY, None),
        ),
        out_specs=(P(EVERY, None), P(EVERY, None), P(TILES, None), P(), P(), P(), P()),
        check_vma=False,
    )
```

```python
import functools
import math

import jax
import jax.numpy as jnp
from jax import lax
from jax.experimental import pallas as pl
from jax.experimental.pallas import tpu as pltpu
from jax.sharding import Mesh
from jax.sharding import PartitionSpec as P

HEADS = 8
HEAD_DIM = 64
PAIR = 2 * HEAD_DIM
KEYS = 128
GAUGE_ROWS = 8
SLOTS = 16
score_cap = 30.0

EVERY = ("y", "far", "near", "x", "c")
TILES = ("y", "far", "near", "x")
GROUP = ("y", "x", "near")
SIZES = {"y": 4, "far": 4, "near": 2, "x": 4, "c": 2}
MEMBERS = SIZES["y"] * SIZES["x"] * SIZES["near"]

bf16 = jnp.bfloat16
f32 = jnp.float32


def mm(left, right):
    return jnp.dot(left, right, preferred_element_type=f32)


def mm_cols(left, right):
    return lax.dot_general(left, right, (((1,), (1,)), ((), ())), preferred_element_type=f32)


def mm_rows(left, right):
    return lax.dot_general(left, right, (((0,), (0,)), ((), ())), preferred_element_type=f32)


def two_parts(value):
    high = value.astype(bf16)
    return high, (value - high.astype(f32)).astype(bf16)


def group_kernel(
    core_ref, rows_ref, places_ref, slot_ref, own_ref, below_ref, above_ref, below_two_ref, above_two_ref,
    mine_ref, other_ref, wk_ref, wv_ref, wq_ref, cells_hbm, wo_hbm,
    grad_cells_ref, inner_ref, middle_ref, outer_ref, roots_ref, keep_ref, send_ref,
    cells_ref, wo_ref, table_ref, sems,
):
    load_cells = pltpu.make_async_copy(cells_hbm, cells_ref, sems.at[0])
    load_wo = pltpu.make_async_copy(wo_hbm, wo_ref, sems.at[1])
    load_cells.start()
    load_wo.start()
    first = core_ref[0] == 0
    width = 2 * mine_ref.shape[1]
    half = width // 2
    gauges = mine_ref.shape[0]
    pairs = width // PAIR
    gauge_chunk = gauges // MEMBERS
    weight_chunk = 4 * width // MEMBERS
    chunk = gauge_chunk + weight_chunk

    def store(row, value):
        low, high = value[:, :half].astype(bf16), value[:, half:].astype(bf16)
        count = value.shape[0]
        keep_ref[row : row + count, :] = jnp.where(first, low, high)
        send_ref[row : row + count, :] = jnp.where(first, high, low)

    def store_weight(which, value):
        per = value.shape[0] // weight_chunk
        for j in range(per):
            store(
                (which * per + j) * chunk,
                value[j * weight_chunk : (j + 1) * weight_chunk, :],
            )

    down = jnp.broadcast_to(rows_ref[...], (KEYS, KEYS)).T
    lanes = lax.broadcasted_iota(jnp.int32, (KEYS, KEYS), 1)
    picks = jnp.concatenate(
        [
            jnp.where(lanes + j * KEYS == down, 1.0, 0.0).astype(bf16)
            for j in range(gauges // KEYS)
        ],
        axis=1,
    )
    sel_mine = mm(picks, mine_ref[...])
    sel_other = mm(picks, other_ref[...])
    encoded_sel = jnp.concatenate(
        [jnp.where(first, sel_mine, sel_other), jnp.where(first, sel_other, sel_mine)], axis=1
    ).astype(bf16)
    keys = mm(encoded_sel, wk_ref[...]).astype(bf16)
    values = mm(encoded_sel, wv_ref[...]).astype(bf16)
    scale = 1.0 / math.sqrt(HEAD_DIM)
    load_cells.wait()
    queries = mm(cells_ref[...], wq_ref[...]).astype(bf16) * jnp.asarray(scale, bf16)
    even = lax.broadcasted_iota(jnp.int32, (KEYS, PAIR), 1) < HEAD_DIM
    upper = lax.broadcasted_iota(jnp.int32, (PAIR, KEYS), 0) < HEAD_DIM
    zero = jnp.zeros((KEYS, PAIR), bf16)

    def both(value):
        return jnp.concatenate([jnp.where(even, value, zero), jnp.where(even, zero, value)], axis=0)

    def both_across(value):
        turned = value.T
        return jnp.concatenate(
            [jnp.where(upper, turned, zero), jnp.where(upper, zero, turned)], axis=1
        )

    saved = []
    attended = []
    for p in range(pairs):
        columns = slice(p * PAIR, (p + 1) * PAIR)
        key_two, value_two = both(keys[:, columns]), both(values[:, columns])
        query_pair = queries[:, columns]
        tanh_val = jnp.tanh(mm_cols(key_two, query_pair) * (1.0 / score_cap))
        exponent = jnp.exp(score_cap * tanh_val)
        parts = []
        for side in range(2):
            part = exponent[side * KEYS : (side + 1) * KEYS]
            parts.append(part * (1.0 / jnp.sum(part, axis=0, keepdims=True)))
        weights = jnp.concatenate(parts, axis=0)
        weights_bf = weights.astype(bf16)
        attended.append(mm(both_across(values[:, columns]), weights_bf).astype(bf16))
        saved.append((value_two, query_pair, tanh_val, weights, weights_bf))
    attended = jnp.concatenate(attended, axis=0)
    load_wo.wait()
    cell_out = mm(attended.T, wo_ref[...]).astype(bf16)
    onehot = jnp.where(
        lax.broadcasted_iota(jnp.int32, (SLOTS, cell_out.shape[0]), 0) == slot_ref[...], 1.0, 0.0
    ).astype(bf16)
    sums = mm(onehot, cell_out)
    basins = own_ref.shape[0] - 1
    low, top = sums[:basins], sums[2 * basins : 3 * basins]
    middle_ref[...] = sums[basins : 2 * basins]
    inner_ref[...] = jnp.where(first, top, low)
    outer_ref[...] = jnp.where(first, low, top)

    row = lax.broadcasted_iota(jnp.int32, (SLOTS, 128), 0)
    lane = lax.broadcasted_iota(jnp.int32, (SLOTS, 128), 1)
    counts = jnp.zeros((SLOTS, 128), f32)
    for offset, source in (
        (2 * basins, below_two_ref[0:1, :]),
        (basins, below_ref[basins : basins + 1, :128]),
        (0, own_ref[basins : basins + 1, :128]),
        (-basins, above_ref[basins : basins + 1, :128]),
        (-2 * basins, above_two_ref[0:1, :]),
    ):
        counts = counts + jnp.where(lane == row + offset, source.astype(f32), 0.0)
    counts = jnp.sum(counts, axis=1, keepdims=True)
    used = lax.broadcasted_iota(jnp.int32, (SLOTS, 1), 0) < 3 * basins
    table_ref[...] = jnp.zeros_like(table_ref)
    for place, source in enumerate((below_ref, own_ref, above_ref)):
        table_ref[place * basins : (place + 1) * basins, :] = source[0:basins, :].astype(f32)
    roots = jnp.sqrt(jnp.where(used, counts, 1.0))
    roots_ref[...] = jnp.broadcast_to(roots, roots_ref.shape)
    table = (table_ref[...] / roots).astype(bf16)
    out_grad = mm_rows(onehot, table).astype(bf16)
    attended_grad = mm_cols(out_grad, wo_ref[...]).astype(bf16)
    store_weight(3, mm(attended, out_grad))

    query_grad, key_grad, value_grad = [], [], []
    for p in range(pairs):
        value_two, query_pair, tanh_val, weights, weights_bf = saved[p]
        columns = slice(p * PAIR, (p + 1) * PAIR)
        grad_pair = attended_grad[:, columns]
        weight_grad = mm_cols(value_two, grad_pair)
        two = mm(weights_bf, grad_pair)
        value_grad.append(jnp.where(even, two[:KEYS], two[KEYS:]))
        product = weights * weight_grad
        parts = []
        for side in range(2):
            rows = slice(side * KEYS, (side + 1) * KEYS)
            parts.append(weight_grad[rows] - jnp.sum(product[rows], axis=0, keepdims=True))
        centred = jnp.concatenate(parts, axis=0)
        score_grad = (weights * centred * (1.0 - tanh_val * tanh_val)).astype(bf16)
        query_grad.append((mm(both_across(keys[:, columns]), score_grad) * scale).astype(bf16))
        two = mm(score_grad, query_pair)
        key_grad.append(jnp.where(even, two[:KEYS], two[KEYS:]))
    query_grad = jnp.concatenate(query_grad, axis=0).T
    grad_cells_ref[...] = mm_cols(query_grad, wq_ref[...]).astype(bf16)
    store_weight(0, mm_rows(cells_ref[...], query_grad))
    encoded_two = jnp.concatenate([encoded_sel, encoded_sel], axis=0).T
    key_two = jnp.concatenate(two_parts(jnp.concatenate(key_grad, axis=1)), axis=0)
    value_two = jnp.concatenate(two_parts(jnp.concatenate(value_grad, axis=1)), axis=0)
    store_weight(1, mm(encoded_two, key_two))
    store_weight(2, mm(encoded_two, value_two))
    grad_gauges = mm_cols(key_two, wk_ref[...]) + mm_cols(value_two, wv_ref[...])
    grad_gauges = (grad_gauges[:KEYS] + grad_gauges[KEYS:]).astype(bf16)
    places = jnp.where(
        lax.broadcasted_iota(jnp.int32, (gauges, KEYS), 0) == places_ref[...], 1.0, 0.0
    ).astype(bf16)
    spread = mm(places, grad_gauges)
    for j in range(MEMBERS):
        store(
            j * chunk + weight_chunk, spread[j * gauge_chunk : (j + 1) * gauge_chunk, :]
        )


def widen_kernel(side_ref, part_ref, *refs):
    out_refs, (wide_ref, sems) = refs[-6:-2], refs[-2:]
    half = part_ref.shape[2]
    columns = pl.ds(pl.multiple_of(side_ref[0] * half, half), half)
    copies = []
    for i, out_ref in enumerate(out_refs):
        wide_ref[i] = part_ref[i].astype(f32)
        copies.append(
            pltpu.make_async_copy(wide_ref.at[i], out_ref.at[:, columns], sems.at[i])
        )
        copies[-1].start()
    for copy in copies:
        copy.wait()


def widen(side, part, grads):
    half = part.shape[1]
    width = 2 * half
    given = () if grads is None else tuple(grads)
    hbm = pl.BlockSpec(memory_space=pltpu.HBM)
    return pl.pallas_call(
        widen_kernel,
        out_shape=(jax.ShapeDtypeStruct((width, width), f32),) * 4,
        in_specs=[
            pl.BlockSpec(memory_space=pltpu.SMEM),
            pl.BlockSpec(memory_space=pltpu.VMEM),
        ]
        + [hbm] * len(given),
        out_specs=(hbm,) * 4,
        scratch_shapes=[
            pltpu.VMEM((4, width, half), f32),
            pltpu.SemaphoreType.DMA((4,)),
        ],
        input_output_aliases={2 + i: i for i in range(len(given))},
        compiler_params=pltpu.CompilerParams(vmem_limit_bytes=32 << 20),
        name="widen_kernel",
    )(side.reshape(1), part.reshape(4, width, half), *given)


def swap(value):
    return lax.ppermute(value, "c", [(0, 1), (1, 0)])


def shifted(value, steps):
    count = lax.axis_size(EVERY)
    return lax.ppermute(value, EVERY, [(i, (i + steps) % count) for i in range(count)])


def copied(value, count):
    rows, width = value.shape
    return jnp.broadcast_to(value[None], (count, rows, width)).reshape(count * rows, width)


def after(value, *others):
    return lax.optimization_barrier((value,) + others)[0]


def per_device(cells, encoded, w_query, w_key, w_value, w_out, pattern, cell_basin, pooled_grad):
    width = cells.shape[1]
    half = width // 2
    core = lax.axis_index("c")
    device = lax.axis_index(EVERY)
    own = pooled_grad.shape[0]
    total = own * lax.axis_size(EVERY)

    rows_own = lax.dynamic_slice_in_dim(encoded, core * half, half, 1)
    copies = copied(rows_own, MEMBERS * SIZES["far"])
    mine = lax.all_to_all(copies, TILES, 0, 0, tiled=True)

    slot = (cell_basin - device * own + own) % total
    counts = jnp.sum(
        (slot[None, :] == jnp.arange(3 * own, dtype=jnp.int32)[:, None]).astype(f32), axis=1
    )
    count_row = jnp.pad(counts.astype(bf16), (0, width - 3 * own))[None, :]
    packet = after(jnp.concatenate([pooled_grad, count_row], axis=0), copies)
    small = packet[own:, :128]
    below, above = shifted(packet, 1), shifted(packet, -1)
    below_two, above_two = shifted(small, 2), shifted(small, -2)
    mine = after(mine, below, above, below_two, above_two)
    other = swap(mine)
    block = pattern[0]
    along_x = block % SIZES["x"]
    near = (block // SIZES["x"]) % SIZES["near"]
    far_z = (block // (SIZES["x"] * SIZES["near"])) % SIZES["far"]
    along_y = block // (SIZES["x"] * SIZES["near"] * SIZES["far"])
    place = (along_y * SIZES["x"] + along_x) * SIZES["near"] + near
    place = place * SIZES["far"] + far_z
    within = jnp.arange(GAUGE_ROWS, dtype=jnp.int32)[None, :]
    rows = (block[:, None] * GAUGE_ROWS + within).reshape(1, KEYS)
    places = (place[:, None] * GAUGE_ROWS + within).reshape(1, KEYS)

    gauges = mine.shape[0]
    payload = gauges + 4 * width
    vmem = pl.BlockSpec(memory_space=pltpu.VMEM)
    smem = pl.BlockSpec(memory_space=pltpu.SMEM)
    hbm = pl.BlockSpec(memory_space=pltpu.HBM)
    grad_cells, inner, middle, outer, roots, keep, send = pl.pallas_call(
        group_kernel,
        out_shape=(
            jax.ShapeDtypeStruct(cells.shape, bf16),
            jax.ShapeDtypeStruct((own, width), f32),
            jax.ShapeDtypeStruct((own, width), f32),
            jax.ShapeDtypeStruct((own, width), f32),
            jax.ShapeDtypeStruct((SLOTS, 128), f32),
            jax.ShapeDtypeStruct((payload, half), bf16),
            jax.ShapeDtypeStruct((payload, half), bf16),
        ),
        in_specs=[smem] + [vmem] * 13 + [hbm] * 2,
        out_specs=(vmem,) * 7,
        scratch_shapes=[
            pltpu.VMEM(cells.shape, bf16),
            pltpu.VMEM(w_out.shape, bf16),
            pltpu.VMEM((SLOTS, width), f32),
            pltpu.SemaphoreType.DMA((2,)),
        ],
        compiler_params=pltpu.CompilerParams(vmem_limit_bytes=24 << 20),
        name="group_kernel",
    )(
        core.reshape(1), rows, places, slot[None, :], packet, below, above, below_two, above_two,
        mine, other,
        w_key, w_value, w_query,
        pltpu.with_memory_space_constraint(cells, pltpu.HBM),
        pltpu.with_memory_space_constraint(w_out, pltpu.HBM),
    )

    from_core = swap(send)
    from_inner = swap(inner)
    total_devices = lax.axis_size(EVERY)
    from_outer = lax.ppermute(
        outer,
        EVERY,
        [(i, (i + (1 if i % 2 else -1)) % total_devices) for i in range(total_devices)],
    )
    from_core = after(from_core, from_inner, from_outer)
    chip = (keep.astype(f32) + from_core.astype(f32)).astype(bf16)
    chunk = payload // MEMBERS
    gauge_chunk = gauges // MEMBERS
    weight_chunk = chunk - gauge_chunk
    parts = lax.all_to_all(chip, GROUP, 0, 0, tiled=True).reshape(MEMBERS, chunk, half)
    column = jnp.sum(parts.astype(f32), axis=0).astype(bf16)
    count = SIZES["far"]
    turns = [
        lax.ppermute(column, "far", [(i, (i + s) % count) for i in range(count)])
        for s in range(1, count)
    ]
    reduced = (
        (column.astype(f32) + turns[1].astype(f32)) + (turns[0].astype(f32) + turns[2].astype(f32))
    ).astype(bf16)
    pooled = ((middle + from_inner + from_outer) / roots[own : 2 * own, :1]).astype(bf16)
    reduced = after(reduced, pooled)
    weights = lax.all_to_all(copied(reduced[:weight_chunk], MEMBERS), GROUP, 0, 0, tiled=True)

    own_gauge = lax.dynamic_slice_in_dim(
        reduced, weight_chunk + lax.axis_index("far") * GAUGE_ROWS, GAUGE_ROWS, 0
    )
    far_gauge = swap(after(own_gauge, weights))
    grad_gauges = jnp.where(
        core == 0,
        jnp.concatenate([own_gauge, far_gauge], axis=1),
        jnp.concatenate([far_gauge, own_gauge], axis=1),
    )
    far = swap(weights)
    grads = widen(core, weights, None)
    grads = widen(1 - core, far, grads)
    return (pooled, grad_cells, grad_gauges, grads[0], grads[1], grads[2], grads[3])


def solution(mesh):
    grid = Mesh(mesh.devices.reshape(tuple(SIZES[a] for a in EVERY)), EVERY)
    return jax.shard_map(
        per_device,
        mesh=grid,
        in_specs=(
            P(EVERY, None), P(TILES, None), P(), P(), P(), P(),
            P(EVERY, None), P(EVERY), P(EVERY, None),
        ),
        out_specs=(P(EVERY, None), P(EVERY, None), P(TILES, None), P(), P(), P(), P()),
        check_vma=False,
    )
```

```python
import functools
import math

import jax
import jax.numpy as jnp
from jax import lax
from jax.experimental import pallas as pl
from jax.experimental.pallas import tpu as pltpu
from jax.sharding import Mesh
from jax.sharding import PartitionSpec as P

HEADS = 8
HEAD_DIM = 64
PAIR = 2 * HEAD_DIM
KEYS = 128
GAUGE_ROWS = 8
SLOTS = 16
score_cap = 30.0

EVERY = ("y", "far", "near", "x", "c")
TILES = ("y", "far", "near", "x")
GROUP = ("y", "x", "near")
SIZES = {"y": 4, "far": 4, "near": 2, "x": 4, "c": 2}
MEMBERS = SIZES["y"] * SIZES["x"] * SIZES["near"]

bf16 = jnp.bfloat16
f32 = jnp.float32


def mm(left, right):
    return jnp.dot(left, right, preferred_element_type=f32)


def mm_cols(left, right):
    return lax.dot_general(left, right, (((1,), (1,)), ((), ())), preferred_element_type=f32)


def mm_rows(left, right):
    return lax.dot_general(left, right, (((0,), (0,)), ((), ())), preferred_element_type=f32)


def two_parts(value):
    high = value.astype(bf16)
    return high, (value - high.astype(f32)).astype(bf16)


def group_kernel(
    core_ref, rows_ref, places_ref, slot_ref, own_ref, below_ref, above_ref, below_two_ref, above_two_ref,
    mine_ref, other_ref, wk_ref, wv_ref, wq_ref, cells_hbm, wo_hbm,
    grad_cells_ref, inner_ref, middle_ref, outer_ref, roots_ref, keep_ref, send_ref,
    cells_ref, wo_ref, table_ref, sems,
):
    load_cells = pltpu.make_async_copy(cells_hbm, cells_ref, sems.at[0])
    load_wo = pltpu.make_async_copy(wo_hbm, wo_ref, sems.at[1])
    load_cells.start()
    load_wo.start()
    first = core_ref[0] == 0
    width = 2 * mine_ref.shape[1]
    half = width // 2
    gauges = mine_ref.shape[0]
    pairs = width // PAIR
    gauge_chunk = gauges // MEMBERS
    weight_chunk = 4 * width // MEMBERS
    chunk = gauge_chunk + weight_chunk

    def store(row, value):
        low, high = value[:, :half].astype(bf16), value[:, half:].astype(bf16)
        count = value.shape[0]
        keep_ref[row : row + count, :] = jnp.where(first, low, high)
        send_ref[row : row + count, :] = jnp.where(first, high, low)

    def store_weight(which, value):
        per = value.shape[0] // weight_chunk
        for j in range(per):
            store(
                (which * per + j) * chunk,
                value[j * weight_chunk : (j + 1) * weight_chunk, :],
            )

    down = jnp.broadcast_to(rows_ref[...], (KEYS, KEYS)).T
    lanes = lax.broadcasted_iota(jnp.int32, (KEYS, KEYS), 1)
    picks = jnp.concatenate(
        [
            jnp.where(lanes + j * KEYS == down, 1.0, 0.0).astype(bf16)
            for j in range(gauges // KEYS)
        ],
        axis=1,
    )
    sel_mine = mm(picks, mine_ref[...])
    sel_other = mm(picks, other_ref[...])
    encoded_sel = jnp.concatenate(
        [jnp.where(first, sel_mine, sel_other), jnp.where(first, sel_other, sel_mine)], axis=1
    ).astype(bf16)
    keys = mm(encoded_sel, wk_ref[...]).astype(bf16)
    values = mm(encoded_sel, wv_ref[...]).astype(bf16)
    scale = 1.0 / math.sqrt(HEAD_DIM)
    load_cells.wait()
    queries = mm(cells_ref[...], wq_ref[...]).astype(bf16) * jnp.asarray(scale, bf16)
    even = lax.broadcasted_iota(jnp.int32, (KEYS, PAIR), 1) < HEAD_DIM
    upper = lax.broadcasted_iota(jnp.int32, (PAIR, KEYS), 0) < HEAD_DIM
    zero = jnp.zeros((KEYS, PAIR), bf16)

    def both(value):
        return jnp.concatenate([jnp.where(even, value, zero), jnp.where(even, zero, value)], axis=0)

    def both_across(value):
        turned = value.T
        return jnp.concatenate(
            [jnp.where(upper, turned, zero), jnp.where(upper, zero, turned)], axis=1
        )

    saved = []
    attended = []
    for p in range(pairs):
        columns = slice(p * PAIR, (p + 1) * PAIR)
        key_two, value_two = both(keys[:, columns]), both(values[:, columns])
        query_pair = queries[:, columns]
        tanh_val = jnp.tanh(mm_cols(key_two, query_pair) * (1.0 / score_cap))
        exponent = jnp.exp(score_cap * tanh_val)
        parts = []
        for side in range(2):
            part = exponent[side * KEYS : (side + 1) * KEYS]
            parts.append(part * (1.0 / jnp.sum(part, axis=0, keepdims=True)))
        weights = jnp.concatenate(parts, axis=0)
        weights_bf = weights.astype(bf16)
        attended.append(mm(both_across(values[:, columns]), weights_bf).astype(bf16))
        saved.append((value_two, query_pair, tanh_val, weights, weights_bf))
    attended = jnp.concatenate(attended, axis=0)
    load_wo.wait()
    cell_out = mm(attended.T, wo_ref[...]).astype(bf16)
    onehot = jnp.where(
        lax.broadcasted_iota(jnp.int32, (SLOTS, cell_out.shape[0]), 0) == slot_ref[...], 1.0, 0.0
    ).astype(bf16)
    sums = mm(onehot, cell_out)
    basins = own_ref.shape[0] - 1
    low, top = sums[:basins], sums[2 * basins : 3 * basins]
    middle_ref[...] = sums[basins : 2 * basins]
    inner_ref[...] = jnp.where(first, top, low)
    outer_ref[...] = jnp.where(first, low, top)

    row = lax.broadcasted_iota(jnp.int32, (SLOTS, 128), 0)
    lane = lax.broadcasted_iota(jnp.int32, (SLOTS, 128), 1)
    counts = jnp.zeros((SLOTS, 128), f32)
    for offset, source in (
        (2 * basins, below_two_ref[0:1, :]),
        (basins, below_ref[basins : basins + 1, :128]),
        (0, own_ref[basins : basins + 1, :128]),
        (-basins, above_ref[basins : basins + 1, :128]),
        (-2 * basins, above_two_ref[0:1, :]),
    ):
        counts = counts + jnp.where(lane == row + offset, source.astype(f32), 0.0)
    counts = jnp.sum(counts, axis=1, keepdims=True)
    used = lax.broadcasted_iota(jnp.int32, (SLOTS, 1), 0) < 3 * basins
    table_ref[...] = jnp.zeros_like(table_ref)
    for place, source in enumerate((below_ref, own_ref, above_ref)):
        table_ref[place * basins : (place + 1) * basins, :] = source[0:basins, :].astype(f32)
    roots = jnp.sqrt(jnp.where(used, counts, 1.0))
    roots_ref[...] = jnp.broadcast_to(roots[basins : 2 * basins], roots_ref.shape)
    table = (table_ref[...] / roots).astype(bf16)
    out_grad = mm_rows(onehot, table).astype(bf16)
    attended_grad = mm_cols(out_grad, wo_ref[...]).astype(bf16)
    store_weight(3, mm(attended, out_grad))

    query_grad, key_grad, value_grad = [], [], []
    for p in range(pairs):
        value_two, query_pair, tanh_val, weights, weights_bf = saved[p]
        columns = slice(p * PAIR, (p + 1) * PAIR)
        grad_pair = attended_grad[:, columns]
        weight_grad = mm_cols(value_two, grad_pair)
        two = mm(weights_bf, grad_pair)
        value_grad.append(jnp.where(even, two[:KEYS], two[KEYS:]))
        product = weights * weight_grad
        parts = []
        for side in range(2):
            rows = slice(side * KEYS, (side + 1) * KEYS)
            parts.append(weight_grad[rows] - jnp.sum(product[rows], axis=0, keepdims=True))
        centred = jnp.concatenate(parts, axis=0)
        score_grad = (weights * centred * (1.0 - tanh_val * tanh_val)).astype(bf16)
        query_grad.append((mm(both_across(keys[:, columns]), score_grad) * scale).astype(bf16))
        two = mm(score_grad, query_pair)
        key_grad.append(jnp.where(even, two[:KEYS], two[KEYS:]))
    query_grad = jnp.concatenate(query_grad, axis=0).T
    grad_cells_ref[...] = mm_cols(query_grad, wq_ref[...]).astype(bf16)
    store_weight(0, mm_rows(cells_ref[...], query_grad))
    encoded_two = jnp.concatenate([encoded_sel, encoded_sel], axis=0).T
    key_two = jnp.concatenate(two_parts(jnp.concatenate(key_grad, axis=1)), axis=0)
    value_two = jnp.concatenate(two_parts(jnp.concatenate(value_grad, axis=1)), axis=0)
    store_weight(1, mm(encoded_two, key_two))
    store_weight(2, mm(encoded_two, value_two))
    grad_gauges = mm_cols(key_two, wk_ref[...]) + mm_cols(value_two, wv_ref[...])
    grad_gauges = (grad_gauges[:KEYS] + grad_gauges[KEYS:]).astype(bf16)
    places = jnp.where(
        lax.broadcasted_iota(jnp.int32, (gauges, KEYS), 0) == places_ref[...], 1.0, 0.0
    ).astype(bf16)
    spread = mm(places, grad_gauges)
    for j in range(MEMBERS):
        store(
            j * chunk + weight_chunk, spread[j * gauge_chunk : (j + 1) * gauge_chunk, :]
        )


def write_half(side_ref, part_ref, out_refs, wide_ref, sems):
    half = part_ref.shape[2]
    columns = pl.ds(pl.multiple_of(side_ref[0] * half, half), half)
    copies = []
    for i, out_ref in enumerate(out_refs):
        wide_ref[i] = part_ref[i].astype(f32)
        copies.append(
            pltpu.make_async_copy(wide_ref.at[i], out_ref.at[:, columns], sems.at[i])
        )
        copies[-1].start()
    return copies


def widen_kernel(side_ref, part_ref, *refs):
    for copy in write_half(side_ref, part_ref, refs[:4], *refs[4:]):
        copy.wait()


def finish_kernel(side_ref, part_ref, own_ref, far_ref, *refs):
    gauge_ref = refs[8]
    copies = write_half(side_ref, part_ref, refs[4:8], *refs[9:])
    half = own_ref.shape[1]
    first = side_ref[0] == 1
    own, far = own_ref[...], far_ref[...]
    gauge_ref[:, :half] = jnp.where(first, own, far)
    gauge_ref[:, half:] = jnp.where(first, far, own)
    for copy in copies:
        copy.wait()


def widen(side, part, *rest):
    half = part.shape[1]
    width = 2 * half
    smem = pl.BlockSpec(memory_space=pltpu.SMEM)
    vmem = pl.BlockSpec(memory_space=pltpu.VMEM)
    hbm = pl.BlockSpec(memory_space=pltpu.HBM)
    shapes = (jax.ShapeDtypeStruct((width, width), f32),) * 4
    if rest:
        shapes += (jax.ShapeDtypeStruct((rest[0].shape[0], width), bf16),)
    return pl.pallas_call(
        finish_kernel if rest else widen_kernel,
        out_shape=shapes,
        in_specs=[smem, vmem] + ([vmem] * 2 + [hbm] * 4 if rest else []),
        out_specs=(hbm,) * 4 + ((vmem,) if rest else ()),
        scratch_shapes=[
            pltpu.VMEM((4, width, half), f32),
            pltpu.SemaphoreType.DMA((4,)),
        ],
        input_output_aliases={4 + i: i for i in range(4)} if rest else {},
        compiler_params=pltpu.CompilerParams(vmem_limit_bytes=32 << 20),
        name="finish_kernel" if rest else "widen_kernel",
    )(side.reshape(1), part.reshape(4, width, half), *rest)


def swap(value):
    return lax.ppermute(value, "c", [(0, 1), (1, 0)])


def shifted(value, steps):
    count = lax.axis_size(EVERY)
    return lax.ppermute(value, EVERY, [(i, (i + steps) % count) for i in range(count)])


def copied(value, count):
    rows, width = value.shape
    return jnp.broadcast_to(value[None], (count, rows, width)).reshape(count * rows, width)


def after(value, *others):
    return lax.optimization_barrier((value,) + others)[0]


def per_device(cells, encoded, w_query, w_key, w_value, w_out, pattern, cell_basin, pooled_grad):
    width = cells.shape[1]
    half = width // 2
    core = lax.axis_index("c")
    device = lax.axis_index(EVERY)
    own = pooled_grad.shape[0]
    total = own * lax.axis_size(EVERY)

    rows_own = lax.dynamic_slice_in_dim(encoded, core * half, half, 1)
    copies = copied(rows_own, MEMBERS * SIZES["far"])
    mine = lax.all_to_all(copies, TILES, 0, 0, tiled=True)

    slot = (cell_basin - device * own + own) % total
    counts = jnp.sum(
        (slot[None, :] == jnp.arange(3 * own, dtype=jnp.int32)[:, None]).astype(f32), axis=1
    )
    count_row = jnp.pad(counts.astype(bf16), (0, width - 3 * own))[None, :]
    packet = after(jnp.concatenate([pooled_grad, count_row], axis=0), copies)
    small = packet[own:, :128]
    below, above = shifted(packet, 1), shifted(packet, -1)
    below_two, above_two = shifted(small, 2), shifted(small, -2)
    mine = after(mine, below, above, below_two, above_two)
    other = swap(mine)
    block = pattern[0]
    along_x = block % SIZES["x"]
    near = (block // SIZES["x"]) % SIZES["near"]
    far_z = (block // (SIZES["x"] * SIZES["near"])) % SIZES["far"]
    along_y = block // (SIZES["x"] * SIZES["near"] * SIZES["far"])
    place = (along_y * SIZES["x"] + along_x) * SIZES["near"] + near
    place = place * SIZES["far"] + far_z
    within = jnp.arange(GAUGE_ROWS, dtype=jnp.int32)[None, :]
    rows = (block[:, None] * GAUGE_ROWS + within).reshape(1, KEYS)
    places = (place[:, None] * GAUGE_ROWS + within).reshape(1, KEYS)

    gauges = mine.shape[0]
    payload = gauges + 4 * width
    vmem = pl.BlockSpec(memory_space=pltpu.VMEM)
    smem = pl.BlockSpec(memory_space=pltpu.SMEM)
    hbm = pl.BlockSpec(memory_space=pltpu.HBM)
    grad_cells, inner, middle, outer, roots, keep, send = pl.pallas_call(
        group_kernel,
        out_shape=(
            jax.ShapeDtypeStruct(cells.shape, bf16),
            jax.ShapeDtypeStruct((own, width), f32),
            jax.ShapeDtypeStruct((own, width), f32),
            jax.ShapeDtypeStruct((own, width), f32),
            jax.ShapeDtypeStruct((own, width), f32),
            jax.ShapeDtypeStruct((payload, half), bf16),
            jax.ShapeDtypeStruct((payload, half), bf16),
        ),
        in_specs=[smem] + [vmem] * 13 + [hbm] * 2,
        out_specs=(vmem,) * 7,
        scratch_shapes=[
            pltpu.VMEM(cells.shape, bf16),
            pltpu.VMEM(w_out.shape, bf16),
            pltpu.VMEM((SLOTS, width), f32),
            pltpu.SemaphoreType.DMA((2,)),
        ],
        compiler_params=pltpu.CompilerParams(vmem_limit_bytes=24 << 20),
        name="group_kernel",
    )(
        core.reshape(1), rows, places, slot[None, :], packet, below, above, below_two, above_two,
        mine, other,
        w_key, w_value, w_query,
        pltpu.with_memory_space_constraint(cells, pltpu.HBM),
        pltpu.with_memory_space_constraint(w_out, pltpu.HBM),
    )

    from_core = swap(send)
    from_inner = swap(inner)
    total_devices = lax.axis_size(EVERY)
    from_outer = lax.ppermute(
        outer,
        EVERY,
        [(i, (i + (1 if i % 2 else -1)) % total_devices) for i in range(total_devices)],
    )
    from_core = after(from_core, from_inner, from_outer)
    chip = (keep.astype(f32) + from_core.astype(f32)).astype(bf16)
    chunk = payload // MEMBERS
    gauge_chunk = gauges // MEMBERS
    weight_chunk = chunk - gauge_chunk
    parts = lax.all_to_all(chip, GROUP, 0, 0, tiled=True).reshape(MEMBERS, chunk, half)
    column = jnp.sum(parts.astype(f32), axis=0).astype(bf16)
    count = SIZES["far"]
    turns = [
        lax.ppermute(column, "far", [(i, (i + s) % count) for i in range(count)])
        for s in range(1, count)
    ]
    reduced = (
        (column.astype(f32) + turns[1].astype(f32)) + (turns[0].astype(f32) + turns[2].astype(f32))
    ).astype(bf16)
    middle = after(middle, column)
    pooled = ((middle + from_inner + from_outer) / roots).astype(bf16)
    reduced = after(reduced, pooled)
    weights = lax.all_to_all(copied(reduced[:weight_chunk], MEMBERS), GROUP, 0, 0, tiled=True)

    own_gauge = lax.dynamic_slice_in_dim(
        reduced, weight_chunk + lax.axis_index("far") * GAUGE_ROWS, GAUGE_ROWS, 0
    )
    far_gauge = swap(after(own_gauge, weights))
    far = swap(weights)
    grads = widen(core, weights)
    *grads, grad_gauges = widen(1 - core, far, own_gauge, far_gauge, *grads)
    return (pooled, grad_cells, grad_gauges, grads[0], grads[1], grads[2], grads[3])


def solution(mesh):
    grid = Mesh(mesh.devices.reshape(tuple(SIZES[a] for a in EVERY)), EVERY)
    return jax.shard_map(
        per_device,
        mesh=grid,
        in_specs=(
            P(EVERY, None), P(TILES, None), P(), P(), P(), P(),
            P(EVERY, None), P(EVERY), P(EVERY, None),
        ),
        out_specs=(P(EVERY, None), P(EVERY, None), P(TILES, None), P(), P(), P(), P()),
        check_vma=False,
    )
```

```python
import functools
import math

import jax
import jax.numpy as jnp
from jax import lax
from jax.experimental import pallas as pl
from jax.experimental.pallas import tpu as pltpu
from jax.sharding import Mesh
from jax.sharding import PartitionSpec as P

HEADS = 8
HEAD_DIM = 64
PAIR = 2 * HEAD_DIM
KEYS = 128
GAUGE_ROWS = 8
SLOTS = 16
score_cap = 30.0

EVERY = ("y", "far", "near", "x", "c")
TILES = ("y", "far", "near", "x")
GROUP = ("y", "x", "near")
SIZES = {"y": 4, "far": 4, "near": 2, "x": 4, "c": 2}
MEMBERS = SIZES["y"] * SIZES["x"] * SIZES["near"]

bf16 = jnp.bfloat16
f32 = jnp.float32


def mm(left, right):
    return jnp.dot(left, right, preferred_element_type=f32)


def mm_cols(left, right):
    return lax.dot_general(left, right, (((1,), (1,)), ((), ())), preferred_element_type=f32)


def mm_rows(left, right):
    return lax.dot_general(left, right, (((0,), (0,)), ((), ())), preferred_element_type=f32)


def two_parts(value):
    high = value.astype(bf16)
    return high, (value - high.astype(f32)).astype(bf16)


def group_kernel(
    core_ref, rows_ref, places_ref, slot_ref, own_ref, below_ref, above_ref, below_two_ref, above_two_ref,
    mine_ref, other_ref, wk_ref, wv_ref, wq_ref, cells_hbm, wo_hbm,
    grad_cells_ref, inner_ref, middle_ref, outer_ref, roots_ref, keep_ref, send_ref,
    cells_ref, wo_ref, table_ref, sems,
):
    load_cells = pltpu.make_async_copy(cells_hbm, cells_ref, sems.at[0])
    load_wo = pltpu.make_async_copy(wo_hbm, wo_ref, sems.at[1])
    load_cells.start()
    load_wo.start()
    first = core_ref[0] == 0
    width = 2 * mine_ref.shape[1]
    half = width // 2
    gauges = mine_ref.shape[0]
    pairs = width // PAIR
    gauge_chunk = gauges // MEMBERS
    weight_chunk = 4 * width // MEMBERS
    chunk = gauge_chunk + weight_chunk

    def store(row, value):
        low, high = value[:, :half].astype(bf16), value[:, half:].astype(bf16)
        count = value.shape[0]
        keep_ref[row : row + count, :] = jnp.where(first, low, high)
        send_ref[row : row + count, :] = jnp.where(first, high, low)

    def store_weight(which, value):
        per = value.shape[0] // weight_chunk
        for j in range(per):
            store(
                (which * per + j) * chunk,
                value[j * weight_chunk : (j + 1) * weight_chunk, :],
            )

    down = jnp.broadcast_to(rows_ref[...], (KEYS, KEYS)).T
    lanes = lax.broadcasted_iota(jnp.int32, (KEYS, KEYS), 1)
    picks = jnp.concatenate(
        [
            jnp.where(lanes + j * KEYS == down, 1.0, 0.0).astype(bf16)
            for j in range(gauges // KEYS)
        ],
        axis=1,
    )
    sel_mine = mm(picks, mine_ref[...])
    sel_other = mm(picks, other_ref[...])
    encoded_sel = jnp.concatenate(
        [jnp.where(first, sel_mine, sel_other), jnp.where(first, sel_other, sel_mine)], axis=1
    ).astype(bf16)
    keys = mm(encoded_sel, wk_ref[...]).astype(bf16)
    values = mm(encoded_sel, wv_ref[...]).astype(bf16)
    scale = 1.0 / math.sqrt(HEAD_DIM)
    load_cells.wait()
    queries = mm(cells_ref[...], wq_ref[...]).astype(bf16) * jnp.asarray(scale, bf16)
    even = lax.broadcasted_iota(jnp.int32, (KEYS, PAIR), 1) < HEAD_DIM
    upper = lax.broadcasted_iota(jnp.int32, (PAIR, KEYS), 0) < HEAD_DIM
    zero = jnp.zeros((KEYS, PAIR), bf16)

    def both(value):
        return jnp.concatenate([jnp.where(even, value, zero), jnp.where(even, zero, value)], axis=0)

    def both_across(value):
        turned = value.T
        return jnp.concatenate(
            [jnp.where(upper, turned, zero), jnp.where(upper, zero, turned)], axis=1
        )

    saved = []
    attended = []
    for p in range(pairs):
        columns = slice(p * PAIR, (p + 1) * PAIR)
        key_two, value_two = both(keys[:, columns]), both(values[:, columns])
        query_pair = queries[:, columns]
        tanh_val = jnp.tanh(mm_cols(key_two, query_pair) * (1.0 / score_cap))
        exponent = jnp.exp(score_cap * tanh_val)
        parts = []
        for side in range(2):
            part = exponent[side * KEYS : (side + 1) * KEYS]
            parts.append(part * (1.0 / jnp.sum(part, axis=0, keepdims=True)))
        weights = jnp.concatenate(parts, axis=0)
        weights_bf = weights.astype(bf16)
        attended.append(mm(both_across(values[:, columns]), weights_bf).astype(bf16))
        saved.append((value_two, query_pair, tanh_val, weights, weights_bf))
    attended = jnp.concatenate(attended, axis=0)
    load_wo.wait()
    cell_out = mm(attended.T, wo_ref[...]).astype(bf16)
    onehot = jnp.where(
        lax.broadcasted_iota(jnp.int32, (SLOTS, cell_out.shape[0]), 0) == slot_ref[...], 1.0, 0.0
    ).astype(bf16)
    sums = mm(onehot, cell_out)
    basins = own_ref.shape[0] - 1
    low, top = sums[:basins], sums[2 * basins : 3 * basins]
    middle_ref[...] = sums[basins : 2 * basins]
    inner_ref[...] = jnp.where(first, top, low)
    outer_ref[...] = jnp.where(first, low, top)

    row = lax.broadcasted_iota(jnp.int32, (SLOTS, 128), 0)
    lane = lax.broadcasted_iota(jnp.int32, (SLOTS, 128), 1)
    counts = jnp.zeros((SLOTS, 128), f32)
    for offset, source in (
        (2 * basins, below_two_ref[0:1, :]),
        (basins, below_ref[basins : basins + 1, :128]),
        (0, own_ref[basins : basins + 1, :128]),
        (-basins, above_ref[basins : basins + 1, :128]),
        (-2 * basins, above_two_ref[0:1, :]),
    ):
        counts = counts + jnp.where(lane == row + offset, source.astype(f32), 0.0)
    counts = jnp.sum(counts, axis=1, keepdims=True)
    used = lax.broadcasted_iota(jnp.int32, (SLOTS, 1), 0) < 3 * basins
    table_ref[...] = jnp.zeros_like(table_ref)
    for place, source in enumerate((below_ref, own_ref, above_ref)):
        table_ref[place * basins : (place + 1) * basins, :] = source[0:basins, :].astype(f32)
    roots = jnp.sqrt(jnp.where(used, counts, 1.0))
    roots_ref[...] = jnp.broadcast_to(roots, roots_ref.shape)
    table = (table_ref[...] / roots).astype(bf16)
    out_grad = mm_rows(onehot, table).astype(bf16)
    attended_grad = mm_cols(out_grad, wo_ref[...]).astype(bf16)
    store_weight(3, mm(attended, out_grad))

    query_grad, key_grad, value_grad = [], [], []
    for p in range(pairs):
        value_two, query_pair, tanh_val, weights, weights_bf = saved[p]
        columns = slice(p * PAIR, (p + 1) * PAIR)
        grad_pair = attended_grad[:, columns]
        weight_grad = mm_cols(value_two, grad_pair)
        two = mm(weights_bf, grad_pair)
        value_grad.append(jnp.where(even, two[:KEYS], two[KEYS:]))
        product = weights * weight_grad
        parts = []
        for side in range(2):
            rows = slice(side * KEYS, (side + 1) * KEYS)
            parts.append(weight_grad[rows] - jnp.sum(product[rows], axis=0, keepdims=True))
        centred = jnp.concatenate(parts, axis=0)
        score_grad = (weights * centred * (1.0 - tanh_val * tanh_val)).astype(bf16)
        query_grad.append((mm(both_across(keys[:, columns]), score_grad) * scale).astype(bf16))
        two = mm(score_grad, query_pair)
        key_grad.append(jnp.where(even, two[:KEYS], two[KEYS:]))
    query_grad = jnp.concatenate(query_grad, axis=0).T
    grad_cells_ref[...] = mm_cols(query_grad, wq_ref[...]).astype(bf16)
    store_weight(0, mm_rows(cells_ref[...], query_grad))
    encoded_two = jnp.concatenate([encoded_sel, encoded_sel], axis=0).T
    key_two = jnp.concatenate(two_parts(jnp.concatenate(key_grad, axis=1)), axis=0)
    value_two = jnp.concatenate(two_parts(jnp.concatenate(value_grad, axis=1)), axis=0)
    store_weight(1, mm(encoded_two, key_two))
    store_weight(2, mm(encoded_two, value_two))
    grad_gauges = mm_cols(key_two, wk_ref[...]) + mm_cols(value_two, wv_ref[...])
    grad_gauges = (grad_gauges[:KEYS] + grad_gauges[KEYS:]).astype(bf16)
    places = jnp.where(
        lax.broadcasted_iota(jnp.int32, (gauges, KEYS), 0) == places_ref[...], 1.0, 0.0
    ).astype(bf16)
    spread = mm(places, grad_gauges)
    for j in range(MEMBERS):
        store(
            j * chunk + weight_chunk, spread[j * gauge_chunk : (j + 1) * gauge_chunk, :]
        )


def widen_kernel(side_ref, part_ref, *refs):
    out_refs, (wide_ref, sems) = refs[-6:-2], refs[-2:]
    half = part_ref.shape[2]
    columns = pl.ds(pl.multiple_of(side_ref[0] * half, half), half)
    copies = []
    for i, out_ref in enumerate(out_refs):
        wide_ref[i] = part_ref[i].astype(f32)
        copies.append(
            pltpu.make_async_copy(wide_ref.at[i], out_ref.at[:, columns], sems.at[i])
        )
        copies[-1].start()
    for copy in copies:
        copy.wait()


def widen(side, part, grads):
    half = part.shape[1]
    width = 2 * half
    given = () if grads is None else tuple(grads)
    hbm = pl.BlockSpec(memory_space=pltpu.HBM)
    return pl.pallas_call(
        widen_kernel,
        out_shape=(jax.ShapeDtypeStruct((width, width), f32),) * 4,
        in_specs=[
            pl.BlockSpec(memory_space=pltpu.SMEM),
            pl.BlockSpec(memory_space=pltpu.VMEM),
        ]
        + [hbm] * len(given),
        out_specs=(hbm,) * 4,
        scratch_shapes=[
            pltpu.VMEM((4, width, half), f32),
            pltpu.SemaphoreType.DMA((4,)),
        ],
        input_output_aliases={2 + i: i for i in range(len(given))},
        compiler_params=pltpu.CompilerParams(vmem_limit_bytes=32 << 20),
        name="widen_kernel",
    )(side.reshape(1), part.reshape(4, width, half), *given)


def swap(value):
    return lax.ppermute(value, "c", [(0, 1), (1, 0)])


def shifted(value, steps):
    count = lax.axis_size(EVERY)
    return lax.ppermute(value, EVERY, [(i, (i + steps) % count) for i in range(count)])


def copied(value, count):
    rows, width = value.shape
    return jnp.broadcast_to(value[None], (count, rows, width)).reshape(count * rows, width)


def after(value, *others):
    return lax.optimization_barrier((value,) + others)[0]


def per_device(cells, encoded, w_query, w_key, w_value, w_out, pattern, cell_basin, pooled_grad):
    width = cells.shape[1]
    half = width // 2
    core = lax.axis_index("c")
    device = lax.axis_index(EVERY)
    own = pooled_grad.shape[0]
    total = own * lax.axis_size(EVERY)

    rows_own = lax.dynamic_slice_in_dim(encoded, core * half, half, 1)
    copies = copied(rows_own, MEMBERS * SIZES["far"])
    mine = lax.all_to_all(copies, TILES, 0, 0, tiled=True)

    slot = (cell_basin - device * own + own) % total
    counts = jnp.sum(
        (slot[None, :] == jnp.arange(3 * own, dtype=jnp.int32)[:, None]).astype(f32), axis=1
    )
    count_row = jnp.pad(counts.astype(bf16), (0, width - 3 * own))[None, :]
    packet = after(jnp.concatenate([pooled_grad, count_row], axis=0), copies)
    small = packet[own:, :128]
    below, above = shifted(packet, 1), shifted(packet, -1)
    below_two, above_two = shifted(small, 2), shifted(small, -2)
    mine = after(mine, below, above, below_two, above_two)
    other = swap(mine)
    block = pattern[0]
    along_x = block % SIZES["x"]
    near = (block // SIZES["x"]) % SIZES["near"]
    far_z = (block // (SIZES["x"] * SIZES["near"])) % SIZES["far"]
    along_y = block // (SIZES["x"] * SIZES["near"] * SIZES["far"])
    place = (along_y * SIZES["x"] + along_x) * SIZES["near"] + near
    place = place * SIZES["far"] + far_z
    within = jnp.arange(GAUGE_ROWS, dtype=jnp.int32)[None, :]
    rows = (block[:, None] * GAUGE_ROWS + within).reshape(1, KEYS)
    places = (place[:, None] * GAUGE_ROWS + within).reshape(1, KEYS)

    gauges = mine.shape[0]
    payload = gauges + 4 * width
    vmem = pl.BlockSpec(memory_space=pltpu.VMEM)
    smem = pl.BlockSpec(memory_space=pltpu.SMEM)
    hbm = pl.BlockSpec(memory_space=pltpu.HBM)
    grad_cells, inner, middle, outer, roots, keep, send = pl.pallas_call(
        group_kernel,
        out_shape=(
            jax.ShapeDtypeStruct(cells.shape, bf16),
            jax.ShapeDtypeStruct((own, width), f32),
            jax.ShapeDtypeStruct((own, width), f32),
            jax.ShapeDtypeStruct((own, width), f32),
            jax.ShapeDtypeStruct((SLOTS, 128), f32),
            jax.ShapeDtypeStruct((payload, half), bf16),
            jax.ShapeDtypeStruct((payload, half), bf16),
        ),
        in_specs=[smem] + [vmem] * 13 + [hbm] * 2,
        out_specs=(vmem,) * 7,
        scratch_shapes=[
            pltpu.VMEM(cells.shape, bf16),
            pltpu.VMEM(w_out.shape, bf16),
            pltpu.VMEM((SLOTS, width), f32),
            pltpu.SemaphoreType.DMA((2,)),
        ],
        compiler_params=pltpu.CompilerParams(vmem_limit_bytes=24 << 20),
        name="group_kernel",
    )(
        core.reshape(1), rows, places, slot[None, :], packet, below, above, below_two, above_two,
        mine, other,
        w_key, w_value, w_query,
        pltpu.with_memory_space_constraint(cells, pltpu.HBM),
        pltpu.with_memory_space_constraint(w_out, pltpu.HBM),
    )

    chip = (keep.astype(f32) + swap(send).astype(f32)).astype(bf16)
    chunk = payload // MEMBERS
    gauge_chunk = gauges // MEMBERS
    weight_chunk = chunk - gauge_chunk
    parts = lax.all_to_all(chip, GROUP, 0, 0, tiled=True).reshape(MEMBERS, chunk, half)
    column = jnp.sum(parts.astype(f32), axis=0).astype(bf16)
    count = SIZES["far"]
    turns = [
        lax.ppermute(column, "far", [(i, (i + s) % count) for i in range(count)])
        for s in range(1, count)
    ]
    reduced = (
        (column.astype(f32) + turns[1].astype(f32)) + (turns[0].astype(f32) + turns[2].astype(f32))
    ).astype(bf16)
    copies = copied(reduced[:weight_chunk], MEMBERS)
    weights = lax.all_to_all(copies, GROUP, 0, 0, tiled=True)
    own_gauge = lax.dynamic_slice_in_dim(
        reduced, weight_chunk + lax.axis_index("far") * GAUGE_ROWS, GAUGE_ROWS, 0
    )
    inner, outer, late_gauge = lax.optimization_barrier((inner, outer, own_gauge, copies))[:3]
    from_inner = swap(inner)
    total_devices = lax.axis_size(EVERY)
    from_outer = lax.ppermute(
        outer,
        EVERY,
        [(i, (i + (1 if i % 2 else -1)) % total_devices) for i in range(total_devices)],
    )
    far_gauge = swap(late_gauge)
    pooled = ((middle + from_inner + from_outer) / roots[own : 2 * own, :1]).astype(bf16)
    grad_gauges = jnp.where(
        core == 0,
        jnp.concatenate([own_gauge, far_gauge], axis=1),
        jnp.concatenate([far_gauge, own_gauge], axis=1),
    )
    weights = after(weights, pooled, grad_gauges)
    far = swap(weights)
    grads = widen(core, weights, None)
    grads = widen(1 - core, far, grads)
    return (pooled, grad_cells, grad_gauges, grads[0], grads[1], grads[2], grads[3])


def solution(mesh):
    grid = Mesh(mesh.devices.reshape(tuple(SIZES[a] for a in EVERY)), EVERY)
    return jax.shard_map(
        per_device,
        mesh=grid,
        in_specs=(
            P(EVERY, None), P(TILES, None), P(), P(), P(), P(),
            P(EVERY, None), P(EVERY), P(EVERY, None),
        ),
        out_specs=(P(EVERY, None), P(EVERY, None), P(TILES, None), P(), P(), P(), P()),
        check_vma=False,
    )
```

```python
import functools
import math

import jax
import jax.numpy as jnp
from jax import lax
from jax.experimental import pallas as pl
from jax.experimental.pallas import tpu as pltpu
from jax.sharding import Mesh
from jax.sharding import PartitionSpec as P

HEADS = 8
HEAD_DIM = 64
PAIR = 2 * HEAD_DIM
KEYS = 128
GAUGE_ROWS = 8
SLOTS = 16
score_cap = 30.0

EVERY = ("y", "far", "near", "x", "c")
TILES = ("y", "far", "near", "x")
GROUP = ("y", "x", "near")
SIZES = {"y": 4, "far": 4, "near": 2, "x": 4, "c": 2}
MEMBERS = SIZES["y"] * SIZES["x"] * SIZES["near"]

bf16 = jnp.bfloat16
f32 = jnp.float32


def mm(left, right):
    return jnp.dot(left, right, preferred_element_type=f32)


def mm_cols(left, right):
    return lax.dot_general(left, right, (((1,), (1,)), ((), ())), preferred_element_type=f32)


def mm_rows(left, right):
    return lax.dot_general(left, right, (((0,), (0,)), ((), ())), preferred_element_type=f32)


def two_parts(value):
    high = value.astype(bf16)
    return high, (value - high.astype(f32)).astype(bf16)


def group_kernel(
    core_ref, rows_ref, places_ref, slot_ref, own_ref, mate_ref, side_ref, before_ref, behind_ref,
    mine_ref, other_ref, wk_ref, wv_ref, wq_ref, cells_hbm, wo_hbm,
    grad_cells_ref, inner_ref, middle_ref, outer_ref, roots_ref, keep_ref, send_ref,
    cells_ref, wo_ref, table_ref, sems,
):
    load_cells = pltpu.make_async_copy(cells_hbm, cells_ref, sems.at[0])
    load_wo = pltpu.make_async_copy(wo_hbm, wo_ref, sems.at[1])
    load_cells.start()
    load_wo.start()
    first = core_ref[0] == 0
    width = 2 * mine_ref.shape[1]
    half = width // 2
    gauges = mine_ref.shape[0]
    pairs = width // PAIR
    gauge_chunk = gauges // MEMBERS
    weight_chunk = 4 * width // MEMBERS
    chunk = gauge_chunk + weight_chunk

    def store(row, value):
        low, high = value[:, :half].astype(bf16), value[:, half:].astype(bf16)
        count = value.shape[0]
        keep_ref[row : row + count, :] = jnp.where(first, low, high)
        send_ref[row : row + count, :] = jnp.where(first, high, low)

    def store_weight(which, value):
        per = value.shape[0] // weight_chunk
        for j in range(per):
            store(
                (which * per + j) * chunk,
                value[j * weight_chunk : (j + 1) * weight_chunk, :],
            )

    down = jnp.broadcast_to(rows_ref[...], (KEYS, KEYS)).T
    lanes = lax.broadcasted_iota(jnp.int32, (KEYS, KEYS), 1)
    picks = jnp.concatenate(
        [
            jnp.where(lanes + j * KEYS == down, 1.0, 0.0).astype(bf16)
            for j in range(gauges // KEYS)
        ],
        axis=1,
    )
    sel_mine = mm(picks, mine_ref[...])
    sel_other = mm(picks, other_ref[...])
    encoded_sel = jnp.concatenate(
        [jnp.where(first, sel_mine, sel_other), jnp.where(first, sel_other, sel_mine)], axis=1
    ).astype(bf16)
    keys = mm(encoded_sel, wk_ref[...]).astype(bf16)
    values = mm(encoded_sel, wv_ref[...]).astype(bf16)
    scale = 1.0 / math.sqrt(HEAD_DIM)
    load_cells.wait()
    queries = mm(cells_ref[...], wq_ref[...]).astype(bf16) * jnp.asarray(scale, bf16)
    even = lax.broadcasted_iota(jnp.int32, (KEYS, PAIR), 1) < HEAD_DIM
    upper = lax.broadcasted_iota(jnp.int32, (PAIR, KEYS), 0) < HEAD_DIM
    zero = jnp.zeros((KEYS, PAIR), bf16)

    def both(value):
        return jnp.concatenate([jnp.where(even, value, zero), jnp.where(even, zero, value)], axis=0)

    def both_across(value):
        turned = value.T
        return jnp.concatenate(
            [jnp.where(upper, turned, zero), jnp.where(upper, zero, turned)], axis=1
        )

    saved = []
    attended = []
    for p in range(pairs):
        columns = slice(p * PAIR, (p + 1) * PAIR)
        key_two, value_two = both(keys[:, columns]), both(values[:, columns])
        query_pair = queries[:, columns]
        tanh_val = jnp.tanh(mm_cols(key_two, query_pair) * (1.0 / score_cap))
        exponent = jnp.exp(score_cap * tanh_val)
        parts = []
        for side in range(2):
            part = exponent[side * KEYS : (side + 1) * KEYS]
            parts.append(part * (1.0 / jnp.sum(part, axis=0, keepdims=True)))
        weights = jnp.concatenate(parts, axis=0)
        weights_bf = weights.astype(bf16)
        attended.append(mm(both_across(values[:, columns]), weights_bf).astype(bf16))
        saved.append((value_two, query_pair, tanh_val, weights, weights_bf))
    attended = jnp.concatenate(attended, axis=0)
    load_wo.wait()
    cell_out = mm(attended.T, wo_ref[...]).astype(bf16)
    onehot = jnp.where(
        lax.broadcasted_iota(jnp.int32, (SLOTS, cell_out.shape[0]), 0) == slot_ref[...], 1.0, 0.0
    ).astype(bf16)
    sums = mm(onehot, cell_out)
    basins = own_ref.shape[0] - 1
    low, top = sums[:basins], sums[2 * basins : 3 * basins]
    middle_ref[...] = sums[basins : 2 * basins]
    inner_ref[...] = jnp.where(first, top, low)
    outer_ref[...] = jnp.where(first, low, top)

    below = jnp.where(first, side_ref[...], mate_ref[...])
    above = jnp.where(first, mate_ref[...], side_ref[...])
    row = lax.broadcasted_iota(jnp.int32, (SLOTS, 128), 0)
    lane = lax.broadcasted_iota(jnp.int32, (SLOTS, 128), 1)
    counts = jnp.zeros((SLOTS, 128), f32)
    for offset, source in (
        (2 * basins, before_ref[basins : basins + 1, :128]),
        (basins, below[basins : basins + 1, :128]),
        (0, own_ref[basins : basins + 1, :128]),
        (-basins, above[basins : basins + 1, :128]),
        (-2 * basins, behind_ref[basins : basins + 1, :128]),
    ):
        counts = counts + jnp.where(lane == row + offset, source.astype(f32), 0.0)
    counts = jnp.sum(counts, axis=1, keepdims=True)
    used = lax.broadcasted_iota(jnp.int32, (SLOTS, 1), 0) < 3 * basins
    table_ref[...] = jnp.zeros_like(table_ref)
    for place, source in enumerate((below, own_ref[...], above)):
        table_ref[place * basins : (place + 1) * basins, :] = source[:basins, :].astype(f32)
    roots = jnp.sqrt(jnp.where(used, counts, 1.0))
    roots_ref[...] = jnp.broadcast_to(roots, roots_ref.shape)
    table = (table_ref[...] / roots).astype(bf16)
    out_grad = mm_rows(onehot, table).astype(bf16)
    attended_grad = mm_cols(out_grad, wo_ref[...]).astype(bf16)
    store_weight(3, mm(attended, out_grad))

    query_grad, key_grad, value_grad = [], [], []
    for p in range(pairs):
        value_two, query_pair, tanh_val, weights, weights_bf = saved[p]
        columns = slice(p * PAIR, (p + 1) * PAIR)
        grad_pair = attended_grad[:, columns]
        weight_grad = mm_cols(value_two, grad_pair)
        two = mm(weights_bf, grad_pair)
        value_grad.append(jnp.where(even, two[:KEYS], two[KEYS:]))
        product = weights * weight_grad
        parts = []
        for side in range(2):
            rows = slice(side * KEYS, (side + 1) * KEYS)
            parts.append(weight_grad[rows] - jnp.sum(product[rows], axis=0, keepdims=True))
        centred = jnp.concatenate(parts, axis=0)
        score_grad = (weights * centred * (1.0 - tanh_val * tanh_val)).astype(bf16)
        query_grad.append((mm(both_across(keys[:, columns]), score_grad) * scale).astype(bf16))
        two = mm(score_grad, query_pair)
        key_grad.append(jnp.where(even, two[:KEYS], two[KEYS:]))
    query_grad = jnp.concatenate(query_grad, axis=0).T
    grad_cells_ref[...] = mm_cols(query_grad, wq_ref[...]).astype(bf16)
    store_weight(0, mm_rows(cells_ref[...], query_grad))
    encoded_two = jnp.concatenate([encoded_sel, encoded_sel], axis=0).T
    key_two = jnp.concatenate(two_parts(jnp.concatenate(key_grad, axis=1)), axis=0)
    value_two = jnp.concatenate(two_parts(jnp.concatenate(value_grad, axis=1)), axis=0)
    store_weight(1, mm(encoded_two, key_two))
    store_weight(2, mm(encoded_two, value_two))
    grad_gauges = mm_cols(key_two, wk_ref[...]) + mm_cols(value_two, wv_ref[...])
    grad_gauges = (grad_gauges[:KEYS] + grad_gauges[KEYS:]).astype(bf16)
    places = jnp.where(
        lax.broadcasted_iota(jnp.int32, (gauges, KEYS), 0) == places_ref[...], 1.0, 0.0
    ).astype(bf16)
    spread = mm(places, grad_gauges)
    for j in range(MEMBERS):
        store(
            j * chunk + weight_chunk, spread[j * gauge_chunk : (j + 1) * gauge_chunk, :]
        )


def widen_kernel(side_ref, part_ref, *refs):
    out_refs, (wide_ref, sems) = refs[-6:-2], refs[-2:]
    half = part_ref.shape[2]
    columns = pl.ds(pl.multiple_of(side_ref[0] * half, half), half)
    copies = []
    for i, out_ref in enumerate(out_refs):
        wide_ref[i] = part_ref[i].astype(f32)
        copies.append(
            pltpu.make_async_copy(wide_ref.at[i], out_ref.at[:, columns], sems.at[i])
        )
        copies[-1].start()
    for copy in copies:
        copy.wait()


def widen(side, part, grads):
    half = part.shape[1]
    width = 2 * half
    given = () if grads is None else tuple(grads)
    hbm = pl.BlockSpec(memory_space=pltpu.HBM)
    return pl.pallas_call(
        widen_kernel,
        out_shape=(jax.ShapeDtypeStruct((width, width), f32),) * 4,
        in_specs=[
            pl.BlockSpec(memory_space=pltpu.SMEM),
            pl.BlockSpec(memory_space=pltpu.VMEM),
        ]
        + [hbm] * len(given),
        out_specs=(hbm,) * 4,
        scratch_shapes=[
            pltpu.VMEM((4, width, half), f32),
            pltpu.SemaphoreType.DMA((4,)),
        ],
        input_output_aliases={2 + i: i for i in range(len(given))},
        compiler_params=pltpu.CompilerParams(vmem_limit_bytes=32 << 20),
        name="widen_kernel",
    )(side.reshape(1), part.reshape(4, width, half), *given)


def swap(value):
    return lax.ppermute(value, "c", [(0, 1), (1, 0)])


def chips_over(value, steps):
    count = lax.axis_size(TILES)
    return lax.ppermute(value, TILES, [(i, (i + steps) % count) for i in range(count)])


def copied(value, count):
    rows, width = value.shape
    return jnp.broadcast_to(value[None], (count, rows, width)).reshape(count * rows, width)


def after(value, *others):
    return lax.optimization_barrier((value,) + others)[0]


def per_device(cells, encoded, w_query, w_key, w_value, w_out, pattern, cell_basin, pooled_grad):
    width = cells.shape[1]
    half = width // 2
    core = lax.axis_index("c")
    device = lax.axis_index(EVERY)
    own = pooled_grad.shape[0]
    total = own * lax.axis_size(EVERY)

    rows_own = lax.dynamic_slice_in_dim(encoded, core * half, half, 1)
    copies = copied(rows_own, MEMBERS * SIZES["far"])

    slot = (cell_basin - device * own + own) % total
    counts = jnp.sum(
        (slot[None, :] == jnp.arange(3 * own, dtype=jnp.int32)[:, None]).astype(f32), axis=1
    )
    count_row = jnp.pad(counts.astype(bf16), (0, width - 3 * own))[None, :]
    packet = after(jnp.concatenate([pooled_grad, count_row], axis=0), copies)
    before, behind = chips_over(packet, 1), chips_over(packet, -1)
    mate = swap(packet)
    mine = lax.all_to_all(copies, TILES, 0, 0, tiled=True)
    before, behind, mate, mine = lax.optimization_barrier((before, behind, mate, mine))
    other = swap(mine)
    side = swap(jnp.where(core == 0, behind, before))

    block = pattern[0]
    along_x = block % SIZES["x"]
    near = (block // SIZES["x"]) % SIZES["near"]
    far_z = (block // (SIZES["x"] * SIZES["near"])) % SIZES["far"]
    along_y = block // (SIZES["x"] * SIZES["near"] * SIZES["far"])
    place = (along_y * SIZES["x"] + along_x) * SIZES["near"] + near
    place = place * SIZES["far"] + far_z
    within = jnp.arange(GAUGE_ROWS, dtype=jnp.int32)[None, :]
    rows = (block[:, None] * GAUGE_ROWS + within).reshape(1, KEYS)
    places = (place[:, None] * GAUGE_ROWS + within).reshape(1, KEYS)

    gauges = mine.shape[0]
    payload = gauges + 4 * width
    vmem = pl.BlockSpec(memory_space=pltpu.VMEM)
    smem = pl.BlockSpec(memory_space=pltpu.SMEM)
    hbm = pl.BlockSpec(memory_space=pltpu.HBM)
    grad_cells, inner, middle, outer, roots, keep, send = pl.pallas_call(
        group_kernel,
        out_shape=(
            jax.ShapeDtypeStruct(cells.shape, bf16),
            jax.ShapeDtypeStruct((own, width), f32),
            jax.ShapeDtypeStruct((own, width), f32),
            jax.ShapeDtypeStruct((own, width), f32),
            jax.ShapeDtypeStruct((SLOTS, 128), f32),
            jax.ShapeDtypeStruct((payload, half), bf16),
            jax.ShapeDtypeStruct((payload, half), bf16),
        ),
        in_specs=[smem] + [vmem] * 13 + [hbm] * 2,
        out_specs=(vmem,) * 7,
        scratch_shapes=[
            pltpu.VMEM(cells.shape, bf16),
            pltpu.VMEM(w_out.shape, bf16),
            pltpu.VMEM((SLOTS, width), f32),
            pltpu.SemaphoreType.DMA((2,)),
        ],
        compiler_params=pltpu.CompilerParams(vmem_limit_bytes=24 << 20),
        name="group_kernel",
    )(
        core.reshape(1), rows, places, slot[None, :], packet, mate, side, before, behind,
        mine, other,
        w_key, w_value, w_query,
        pltpu.with_memory_space_constraint(cells, pltpu.HBM),
        pltpu.with_memory_space_constraint(w_out, pltpu.HBM),
    )

    chip = (keep.astype(f32) + swap(send).astype(f32)).astype(bf16)
    chunk = payload // MEMBERS
    gauge_chunk = gauges // MEMBERS
    weight_chunk = chunk - gauge_chunk
    parts = lax.all_to_all(chip, GROUP, 0, 0, tiled=True).reshape(MEMBERS, chunk, half)
    column = jnp.sum(parts.astype(f32), axis=0).astype(bf16)
    count = SIZES["far"]
    turns = [
        lax.ppermute(column, "far", [(i, (i + s) % count) for i in range(count)])
        for s in range(1, count)
    ]
    inner, outer = lax.optimization_barrier((inner, outer, column))[:2]
    from_inner = swap(inner)
    total_devices = lax.axis_size(EVERY)
    from_outer = lax.ppermute(
        outer,
        EVERY,
        [(i, (i + (1 if i % 2 else -1)) % total_devices) for i in range(total_devices)],
    )
    reduced = (
        (column.astype(f32) + turns[1].astype(f32)) + (turns[0].astype(f32) + turns[2].astype(f32))
    ).astype(bf16)
    reduced = after(reduced, from_inner, from_outer)
    weights = lax.all_to_all(copied(reduced[:weight_chunk], MEMBERS), GROUP, 0, 0, tiled=True)

    pooled = ((middle + from_inner + from_outer) / roots[own : 2 * own, :1]).astype(bf16)
    own_gauge = lax.dynamic_slice_in_dim(
        reduced, weight_chunk + lax.axis_index("far") * GAUGE_ROWS, GAUGE_ROWS, 0
    )
    far_gauge = swap(after(own_gauge, weights))
    grad_gauges = jnp.where(
        core == 0,
        jnp.concatenate([own_gauge, far_gauge], axis=1),
        jnp.concatenate([far_gauge, own_gauge], axis=1),
    )
    far = swap(weights)
    grads = widen(core, weights, None)
    grads = widen(1 - core, far, grads)
    return (pooled, grad_cells, grad_gauges, grads[0], grads[1], grads[2], grads[3])


def solution(mesh):
    grid = Mesh(mesh.devices.reshape(tuple(SIZES[a] for a in EVERY)), EVERY)
    return jax.shard_map(
        per_device,
        mesh=grid,
        in_specs=(
            P(EVERY, None), P(TILES, None), P(), P(), P(), P(),
            P(EVERY, None), P(EVERY), P(EVERY, None),
        ),
        out_specs=(P(EVERY, None), P(EVERY, None), P(TILES, None), P(), P(), P(), P()),
        check_vma=False,
    )
```
